32 devices in a mesh: dp: 8 (over y, x, core), mp: 4 (over z).
Axes of the slice: x: 2, y: 2, z: 4, core: 2. Of those that a mesh axis runs over, the one named last changes fastest.
Arguments:
- vq_in: bfloat16 [16, 768, 32], P('dp'), may hold values from -6 to 6
- codes: int32 [16, 768], P('dp'), may hold values from 0 to 4095
- segment: int32 [16, 768], P('dp'), may hold values from 0 to 3, never falling along the last dimension, each value on 1 to 680 neighbouring positions
- live: int32 [16, 768], P('dp'), may hold values from 0 to 1
- labels: int32 [16, 4], P('dp'), may hold values from 0 to 999
- level_weight: int32 [10], replicated, may hold values from 1 to 4
- qkv_w: float32 [3, 1024, 1024], P(None, 'dp', 'mp'), may hold values from -0.1875 to 0.1875
- proj_w: float32 [1024, 1024], P('mp', 'dp'), may hold values from -0.5 to 0.5
- fc1_w: float32 [1024, 4096], P('dp', 'mp'), may hold values from -0.1875 to 0.1875
- fc2_w: float32 [4096, 1024], P('mp', 'dp'), may hold values from -0.09375 to 0.09375
- head_w: float32 [1024, 4096], P('dp', 'mp'), may hold values from -0.5625 to 0.5625
- ada_w: float32 [1024, 8192], P('dp'), may hold values from -0.1875 to 0.1875
- tables: float32 [1042, 1024], P(None, 'dp'), may hold values from -6 to 6
- head_scale: float32 [16], P('mp'), may hold values from 2.3 to 3
- d_stats: float32 [6, 1024], P(None, 'dp'), may hold values from 4.967054e-09 to 7.947286e-08
- qkv_stat: float32 [3, 1024], P(None, 'mp'), may hold values from 1.9868216e-08 to 7.947286e-08
- proj_stat: float32 [1024], P('mp'), may hold values from 1.9868216e-08 to 7.947286e-08
- fc1_stat: float32 [4096], P('mp'), may hold values from 1.9868216e-08 to 7.947286e-08
- fc2_stat: float32 [4096], P('mp'), may hold values from 1.9868216e-08 to 7.947286e-08
- head_stat: float32 [4096], P('mp'), may hold values from 4.967054e-09 to 1.9868216e-08
- ada_stat: float32 [8192], replicated, may hold values from 1.9868216e-08 to 7.947286e-08
- tables_v: float32 [1042, 1024], P(None, 'dp'), may hold values from 1.9868216e-08 to 3.1789145e-07
- scale_v: float32 [16], P('mp'), may hold values from 1.6276041e-07 to 8.138021e-07
Outputs:
- loss_sum: float32 [], replicated
- weight_sum: float32 [], replicated
- qkv_grad: float32 [3, 1024, 1024], P(None, 'dp', 'mp')
- proj_grad: float32 [1024, 1024], P('mp', 'dp')
- fc1_grad: float32 [1024, 4096], P('dp', 'mp')
- fc2_grad: float32 [4096, 1024], P('mp', 'dp')
- head_grad: float32 [1024, 4096], P('dp', 'mp')
- ada_grad: float32 [1024, 8192], P('dp')
- tables_grad: float32 [1042, 1024], P(None, 'dp')
- scale_grad: float32 [16], P('mp')
- d_stats_new: float32 [6, 1024], P(None, 'dp')
- qkv_stat_new: float32 [3, 1024], P(None, 'mp')
- proj_stat_new: float32 [1024], P('mp')
- fc1_stat_new: float32 [4096], P('mp')
- fc2_stat_new: float32 [4096], P('mp')
- head_stat_new: float32 [4096], P('mp')
- ada_stat_new: float32 [8192], replicated
- tables_v_new: float32 [1042, 1024], P(None, 'dp')
- scale_v_new: float32 [16], P('mp')
- qkv_new: float32 [3, 1024, 1024], P(None, 'dp', 'mp')
- proj_new: float32 [1024, 1024], P('mp', 'dp')
- fc1_new: float32 [1024, 4096], P('dp', 'mp')
- fc2_new: float32 [4096, 1024], P('mp', 'dp')
- head_new: float32 [1024, 4096], P('dp', 'mp')
- ada_new: float32 [1024, 8192], P('dp')
- tables_new: float32 [1042, 1024], P(None, 'dp')
- scale_new: float32 [16], P('mp')
The draws below stay inside these ranges and needn't reach their ends.
Inputs may be any that keep to these rules, and one draw needn't show every extreme that they name: `segment`: each packed row holds 4 items in order, each of 1 to 680 tokens, one of exactly 680.
All inputs are finite; a program needn't handle non-finite values.
Results may differ from the reference program's by a relative error of at most 0.0085.
The reference program's roundings to bfloat16 on the way count: a program that leaves them out, or rounds other values in their place, can miss the bound.
Values may be sent and summed in bfloat16 or wider, within the bound.
No kernel may reach another device: no remote copies, remote signals or barrier semaphores. Data moves between devices by JAX's collectives and lax.ppermute only.
A program may use at most 320 MiB of HBM per device.

```python
import math
import jax
import jax.numpy as jnp
import numpy as np
from jax import lax

D = 1024
HEADS = 16
HD = 64
FF = 4096
V = 4096
CODE = 32
CLASSES = 1000
LEVELS = 10
MOST = 680
SEQ = 768
COUNT = 4
STEP = 8
ROWS_DEV = 2
ROWS = 16
TAB = 1042


def draw_live(key, part):
    devices = ROWS // ROWS_DEV
    owner = jnp.arange(ROWS, dtype=jnp.int32) // ROWS_DEV
    border = 300 + 600 * owner // max(devices - 1, 1)
    ticket = jax.random.randint(key, (ROWS, SEQ), 0, 1000, dtype=jnp.int32)
    return (ticket < border[:, None]).astype(jnp.int32)


def draw_head_w(key, part):
    column = jnp.arange(V, dtype=jnp.float32) / (V - 1)
    spread = 1.0 + 2.0 * column
    base = jnp.clip(jax.random.normal(key, (D, V), jnp.float32), -6.0, 6.0)
    return base * spread[None, :] / math.sqrt(D)


def draw_tables(key, part):
    base = jnp.clip(jax.random.normal(key, (TAB, D), jnp.float32), -6.0, 6.0)
    row_index = jnp.arange(TAB)
    factor = jnp.where(row_index < CODE, 1.0 / math.sqrt(CODE), 1.0)
    return base * factor[:, None]


def place_ends(values, stream_key, smallest, top_value):
    index_at = [jax.random.randint(jax.random.fold_in(stream_key, axis), (), 0, length) for axis, length in enumerate(values.shape)]
    widest = values.shape.index(max(values.shape))
    beside = index_at[:widest] + [(index_at[widest] + 1) % values.shape[widest]] + index_at[widest + 1:]
    return values.at[tuple(index_at)].set(smallest).at[tuple(beside)].set(top_value)


def shard_levels(key, dims, pieces, least, largest):
    loudness = 1.0
    for dim, blocks in pieces:
        draws = jax.random.uniform(jax.random.fold_in(jax.random.fold_in(key, 6), dim), (blocks,), jnp.float32, least / len(pieces), largest / len(pieces))
        loudness = loudness * jnp.repeat(jnp.exp(draws), dims[dim] // blocks).reshape((-1,) + (1,) * (len(dims) - 1 - dim))
    return loudness


def length_profile(amount, total, limit, slope):
    weights = [(1 << 20) // math.isqrt(standing ** slope) + 1 for standing in range(2, amount + 1)]
    spare, given = total - limit - (amount - 1), [1] * (amount - 1)
    while spare > 0:
        free = [i for i in range(amount - 1) if given[i] < limit]
        whole, remaining = sum([weights[i] for i in free]), spare
        for i in free:
            extra = min(limit - given[i], max(1, remaining * weights[i] // whole), spare)
            given[i] = given[i] + extra
            spare = spare - extra
    return np.array([limit] + given)


def uneven_parts(stream_key, number_of, total, bound, lean):
    if number_of == 2:
        one = jax.random.randint(stream_key, (), max(1, total - bound), min(bound, total - 1) + 1)
        return jnp.stack([one, total - one])
    sizes = jnp.asarray(length_profile(number_of, total, bound, lean), jnp.int32)
    couples = (number_of - 1) // 2
    giver, taker = sizes[1:1 + 2 * couples:2], sizes[2:2 + 2 * couples:2]
    margin = jnp.minimum(giver - 1, bound - taker)
    moved = jax.random.randint(jax.random.fold_in(stream_key, 1), (couples,), 0, 1 << 20) % (margin + 1)
    sizes = sizes.at[1:1 + 2 * couples:2].set(giver - moved).at[2:2 + 2 * couples:2].set(taker + moved)
    return sizes[jax.random.permutation(jax.random.fold_in(stream_key, 2), number_of)]


def gaussian(rng, shape, deviation, most, cuts=(), held_as=jnp.bfloat16):
    entries = jax.random.normal(rng, shape, jnp.float32) * deviation
    if len(cuts) > 0:
        entries = shard_levels(rng, shape, cuts, -0.22, 0.18) * entries
    return jnp.clip(entries, min=-most, max=most).astype(held_as)


def setup_inputs(seed: int = 0) -> dict:
    key_of = jax.random.split(jax.random.key(seed), 24)
    vq_in = gaussian(key_of[0], (ROWS, SEQ, CODE), 1.0, 6.0, ((0, 8),))
    codes = place_ends(jax.random.randint(key_of[1], (ROWS, SEQ), 0, V), jax.random.fold_in(key_of[1], 1), 0, V - 1).astype(jnp.int32)
    segment = jax.vmap(lambda own: jnp.searchsorted(jnp.cumsum(uneven_parts(own, COUNT, SEQ, MOST, 0)), jnp.arange(SEQ), side="right"))(jax.random.split(key_of[2], ROWS)).reshape((ROWS, SEQ)).astype(jnp.int32)
    live = draw_live(jax.random.fold_in(key_of[23], 71), 0)
    labels = place_ends(jax.random.randint(key_of[4], (ROWS, COUNT), 0, CLASSES), jax.random.fold_in(key_of[4], 1), 0, CLASSES - 1).astype(jnp.int32)
    level_weight = place_ends(jax.random.randint(key_of[5], (LEVELS,), 1, 5), jax.random.fold_in(key_of[5], 1), 1, 4).astype(jnp.int32)
    qkv_w = gaussian(key_of[6], (3, D, D), D ** -0.5, 0.1875, ((1, 8), (2, 4)), jnp.float32)
    proj_w = gaussian(key_of[7], (D, D), (D // 8) ** -0.5, 0.5, ((0, 4), (1, 8)), jnp.float32)
    fc1_w = gaussian(key_of[8], (D, FF), D ** -0.5, 0.1875, ((0, 8), (1, 4)), jnp.float32)
    fc2_w = gaussian(key_of[9], (FF, D), FF ** -0.5, 0.09375, ((0, 4), (1, 8)), jnp.float32)
    head_w = draw_head_w(jax.random.fold_in(key_of[23], 71), 0)
    ada_w = gaussian(key_of[11], (D, 8 * D), D ** -0.5, 0.1875, ((0, 8),), jnp.float32)
    tables = draw_tables(jax.random.fold_in(key_of[23], 71), 0)
    head_scale = jnp.clip(2.3 + 0.70000005 * jax.random.uniform(key_of[13], (HEADS,), jnp.float32) ** shard_levels(key_of[13], (HEADS,), ((0, 4),), -0.2, 0.2), 2.3, 3.0)
    d_stats = jnp.clip(jnp.exp(math.log(7.947286206899662e-08) - 2.7725887 * jax.random.uniform(key_of[14], (6, D), jnp.float32) ** shard_levels(key_of[14], (6, D), ((1, 8),), -0.2, 0.2)), 4.967053879312289e-09, 7.947286206899662e-08)
    qkv_stat = jnp.clip(jnp.exp(math.log(7.947286206899662e-08) - 1.3862944 * jax.random.uniform(key_of[15], (3, D), jnp.float32) ** shard_levels(key_of[15], (3, D), ((1, 4),), -0.2, 0.2)), 1.9868215517249155e-08, 7.947286206899662e-08)
    proj_stat = jnp.clip(jnp.exp(math.log(7.947286206899662e-08) - 1.3862944 * jax.random.uniform(key_of[16], (D,), jnp.float32) ** shard_levels(key_of[16], (D,), ((0, 4),), -0.2, 0.2)), 1.9868215517249155e-08, 7.947286206899662e-08)
    fc1_stat = jnp.clip(jnp.exp(math.log(7.947286206899662e-08) - 1.3862944 * jax.random.uniform(key_of[17], (FF,), jnp.float32) ** shard_levels(key_of[17], (FF,), ((0, 4),), -0.2, 0.2)), 1.9868215517249155e-08, 7.947286206899662e-08)
    fc2_stat = jnp.clip(jnp.exp(math.log(7.947286206899662e-08) - 1.3862944 * jax.random.uniform(key_of[18], (FF,), jnp.float32) ** shard_levels(key_of[18], (FF,), ((0, 4),), -0.2, 0.2)), 1.9868215517249155e-08, 7.947286206899662e-08)
    head_stat = jnp.clip(jnp.exp(math.log(1.9868215517249155e-08) - 1.3862944 * jax.random.uniform(key_of[19], (V,), jnp.float32) ** shard_levels(key_of[19], (V,), ((0, 4),), -0.2, 0.2)), 4.967053879312289e-09, 1.9868215517249155e-08)
    ada_stat = jnp.clip(jnp.exp(jax.random.uniform(key_of[20], (8 * D,), jnp.float32, math.log(1.9868215517249155e-08), math.log(7.947286206899662e-08))), 1.9868215517249155e-08, 7.947286206899662e-08)
    tables_v = jnp.clip(jnp.exp(math.log(3.178914482759865e-07) - 2.7725887 * jax.random.uniform(key_of[21], (TAB, D), jnp.float32) ** shard_levels(key_of[21], (TAB, D), ((1, 8),), -0.2, 0.2)), 1.9868215517249155e-08, 3.178914482759865e-07)
    scale_v = jnp.clip(jnp.exp(math.log(8.138021030390519e-07) - 1.609438 * jax.random.uniform(key_of[22], (HEADS,), jnp.float32) ** shard_levels(key_of[22], (HEADS,), ((0, 4),), -0.2, 0.2)), 1.627604149234685e-07, 8.138021030390519e-07)
    return {"vq_in": vq_in, "codes": codes, "segment": segment, "live": live, "labels": labels, "level_weight": level_weight, "qkv_w": qkv_w, "proj_w": proj_w, "fc1_w": fc1_w, "fc2_w": fc2_w, "head_w": head_w, "ada_w": ada_w, "tables": tables, "head_scale": head_scale, "d_stats": d_stats, "qkv_stat": qkv_stat, "proj_stat": proj_stat, "fc1_stat": fc1_stat, "fc2_stat": fc2_stat, "head_stat": head_stat, "ada_stat": ada_stat, "tables_v": tables_v, "scale_v": scale_v}


level_starts = (1, 5, 14, 30, 55, 91, 155, 255, 424)
eps_norm = 1e-06
eps_one = 1e-30
eps_two = 0.001
rate_step = 0.3
clip_rms = 1.0

@jax.custom_vjp
def low(v):
    return lax.optimization_barrier(v.astype(jnp.bfloat16)).astype(jnp.float32)

@jax.custom_vjp
def low_back(v):
    return v

def low_keep(v):
    return (low(v), None)

def low_pass(kept, grad):
    return (grad,)

def back_keep(v):
    return (v, None)

def back_low(kept, grad):
    return (low(grad),)
low.defvjp(low_keep, low_pass)
low_back.defvjp(back_keep, back_low)

def exact_dot(left_side, right_side):
    return jnp.dot(left_side, right_side, precision=lax.Precision.HIGHEST, preferred_element_type=jnp.float32)

def layer_norm(values):
    centered = values - lax.optimization_barrier(jnp.mean(values, -1, keepdims=True))
    return centered * lax.rsqrt(lax.optimization_barrier(jnp.mean(centered * centered, -1, keepdims=True)) + eps_norm)

def unit_rows(values, gain):
    return values * lax.rsqrt(lax.optimization_barrier(jnp.mean(values * values, -1, keepdims=True)) + eps_norm) * gain

def layout(seg_row):
    seg_hot = seg_row[:, None] == jnp.arange(COUNT, dtype=jnp.int32)[None, :]
    counts = lax.optimization_barrier(jnp.sum(seg_hot.astype(jnp.int32), 0))
    starts = jnp.cumsum(counts) - counts
    first_pos = lax.optimization_barrier(jnp.sum(jnp.where(seg_hot, starts[None, :], 0), 1))
    within = jnp.arange(SEQ, dtype=jnp.int32) - first_pos
    level_row = lax.optimization_barrier(jnp.sum((within[:, None] >= jnp.array(level_starts, dtype=jnp.int32)[None, :]).astype(jnp.int32), 1))
    return (seg_hot.astype(jnp.float32), level_row)

def allowed_mask(seg_row, level_row, live_row):
    length = seg_row.shape[0]
    same_item = seg_row[:, None] == seg_row[None, :]
    earlier = level_row[None, :] <= level_row[:, None]
    diagonal = jnp.arange(length)[:, None] == jnp.arange(length)[None, :]
    usable = (live_row[None, :] > 0) | diagonal
    return same_item & earlier & usable

def row_loss(weights, vq_row, code_row, seg_row, live_row, label_row, level_weight):
    qkv_low, proj_low, fc1_low, fc2_low, head_low, ada_low, table_low, head_scale = weights
    highest = lax.Precision.HIGHEST
    seg_hot, level_row = layout(seg_row)
    level_hot = (level_row[:, None] == jnp.arange(LEVELS, dtype=jnp.int32)[None, :]).astype(jnp.float32)
    class_hot = (label_row[:, None] == jnp.arange(CLASSES, dtype=jnp.int32)[None, :]).astype(jnp.float32)
    stream_zero = exact_dot(vq_row.astype(jnp.float32), table_low[:CODE]) + exact_dot(level_hot, table_low[CODE:CODE + LEVELS])
    class_vec = exact_dot(class_hot, table_low[CODE + LEVELS:])
    modulation = exact_dot(seg_hot, exact_dot(low(jax.nn.silu(class_vec)), ada_low))
    shift_one, scale_one, gate_one, shift_two, scale_two, gate_two, shift_out, scale_out = jnp.split(modulation, 8, axis=1)
    input_one = low(layer_norm(stream_zero) * (1.0 + scale_one) + shift_one)
    qkv_out = low_back(jnp.einsum('td,cde->cte', input_one, qkv_low, precision=highest))
    query = qkv_out[0].reshape(SEQ, HEADS, HD)
    keyed = qkv_out[1].reshape(SEQ, HEADS, HD)
    query_low = low(unit_rows(query, (jnp.exp(head_scale) / math.sqrt(HD))[:, None]))
    key_low = low(unit_rows(keyed, 1.0 / math.sqrt(HD)))
    value_low = low(qkv_out[2].reshape(SEQ, HEADS, HD))
    scores = low_back(jnp.einsum('thd,shd->hts', query_low, key_low, precision=highest))
    scores = jnp.where(allowed_mask(seg_row, level_row, live_row)[None], scores, -1e+30)
    row_peak = lax.optimization_barrier(jnp.max(scores, -1, keepdims=True))
    exponent = jnp.exp(scores - row_peak)
    attention = exponent / lax.optimization_barrier(jnp.sum(exponent, -1, keepdims=True))
    mixed = low(low_back(jnp.einsum('hts,shd->thd', low(attention), value_low, precision=highest))).reshape(SEQ, D)
    branch_one = low_back(exact_dot(mixed, proj_low))
    stream_one = stream_zero + gate_one * branch_one
    input_two = low(layer_norm(stream_one) * (1.0 + scale_two) + shift_two)
    hidden = low_back(exact_dot(input_two, fc1_low))
    branch_two = low_back(exact_dot(low(jax.nn.gelu(hidden, approximate=True)), fc2_low))
    stream_two = stream_one + gate_two * branch_two
    input_out = low(layer_norm(stream_two) * (1.0 + scale_out) + shift_out)
    logits = low_back(exact_dot(input_out, head_low))
    logit_peak = lax.optimization_barrier(jnp.max(logits, -1, keepdims=True))
    log_total = logit_peak[:, 0] + jnp.log(lax.optimization_barrier(jnp.sum(jnp.exp(logits - logit_peak), -1)))
    picked = lax.optimization_barrier(jnp.sum(jnp.where(code_row[:, None] == jnp.arange(V, dtype=jnp.int32)[None, :], logits, 0.0), -1))
    weight_tok = (live_row * level_weight[level_row]).astype(jnp.float32)
    return jnp.sum(weight_tok * (log_total - picked))

def adjust(master, raw_step):
    ratio = jnp.sqrt(jnp.mean(raw_step * raw_step)) / clip_rms
    spread = jnp.maximum(eps_two, jnp.sqrt(jnp.mean(master * master)))
    return master - rate_step * spread * raw_step / jnp.maximum(1.0, ratio)

def factored(master, gradient, row_old, col_old, decay_rate):
    squares = gradient * gradient + eps_one
    row_new = decay_rate * row_old + (1.0 - decay_rate) * lax.optimization_barrier(jnp.mean(squares, 1))
    col_new = decay_rate * col_old + (1.0 - decay_rate) * lax.optimization_barrier(jnp.mean(squares, 0))
    raw_step = gradient * lax.rsqrt(row_new[:, None] * col_new[None, :] / jnp.mean(row_new))
    return (row_new, col_new, adjust(master, raw_step))

def plain_update(master, gradient, second_old, decay_rate):
    second_new = decay_rate * second_old + (1.0 - decay_rate) * (gradient * gradient + eps_one)
    return (second_new, adjust(master, gradient * lax.rsqrt(second_new)))

def qkv_view(array_in):
    return jnp.transpose(array_in, (1, 0, 2)).reshape(array_in.shape[1], -1)

def qkv_unview(array_in):
    return jnp.transpose(array_in.reshape(array_in.shape[0], 3, -1), (1, 0, 2))

def reference(vq_in, codes, segment, live, labels, level_weight, qkv_w, proj_w, fc1_w, fc2_w, head_w, ada_w, tables, head_scale, d_stats, qkv_stat, proj_stat, fc1_stat, fc2_stat, head_stat, ada_stat, tables_v, scale_v):
    masters = (qkv_w, proj_w, fc1_w, fc2_w, head_w, ada_w, tables, head_scale)
    checked_row = jax.checkpoint(row_loss)

    def total_loss(parameters):
        rounded = tuple((low(parameter) for parameter in parameters[:7])) + (parameters[7],)

        def add_row(carried, row_data):
            return (carried + checked_row(rounded, *row_data, level_weight), None)
        summed, unused = lax.scan(add_row, jnp.zeros((), jnp.float32), (vq_in, codes, segment, live, labels))
        return summed
    level_all = jax.vmap(layout)(segment)[1]
    weight_sum = jnp.sum((live * level_weight[level_all]).astype(jnp.float32))
    loss_sum, pull_back = jax.vjp(total_loss, masters)
    gradients = pull_back(1.0 / weight_sum)[0]
    qkv_grad, proj_grad, fc1_grad, fc2_grad, head_grad, ada_grad, tables_grad, scale_grad = gradients
    decay_rate = 1.0 - STEP ** (-0.8)
    pairs = [(qkv_view(qkv_w), qkv_view(qkv_grad), qkv_stat.reshape(3 * D)), (proj_w.T, proj_grad.T, proj_stat), (fc1_w, fc1_grad, fc1_stat), (fc2_w.T, fc2_grad.T, fc2_stat), (head_w, head_grad, head_stat), (ada_w, ada_grad, ada_stat)]
    results = [factored(pair[0], pair[1], d_stats[position], pair[2], decay_rate) for position, pair in enumerate(pairs)]
    tables_v_new, tables_new = plain_update(tables, tables_grad, tables_v, decay_rate)
    scale_v_new, scale_new = plain_update(head_scale, scale_grad, scale_v, decay_rate)
    d_stats_new = jnp.stack([result[0] for result in results])
    return (loss_sum, weight_sum, qkv_grad, proj_grad, fc1_grad, fc2_grad, head_grad, ada_grad, tables_grad, scale_grad, d_stats_new, results[0][1].reshape(3, D), results[1][1], results[2][1], results[3][1], results[4][1], results[5][1], tables_v_new, scale_v_new, qkv_unview(results[0][2]), results[1][2].T, results[2][2], results[3][2].T, results[4][2], results[5][2], tables_new, scale_new)
```

```python
import functools
import math

import jax
import jax.numpy as jnp
from jax import lax
from jax.experimental import pallas as pl
from jax.experimental.pallas import tpu as pltpu
from jax.sharding import Mesh, PartitionSpec as P

STEP = 8
level_starts = (1, 5, 14, 30, 55, 91, 155, 255, 424)
eps_norm = 1e-06
eps_one = 1e-30
eps_two = 0.001
rate_step = 0.3
clip_rms = 1.0
low_type = jnp.bfloat16
full_type = jnp.float32
high = lax.Precision.HIGH
highest = lax.Precision.HIGHEST
swap_pairs = ((0, 1), (1, 0))
busy_us = {
    "row_layout": 2, "enter": 5, "enter_first": 6, "attend": 11, "onward": 4, "feed": 9, "head": 6, "merge": 2,
    "head_back": 5, "back": 5, "feed_back": 7, "attend_back": 16, "old_stats": 4, "row_stats": 3,
    "column_stats": 5, "finish": 2, "head_grad": 6, "feed_grad": 12, "first_grad": 6,
}
DP = ("g", "c")
MP = ("h", "l")


def cost(name):
    return pl.CostEstimate(flops=busy_us[name] * 10**9, transcendentals=0, bytes_accessed=busy_us[name] * 10**6)


def low(a):
    return a.astype(low_type)


def full(a):
    return a.astype(full_type)


def dot_nn(a, b, precision=None):
    return jnp.dot(a, b, preferred_element_type=full_type, precision=precision)


def dot_nt(a, b, precision=None):
    return lax.dot_general(
        a, b, (((1,), (1,)), ((), ())), preferred_element_type=full_type, precision=precision
    )


def dot_tn(a, b, precision=None):
    return lax.dot_general(
        a, b, (((0,), (0,)), ((), ())), preferred_element_type=full_type, precision=precision
    )


def over_c(a):
    return lax.ppermute(a, "c", swap_pairs)


def over_l(a):
    return lax.ppermute(a, "l", swap_pairs)


def over_h(a):
    return lax.ppermute(a, "h", swap_pairs)


def over_cl(a):
    return lax.ppermute(a, ("c", "l"), [(i, i ^ 3) for i in range(4)])


def over_g(a, k):
    return lax.ppermute(a, "g", [(i, i ^ k) for i in range(lax.axis_size("g"))])


def ordered(flag, mine, other, axis):
    return jnp.where(
        flag == 0,
        jnp.concatenate([mine, other], axis),
        jnp.concatenate([other, mine], axis),
    )


def gather_g(a):
    count = lax.axis_size("g")
    if count != 4:
        return lax.all_gather(a, "g", axis=0, tiled=True)
    here = lax.axis_index("g")
    out = jnp.zeros((4,) + a.shape, a.dtype)
    for k in range(4):
        piece = a if k == 0 else over_g(a, k)
        out = lax.dynamic_update_index_in_dim(out, piece, here ^ k, 0)
    return out.reshape((4 * a.shape[0],) + a.shape[1:])


def scatter_g(a):
    count = lax.axis_size("g")
    if count != 4:
        return full(lax.psum_scatter(a, "g", scatter_dimension=0, tiled=True))
    here = lax.axis_index("g")
    blocks = a.reshape((4, a.shape[0] // 4) + a.shape[1:])
    total = full(lax.dynamic_index_in_dim(blocks, here, 0, False))
    for k in range(1, 4):
        total = total + full(over_g(lax.dynamic_index_in_dim(blocks, here ^ k, 0, False), k))
    return total


def tie(a, *others):
    return lax.optimization_barrier((a,) + others)[0]


def centre(values):
    centered = values - jnp.mean(values, -1, keepdims=True)
    scale = lax.rsqrt(jnp.mean(centered * centered, -1, keepdims=True) + eps_norm)
    return centered * scale, scale


def centre_back(normed, scale, incoming):
    return (
        incoming
        - jnp.mean(incoming, -1, keepdims=True)
        - normed * jnp.mean(incoming * normed, -1, keepdims=True)
    ) * scale


def gelu_parts(values):
    root = math.sqrt(2.0 / math.pi)
    square = values * values
    bent = jnp.tanh(values * (root + (root * 0.044715) * square))
    half = 0.5 + 0.5 * bent
    slope = half + values * (0.5 - 0.5 * (bent * bent)) * (root + (root * 3.0 * 0.044715) * square)
    return values * half, slope


def split_parts(a, count):
    parts = []
    for _ in range(count):
        parts.append(low(a))
        a = a - full(parts[-1])
    return parts


def item_parts(vectors):
    return jnp.concatenate(split_parts(vectors, 3) + [jnp.zeros(vectors.shape, low_type)], 0)


def item_sums(hot, values):
    upper, lower = split_parts(values, 2)
    return (dot_tn(hot, upper) + dot_tn(hot, lower))[:8]


def whole(shape):
    return pl.BlockSpec(shape, lambda i: (0,) * len(shape), pipeline_mode=pl.Buffered(1))


def tiled(tile, columns):
    return pl.BlockSpec((tile, columns), lambda i: (i, 0))


def call(kernel, grid, in_specs, out_specs, out_shape, scratch, name):
    return pl.pallas_call(
        kernel,
        grid=grid,
        in_specs=in_specs,
        out_specs=out_specs,
        out_shape=[jax.ShapeDtypeStruct(shape, dtype) for shape, dtype in out_shape],
        scratch_shapes=scratch,
        compiler_params=pltpu.CompilerParams(vmem_limit_bytes=48 * 2**20),
        cost_estimate=cost(name),
        name=name,
    )


def rows_kernel(lw_ref, seg_ref, live_ref, place_ref, weight_ref, sum_ref):
    seg, live = seg_ref[...], live_ref[...]
    at = lax.broadcasted_iota(jnp.int32, seg.shape, 1)
    first = jnp.zeros_like(seg)
    for item in range(1, 4):
        count = jnp.sum(full(jnp.where(seg < item, 1, 0)), 1, keepdims=True).astype(jnp.int32)
        first = jnp.where(seg == item, count, first)
    within = at - first
    level = jnp.zeros_like(seg)
    for start in level_starts:
        level = level + jnp.where(within >= start, 1, 0)
    weight = jnp.zeros_like(seg)
    for position in range(lw_ref.shape[0]):
        weight = jnp.where(level == position, lw_ref[position], weight)
    weight = weight * live
    place_ref[...] = seg * 16 + level
    weight_ref[...] = weight
    each = jnp.sum(full(weight), 1, keepdims=True)
    sum_ref[...] = jnp.sum(each, 0, keepdims=True).astype(jnp.int32)


def row_layout(level_weight, segment, live):
    shape = segment.shape
    return pl.pallas_call(
        rows_kernel,
        in_specs=[pl.BlockSpec(memory_space=pltpu.SMEM)] + [pl.BlockSpec(memory_space=pltpu.VMEM)] * 2,
        out_shape=[
            jax.ShapeDtypeStruct(shape, jnp.int32),
            jax.ShapeDtypeStruct(shape, jnp.int32),
            jax.ShapeDtypeStruct((1, 1), jnp.int32),
        ],
        cost_estimate=cost("row_layout"),
        name="row_layout",
    )(level_weight, segment, live)


def enter_tile(feat_ref, table_ref, hot_ref, w, in_ref, qkv_ref, stream_ref, parts_s):
    stream = dot_nn(feat_ref[...], table_ref[...])

    @pl.when(pl.program_id(0) == 0)
    def _():
        stream_ref[...] = stream[: stream_ref.shape[0]]

    normed, _ = centre(stream)
    hot = hot_ref[...]
    given = low(normed * (1.0 + dot_nn(hot, parts_s[1])) + dot_nn(hot, parts_s[0]))
    in_ref[...] = given
    qkv_ref[...] = dot_nn(given, w)


def enter_parts(mod_ref, parts_s):
    parts_s[0] = item_parts(mod_ref[0])
    parts_s[1] = item_parts(mod_ref[1])


def enter_kernel(feat_ref, table_ref, hot_ref, mod_ref, w_ref, in_ref, qkv_ref, stream_ref, parts_s):
    @pl.when(pl.program_id(0) == 0)
    def _():
        enter_parts(mod_ref, parts_s)

    enter_tile(feat_ref, table_ref, hot_ref, w_ref[...], in_ref, qkv_ref, stream_ref, parts_s)


def enter(feats, table, hot, mods, w):
    n, k = feats.shape
    width, columns = w.shape
    tile = n // 2
    return call(
        enter_kernel,
        (2,),
        [tiled(tile, k), whole((k, width)), tiled(tile, 16), whole(mods.shape), whole(w.shape)],
        [tiled(tile, width), tiled(tile, columns), fixed((tile // 2, width))],
        [((n, width), low_type), ((n, columns), full_type), ((tile // 2, width), full_type)],
        [pltpu.VMEM((2, 16, width), low_type)],
        "enter",
    )(feats, table, hot, mods, w)


def enter_first_kernel(
    at_ref, feat_ref, table_ref, hot_ref, mod_ref, a_ref, b_ref, c_ref, d_ref, in_ref, qkv_ref, stream_ref,
    w_ref, p_ref, parts_s
):
    @pl.when(pl.program_id(0) == 0)
    def _():
        enter_parts(mod_ref, parts_s)
        for k, ref in enumerate((a_ref, b_ref, c_ref, d_ref)):
            rows = ref.shape[2]
            start = pl.multiple_of(jnp.bitwise_xor(at_ref[0], k) * rows, rows)
            for j in range(2):
                for c in range(3):
                    w_ref[pl.ds(start, rows), (2 * c + j) * 128 : (2 * c + j + 1) * 128] = ref[j, c]
                p_ref[pl.ds(start, rows), j * 128 : (j + 1) * 128] = ref[j, 3]

    enter_tile(feat_ref, table_ref, hot_ref, w_ref[...], in_ref, qkv_ref, stream_ref, parts_s)


def enter_first(here, feats, table, hot, mods, pieces):
    n, k = feats.shape
    width = table.shape[1]
    columns = 768
    tile = n // 2
    shape = pieces[0].shape
    return call(
        enter_first_kernel,
        (n // tile,),
        [pl.BlockSpec(memory_space=pltpu.SMEM), tiled(tile, k), whole((k, width)), tiled(tile, 16), whole(mods.shape)]
        + [whole(shape)] * 4,
        [tiled(tile, width), tiled(tile, columns), fixed((tile // 2, width))]
        + [fixed((width, columns)), fixed((width, columns // 3))],
        [((n, width), low_type), ((n, columns), full_type), ((tile // 2, width), full_type)]
        + [((width, columns), low_type), ((width, columns // 3), low_type)],
        [pltpu.VMEM((2, 16, width), low_type)],
        "enter_first",
    )(here[None], feats, table, hot, mods, *pieces)


def onward_kernel(a_ref, b_ref, c_ref, x_ref, hot_ref, mod_ref, br_ref, y_ref, in_ref, parts_s, *, picks):
    @pl.when(pl.program_id(0) == 0)
    def _():
        for k, pick in enumerate(picks):
            parts_s[k] = item_parts(mod_ref[pick])

    branch = full(a_ref[...]) + full(b_ref[...]) + full(c_ref[...])
    br_ref[...] = branch
    hot = hot_ref[...]
    stream = x_ref[...] + dot_nn(hot, parts_s[0]) * branch
    y_ref[...] = stream
    normed, _ = centre(stream)
    in_ref[...] = low(normed * (1.0 + dot_nn(hot, parts_s[2])) + dot_nn(hot, parts_s[1]))


def onward(parts, stream, hot, mods, picks):
    n, width = parts[2].shape
    tile = n // 2
    return call(
        functools.partial(onward_kernel, picks=picks),
        (n // tile,),
        [tiled(tile, width)] * 4 + [tiled(tile, 16), whole(mods.shape)],
        [tiled(tile, width)] * 3,
        [((n, width), full_type), ((n, width), full_type), ((n, width), low_type)],
        [pltpu.VMEM((3, 16, width), low_type)],
        "onward",
    )(*parts, stream, hot, mods)


def back_kernel(*refs, gated, carried, picks):
    refs = list(refs)
    a_ref, b_ref, c_ref, x_ref, hot_ref, mod_ref = refs[:6]
    del refs[:6]
    res_ref = refs.pop(0) if carried else None
    br_ref = refs.pop(0) if gated else None
    feat_ref = None if gated else refs.pop(0)
    res_out = refs.pop(0) if gated else None
    d_ref = refs.pop(0) if gated else None
    items_ref = refs.pop(0)
    lead_ref = None if gated else refs.pop(0)
    parts_s = refs.pop(0)

    @pl.when(pl.program_id(0) == 0)
    def _():
        for k, pick in enumerate(picks):
            parts_s[k] = item_parts(mod_ref[pick])
        items_ref[...] = jnp.zeros_like(items_ref)
        if not gated:
            lead_ref[...] = jnp.zeros_like(lead_ref)

    hot = hot_ref[...]
    incoming = full(a_ref[...]) + full(b_ref[...]) + full(c_ref[...])
    normed, scale = centre(x_ref[...])
    items_ref[0] += item_sums(hot, incoming)
    items_ref[1] += item_sums(hot, incoming * normed)
    res = centre_back(normed, scale, incoming * (1.0 + dot_nn(hot, parts_s[0])))
    if carried:
        res = res + res_ref[...]
    if gated:
        res_out[...] = res
        items_ref[2] += item_sums(hot, res * br_ref[...])
        d_ref[...] = low(res * dot_nn(hot, parts_s[1]))
    else:
        upper, lower = split_parts(res, 2)
        feats = feat_ref[...]
        lead_ref[...] += dot_tn(feats, upper) + dot_tn(feats, lower)


def back(parts, stream, hot, mods, picks, carried, branch, feats):
    n, width = parts[2].shape
    tile = n // 2
    gated, has = branch is not None, carried is not None
    extra = ([carried] if has else []) + ([branch] if gated else [feats])
    specs = [tiled(tile, width)] * 4 + [tiled(tile, 16), whole(mods.shape)]
    specs += [tiled(tile, a.shape[1]) for a in extra]
    count = 3 if gated else 2
    out_specs, out_shape = [], []
    if gated:
        out_specs += [tiled(tile, width)] * 2
        out_shape += [((n, width), full_type), ((n, width), low_type)]
    out_specs.append(fixed((count, 8, width)))
    out_shape.append(((count, 8, width), full_type))
    if not gated:
        out_specs.append(fixed((feats.shape[1], width)))
        out_shape.append(((feats.shape[1], width), full_type))
    return call(
        functools.partial(back_kernel, gated=gated, carried=has, picks=picks),
        (n // tile,),
        specs,
        out_specs,
        out_shape,
        [pltpu.VMEM((2, 16, width), low_type)],
        "back",
    )(*parts, stream, hot, mods, *extra)


def either(a_ref, b_ref, c_ref, d_ref):
    top = jnp.concatenate([a_ref[...], b_ref[...]], 0)
    return jnp.where(pl.program_id(0) == 0, top, jnp.concatenate([c_ref[...], d_ref[...]], 0))


def put(value, top_ref, bottom_ref):
    @pl.when(pl.program_id(0) == 0)
    def _():
        top_ref[...] = value

    @pl.when(pl.program_id(0) == 1)
    def _():
        bottom_ref[...] = value


def fixed(shape):
    return pl.BlockSpec(shape, lambda i: (0,) * len(shape))


def column_half(shape, number):
    return pl.BlockSpec(
        shape[:2] + (shape[2] // 2,), lambda i: (0, 0, number), pipeline_mode=pl.Buffered(1)
    )


def feed_kernel(a_ref, b_ref, c_ref, d_ref, one_ref, two_ref, row_ref, act_ref, slope_ref, top_ref, bottom_ref):
    given = either(a_ref, b_ref, c_ref, d_ref)
    row_ref[...] = given
    units = one_ref.shape[2]
    total = None
    for h in range(2):
        at = slice(h * units, (h + 1) * units)
        act, slope = gelu_parts(dot_nn(given, one_ref[h]))
        act = low(act)
        act_ref[:, at] = act
        slope_ref[:, at] = slope
        part = dot_nt(act, two_ref[h])
        total = part if total is None else total + part
    put(low(total), top_ref, bottom_ref)


def feed(pieces, both):
    tile, width = 2 * pieces[0].shape[0], pieces[0].shape[1]
    units = both.shape[2]
    return call(
        feed_kernel,
        (2,),
        [whole(pieces[0].shape)] * 4 + [column_half(both.shape, k) for k in range(2)],
        [tiled(tile, width), tiled(tile, units), tiled(tile, units), fixed((tile, width)), fixed((tile, width))],
        [((2 * tile, width), low_type), ((2 * tile, units), low_type), ((2 * tile, units), full_type)]
        + [((tile, width), low_type)] * 2,
        [],
        "feed",
    )(*pieces, both, both)


def feed_back_kernel(a_ref, b_ref, c_ref, d_ref, slope_ref, one_ref, two_ref, row_ref, dh_ref, top_ref, bottom_ref):
    given = either(a_ref, b_ref, c_ref, d_ref)
    row_ref[...] = given
    units = one_ref.shape[2]
    total = None
    for h in range(2):
        at = slice(h * units, (h + 1) * units)
        d_hidden = low(dot_nn(given, two_ref[h]) * slope_ref[:, at])
        dh_ref[:, at] = d_hidden
        part = dot_nt(d_hidden, one_ref[h])
        total = part if total is None else total + part
    put(low(total), top_ref, bottom_ref)


def feed_back(pieces, slope, both):
    tile, width = 2 * pieces[0].shape[0], pieces[0].shape[1]
    units = both.shape[2]
    return call(
        feed_back_kernel,
        (2,),
        [whole(pieces[0].shape)] * 4 + [tiled(tile, units)] + [column_half(both.shape, k) for k in range(2)],
        [tiled(tile, width), tiled(tile, units), fixed((tile, width)), fixed((tile, width))],
        [((2 * tile, width), low_type), ((2 * tile, units), low_type)] + [((tile, width), low_type)] * 2,
        [],
        "feed_back",
    )(*pieces, slope, both, both)


def head_kernel(a_ref, b_ref, c_ref, d_ref, w_ref, code_ref, column_ref, row_ref, logit_ref, stat_ref):
    given = either(a_ref, b_ref, c_ref, d_ref)
    row_ref[...] = given
    logits = jnp.concatenate([dot_nn(given, w_ref[h]) for h in range(2)], 1)
    logit_ref[...] = logits
    peak = jnp.max(logits, 1, keepdims=True)
    total = jnp.sum(jnp.exp(logits - peak), 1, keepdims=True)
    picked = jnp.sum(jnp.where(code_ref[...] == column_ref[...], logits, 0.0), 1, keepdims=True)
    lane = lax.broadcasted_iota(jnp.int32, (logits.shape[0], 128), 1)
    turned = jnp.where(lane == 0, peak, jnp.where(lane == 1, total, picked)).T
    stat_ref[...] = turned[0:8, :]


def head(pieces, w, code, column):
    tile, width = 2 * pieces[0].shape[0], pieces[0].shape[1]
    units = 2 * w.shape[2]
    return call(
        head_kernel,
        (2,),
        [whole(pieces[0].shape)] * 4 + [whole(w.shape), tiled(tile, 1), whole((1, units))],
        [tiled(tile, width), tiled(tile, units), pl.BlockSpec((8, tile), lambda i: (0, i))],
        [((2 * tile, width), low_type), ((2 * tile, units), full_type), ((8, 2 * tile), full_type)],
        [],
        "head",
    )(*pieces, w, code, column)


def merge_kernel(sum_ref, here_ref, c_ref, l_ref, d_ref, weight_ref, out_ref, loss_ref):
    half = here_ref.shape[1] // 2

    def over_core(a):
        return jnp.concatenate([a[:, half:], a[:, :half]], 1)

    def over_line(a):
        return jnp.concatenate(
            [pltpu.roll(a[:, :half], half // 2, 1), pltpu.roll(a[:, half:], half // 2, 1)], 1
        )

    parts = (here_ref[...], over_core(c_ref[...]), over_line(l_ref[...]), over_core(over_line(d_ref[...])))
    peak = functools.reduce(jnp.maximum, [part[0:1] for part in parts])
    total = sum(part[1:2] * jnp.exp(part[0:1] - peak) for part in parts)
    picked = sum(part[2:3] for part in parts)
    log_total = peak + jnp.log(total)
    weight = weight_ref[...]
    spot = lax.broadcasted_iota(jnp.int32, (1, 2 * half), 1)
    loss = jnp.where(spot < half // 2, weight * (log_total - picked), 0.0)
    loss_ref[...] = jnp.broadcast_to(jnp.sum(loss, 1, keepdims=True), loss_ref.shape)
    blank = jnp.zeros((126, 2 * half), full_type)
    out_ref[...] = jnp.concatenate([log_total, weight / sum_ref[0], blank], 0).T


def merge(weight_sum, here, over_core, over_line, over_both, weights):
    n = here.shape[1]
    return pl.pallas_call(
        merge_kernel,
        in_specs=[pl.BlockSpec(memory_space=pltpu.SMEM)] + [pl.BlockSpec(memory_space=pltpu.VMEM)] * 5,
        out_shape=[jax.ShapeDtypeStruct((n, 128), full_type), jax.ShapeDtypeStruct((1, 128), full_type)],
        cost_estimate=cost("merge"),
        name="merge",
    )(weight_sum[None], here, over_core, over_line, over_both, weights)


def head_back_kernel(logit_ref, w_ref, code_ref, column_ref, line_ref, d_ref, top_ref, bottom_ref):
    hit = jnp.where(code_ref[...] == column_ref[...], 1.0, 0.0)
    line = line_ref[...]
    d_logits = low(line[:, 1:2] * (jnp.exp(logit_ref[...] - line[:, 0:1]) - hit))
    d_ref[...] = d_logits
    units = w_ref.shape[2]
    total = dot_nt(d_logits[:, :units], w_ref[0]) + dot_nt(d_logits[:, units:], w_ref[1])
    put(low(total), top_ref, bottom_ref)


def head_back(logits, w, code, column, lines):
    n, units = logits.shape
    width = w.shape[1]
    tile = n // 2
    return call(
        head_back_kernel,
        (2,),
        [tiled(tile, units), whole(w.shape), tiled(tile, 1), whole((1, units)), tiled(tile, 128)],
        [tiled(tile, units), fixed((tile, width)), fixed((tile, width))],
        [((n, units), low_type)] + [((tile, width), low_type)] * 2,
        [],
        "head_back",
    )(logits, w, code, column, lines)


def old_stats_kernel(qkv_ref, proj_ref, one_ref, two_ref, head_ref, ada_ref, tab_ref, scale_ref, out_ref):
    def total(values):
        return jnp.sum(jnp.sum(values * values, 1, keepdims=True), 0, keepdims=True)

    spot = lax.broadcasted_iota(jnp.int32, (1, 128), 1)
    line = jnp.zeros((1, 128), full_type)
    sums = [sum(total(qkv_ref[c]) for c in range(3))]
    sums += [total(ref[...]) for ref in (proj_ref, one_ref, two_ref, head_ref, scale_ref)]
    for k, value in enumerate(sums):
        line = jnp.where(spot == 16 + k, value, line)
    out_ref[0:1, :] = line
    line = jnp.where(spot == 8, total(ada_ref[...]), 0.0)
    out_ref[1:2, :] = jnp.where(spot == 9, total(tab_ref[...]), line)


def old_stats(*olds):
    return pl.pallas_call(
        old_stats_kernel,
        out_shape=jax.ShapeDtypeStruct((2, 128), full_type),
        compiler_params=pltpu.CompilerParams(vmem_limit_bytes=48 * 2**20),
        cost_estimate=cost("old_stats"),
        name="old_stats",
    )(*olds)


def put_rows(out_ref, start, value):
    groups, _, rows, _ = out_ref.shape
    for g in range(groups):
        out_ref[g, 0, :, start : start + value.shape[1]] = value[g * rows : (g + 1) * rows]


def head_grad_kernel(a_ref, b_ref, c_ref, d_ref, out_ref):
    put_rows(out_ref, 0, low(dot_tn(a_ref[...], c_ref[...]) + dot_tn(b_ref[...], d_ref[...])))


def head_grad_of(inputs, wanted, groups):
    n, width = inputs[0].shape
    columns = wanted[0].shape[1] // 2
    block = pl.BlockSpec((n, columns), lambda i: (0, i))
    return call(
        head_grad_kernel,
        (2,),
        [whole((n, width))] * 2 + [block] * 2,
        [pl.BlockSpec((groups, 1, width // groups, columns), lambda i: (0, i, 0, 0))],
        [((groups, 2, width // groups, columns), low_type)],
        [],
        "head_grad",
    )(*inputs, *wanted)[0]


def feed_grad_kernel(a_ref, b_ref, c_ref, d_ref, e_ref, f_ref, g_ref, h_ref, out_ref):
    @pl.when(pl.program_id(0) < 2)
    def _():
        put_rows(out_ref, 0, low(dot_tn(a_ref[...], c_ref[...]) + dot_tn(b_ref[...], d_ref[...])))

    @pl.when(pl.program_id(0) >= 2)
    def _():
        put_rows(out_ref, 0, low(dot_tn(e_ref[...], g_ref[...]) + dot_tn(f_ref[...], h_ref[...])))


def feed_grad_of(inputs, d_hidden, d_branch, acts, groups):
    n, width = inputs[0].shape
    columns = acts[0].shape[1] // 2
    early = pl.BlockSpec((n, columns), lambda i: (0, jnp.minimum(i, 1)))
    late = pl.BlockSpec((n, columns), lambda i: (0, jnp.maximum(i - 2, 0)))
    return call(
        feed_grad_kernel,
        (4,),
        [whole((n, width))] * 2 + [early] * 2 + [whole((n, width))] * 2 + [late] * 2,
        [pl.BlockSpec((groups, 1, width // groups, columns), lambda i: (0, i % 2, 0, i // 2))],
        [((groups, 2, width // groups, 2 * columns), low_type)],
        [],
        "feed_grad",
    )(*inputs, *d_hidden, *d_branch, *acts)[0]


def first_grad_kernel(a_ref, b_ref, c_ref, d_ref, e_ref, f_ref, g_ref, h_ref, out_ref):
    group = c_ref.shape[1] // 3
    start = pl.program_id(0) * 128

    def columns(ref):
        return jnp.concatenate(
            [ref[:, pl.ds(pl.multiple_of(start + c * group, 128), 128)] for c in range(3)], 1
        )

    put_rows(out_ref, 0, low(dot_tn(a_ref[...], columns(c_ref)) + dot_tn(b_ref[...], columns(d_ref))))
    put_rows(out_ref, 384, low(dot_tn(e_ref[...], g_ref[...]) + dot_tn(f_ref[...], h_ref[...])))


def first_grad_of(inputs, d_qkv, d_branch, mixed, groups):
    n, width = inputs[0].shape
    return call(
        first_grad_kernel,
        (2,),
        [whole((n, width))] * 2 + [whole(d_qkv[0].shape)] * 2 + [whole((n, width))] * 2
        + [pl.BlockSpec((n, 128), lambda i: (0, i))] * 2,
        [pl.BlockSpec((groups, 1, width // groups, 512), lambda i: (0, i, 0, 0))],
        [((groups, 2, width // groups, 512), low_type)],
        [],
        "first_grad",
    )(*inputs, *d_qkv, *d_branch, *mixed)[0]


def row_stats_kernel(qkv_ref, proj_ref, one_ref, two_ref, head_ref, out_ref):
    n = out_ref.shape[1]
    lane = lax.broadcasted_iota(jnp.int32, (n, 128), 1)
    out = jnp.zeros((n, 128), full_type)
    qkv = sum(jnp.sum(qkv_ref[c] * qkv_ref[c], 1, keepdims=True) for c in range(3))
    sums = [qkv + 3 * qkv_ref.shape[2] * eps_one]
    for ref in (proj_ref, one_ref, two_ref, head_ref):
        values = ref[...]
        sums.append(jnp.sum(values * values, 1, keepdims=True) + ref.shape[1] * eps_one)
    for k, column in enumerate(sums):
        out = jnp.where(lane == k, column, out)
    out_ref[...] = out.T[0:8, :]


def row_stats(*gradients):
    n = gradients[1].shape[0]
    return pl.pallas_call(
        row_stats_kernel,
        out_shape=jax.ShapeDtypeStruct((8, n), full_type),
        compiler_params=pltpu.CompilerParams(vmem_limit_bytes=48 * 2**20),
        cost_estimate=cost("row_stats"),
        name="row_stats",
    )(*gradients)


def column_stats_kernel(
    at_ref, row_ref, old_ref, tail_ref, tables_ref, scale_ref, qkv_ref, proj_ref, one_ref, two_ref, head_ref, ada_ref, out_ref, new_ref, *, decay
):
    n = proj_ref.shape[0]
    rows = row_ref[...]
    padded = jnp.concatenate([rows, jnp.zeros((128 - rows.shape[0], n), full_type)], 0).T
    at = 0
    pieces = [(qkv_ref[c], 0) for c in range(3)]
    pieces += [(ref[...], k + 1) for k, ref in enumerate((proj_ref, one_ref, two_ref, head_ref))]
    for values, k in pieces:
        square = values * values
        columns = square.shape[1]
        out_ref[0:1, at : at + columns] = jnp.sum(square, 0, keepdims=True) + n * eps_one
        out_ref[1:2, at : at + columns] = jnp.sum(
            square * (1.0 / padded[:, k : k + 1]), 0, keepdims=True
        )
        at += columns
    columns = ada_ref.shape[1]
    step = 1024
    total = jnp.zeros((n, 1), full_type)
    for start in range(0, columns, step):
        values = ada_ref[:, start : start + step]
        total = total + jnp.sum(values * values, 1, keepdims=True)
    old = jnp.concatenate([old_ref[...], jnp.zeros((127, n), full_type)], 0).T[:, 0:1]
    row = decay * old + (1.0 - decay) * (total / columns + eps_one)
    lane = lax.broadcasted_iota(jnp.int32, (n, 128), 1)
    new_ref[...] = jnp.where(lane == 0, row, 0.0).T[0:8, :]
    for start in range(0, columns, step):
        values = ada_ref[:, start : start + step]
        square = values * values
        out_ref[0:1, at : at + step] = jnp.sum(square, 0, keepdims=True) + n * eps_one
        out_ref[1:2, at : at + step] = jnp.sum(square * (1.0 / row), 0, keepdims=True)
        at += step
    spots = lax.broadcasted_iota(jnp.int32, (1, 128), 1)
    line = tail_ref[...]
    for k in range(5):
        line = jnp.where(spots == k, jnp.sum(rows[k : k + 1, :], 1, keepdims=True), line)
    line = jnp.where(spots == 5, jnp.sum(row, 0, keepdims=True), line)
    line = jnp.where(spots == 10, tables_ref[...], line)
    scales = scale_ref[...]
    for k in range(2):
        value = jnp.sum(jnp.where((spots < 64) == (k == 0), scales, 0.0), 1, keepdims=True)
        line = jnp.where(spots == 11 + k + 2 * at_ref[0], value, line)
    out_ref[0:1, at : at + 128] = line
    out_ref[1:2, at : at + 128] = jnp.zeros_like(line)


def column_stats(at_c, row_new, old, tail, tables_sum, scales, gradients, decay):
    n = gradients[1].shape[0]
    columns = sum(g.size // n for g in gradients)
    return pl.pallas_call(
        functools.partial(column_stats_kernel, decay=decay),
        out_shape=[
            jax.ShapeDtypeStruct((2, columns + 128), full_type),
            jax.ShapeDtypeStruct((8, n), full_type),
        ],
        in_specs=[pl.BlockSpec(memory_space=pltpu.SMEM)]
        + [pl.BlockSpec(memory_space=pltpu.VMEM)] * (5 + len(gradients)),
        compiler_params=pltpu.CompilerParams(vmem_limit_bytes=48 * 2**20),
        cost_estimate=cost("column_stats"),
        name="column_stats",
    )(at_c[None], row_new, old, tail, tables_sum, scales, *gradients)


def finish_kernel(flat_ref, old_ref, col_ref, sum_ref, *, decay, width, starts):
    columns = old_ref.shape[1]
    line = flat_ref[0:1, columns:]
    new = decay * old_ref[...] + (1.0 - decay) * (flat_ref[0:1, :columns] / width)
    col_ref[...] = new
    ratio = flat_ref[1:2, :columns] / new
    spots = lax.broadcasted_iota(jnp.int32, (1, 128), 1)
    out = jnp.zeros((1, 128), full_type)
    for k in range(6):
        mean = jnp.sum(jnp.where(spots == k, line, 0.0), 1, keepdims=True) / width
        value = jnp.sum(ratio[:, starts[k] : starts[k + 1]], 1, keepdims=True) * mean
        out = jnp.where(spots == k, value, out)
    sum_ref[...] = out


def finish(flat, col_old, decay, width, starts):
    return pl.pallas_call(
        functools.partial(finish_kernel, decay=decay, width=width, starts=starts),
        out_shape=[
            jax.ShapeDtypeStruct(col_old.shape, full_type),
            jax.ShapeDtypeStruct((1, 128), full_type),
        ],
        cost_estimate=cost("finish"),
        name="finish",
    )(flat, col_old)


def head_lanes(shape):
    return lax.broadcasted_iota(jnp.int32, shape, len(shape) - 1) < 64


def per_head(values, first):
    left = jnp.sum(jnp.where(first, values, 0.0), -1, keepdims=True)
    right = jnp.sum(jnp.where(first, 0.0, values), -1, keepdims=True)
    return jnp.where(first, left, right)


def attend_kernel(
    q_ref, k_ref, v_ref, gain_ref, cq_ref, sq_ref, ck_ref, proj_ref,
    mix_ref, lse_ref, top_ref, bottom_ref, q_s, k_s, v_s, bias_s, sum_s
):
    length = q_ref.shape[0]
    tile = length // 2
    first = head_lanes((length, 128))
    query = q_ref[...]
    key = k_ref[...]
    q_s[...] = low(
        query * (lax.rsqrt(per_head(query * query, first) / 64.0 + eps_norm) * gain_ref[...])
    )
    k_s[...] = low(key * (lax.rsqrt(per_head(key * key, first) / 64.0 + eps_norm) * 0.125))
    v_s[...] = low(v_ref[...])
    first_t = head_lanes((tile, 128))
    ck = ck_ref[...]

    @pl.when(pl.program_id(0) == 0)
    def _():
        for i in range(2):
            rows = slice(i * tile, (i + 1) * tile)
            shape = (tile, length)
            here = lax.broadcasted_iota(jnp.int32, shape, 1) - lax.broadcasted_iota(jnp.int32, shape, 0)
            keep = ((ck <= cq_ref[rows, :]) & (ck >= sq_ref[rows, :])) | (here == i * tile)
            bias_s[rows, :] = jnp.where(keep, 0.0, -1e30)
        sum_s[...] = jnp.zeros_like(sum_s)

    for i, out_ref in enumerate((top_ref, bottom_ref)):
        rows = slice(i * tile, (i + 1) * tile)
        query_t = q_s[rows, :]
        mixed, logs = [], []
        for head in range(2):
            chosen = first_t if head == 0 else ~first_t
            scores = dot_nt(jnp.where(chosen, query_t, jnp.zeros_like(query_t)), k_s[...]) + bias_s[rows, :]
            peak = jnp.max(scores, -1, keepdims=True)
            exponent = jnp.exp(scores - peak)
            total = jnp.sum(exponent, -1, keepdims=True)
            mixed.append(dot_nn(low(exponent * (1.0 / total)), v_s[...]))
            logs.append(peak + jnp.log(total))
        mixed = low(jnp.where(first_t, mixed[0], mixed[1]))
        mix_ref[rows, :] = mixed
        turned = jnp.where(first_t, logs[0], logs[1]).T
        lse_ref[0, 0:1, rows] = turned[0:1, :]
        lse_ref[0, 1:2, rows] = turned[64:65, :]
        part = sum_s[rows, :] + dot_nt(mixed, proj_ref[...])
        sum_s[rows, :] = part

        @pl.when(pl.program_id(0) == pl.num_programs(0) - 1)
        def _():
            out_ref[...] = low(part)


def attend(qkv, gain, cq, sq, ck, proj):
    length = qkv.shape[0]
    pairs = qkv.shape[1] // 384
    width = proj.shape[0]
    column = pl.BlockSpec((length, 1), lambda p: (0, 0))
    block = pl.BlockSpec((length, 128), lambda p: (0, p))
    return call(
        attend_kernel,
        (pairs,),
        [
            block,
            pl.BlockSpec((length, 128), lambda p: (0, pairs + p)),
            pl.BlockSpec((length, 128), lambda p: (0, 2 * pairs + p)),
            pl.BlockSpec((1, 128), lambda p: (0, p)),
            column,
            column,
            pl.BlockSpec((1, length), lambda p: (0, 0)),
            pl.BlockSpec((width, 128), lambda p: (0, p)),
        ],
        [block, pl.BlockSpec((1, 2, length), lambda p: (p, 0, 0))] + [fixed((length // 2, width))] * 2,
        [((length, 128 * pairs), low_type), ((pairs, 2, length), full_type)]
        + [((length // 2, width), low_type)] * 2,
        [pltpu.VMEM((length, 128), low_type)] * 3
        + [pltpu.VMEM((length, length), full_type), pltpu.VMEM((length, width), full_type)],
        "attend",
    )(qkv, qkv, qkv, gain, cq[:, None], sq[:, None], ck[None, :], proj)


def attend_back_kernel(
    q_ref, k_ref, v_ref, gain_ref, cq_ref, sq_ref, ck_ref, lse_ref, pa_ref, pb_ref, pc_ref, pd_ref,
    proj_ref, wq_ref, wk_ref, wv_ref, row_ref, d_ref, ds_ref, top_ref, bottom_ref,
    q_s, k_s, v_s, dm_ref, dqa, dka, dva, sum_s, *, tile
):
    length = q_ref.shape[0]
    first = head_lanes((length, 128))
    query = q_ref[...]
    key = k_ref[...]
    gain = gain_ref[...]
    q_n = lax.rsqrt(per_head(query * query, first) / 64.0 + eps_norm)
    k_n = lax.rsqrt(per_head(key * key, first) / 64.0 + eps_norm)
    q_s[...] = low(query * (q_n * gain))
    k_s[...] = low(key * (k_n * 0.125))
    v_s[...] = low(v_ref[...])
    quarter = length // 4
    for k, ref in enumerate((pa_ref, pb_ref, pc_ref, pd_ref)):
        rows = slice(k * quarter, (k + 1) * quarter)
        dm_ref[rows, :] = low(dot_nn(ref[...], proj_ref[...]))

    @pl.when(pl.program_id(0) == 0)
    def _():
        sum_s[...] = jnp.zeros_like(sum_s)
        for k, ref in enumerate((pa_ref, pb_ref, pc_ref, pd_ref)):
            row_ref[k * quarter : (k + 1) * quarter, :] = ref[...]

    dka[...] = jnp.zeros_like(dka)
    dva[...] = jnp.zeros_like(dva)
    first_t = head_lanes((tile, 128))
    ck = ck_ref[...]

    def step(i, carry):
        rows = pl.ds(pl.multiple_of(i * tile, tile), tile)
        query_t = q_s[rows, :]
        dmix_t = dm_ref[rows, :]
        shape = (length, tile)
        here = lax.broadcasted_iota(jnp.int32, shape, 0) - lax.broadcasted_iota(jnp.int32, shape, 1)
        keep = ((ck <= cq_ref[:, rows]) & (ck >= sq_ref[:, rows])) | (here == i * tile)
        d_query = []
        for head in range(2):
            chosen = first_t if head == 0 else ~first_t
            zero = jnp.zeros_like(query_t)
            query_h = jnp.where(chosen, query_t, zero)
            dmix_h = jnp.where(chosen, dmix_t, zero)
            scores = dot_nt(k_s[...], query_h)
            attention = jnp.where(keep, jnp.exp(scores - lse_ref[0, head : head + 1, rows]), 0.0)
            dva[...] += dot_nn(low(attention), dmix_h)
            d_att = dot_nt(v_s[...], dmix_h)
            inner = jnp.sum(attention * d_att, 0, keepdims=True)
            d_scores = low(attention * (d_att - inner))
            dka[...] += dot_nn(d_scores, query_h)
            d_query.append(dot_tn(d_scores, k_s[...]))
        dqa[rows, :] = jnp.where(first_t, d_query[0], d_query[1])
        return carry

    lax.fori_loop(0, length // tile, step, 0)
    q_hat = query * q_n
    k_hat = key * k_n
    d_query = dqa[...]
    along = d_query * q_hat
    ds_ref[0] = jnp.sum(along, 0, keepdims=True) * gain
    group = d_ref.shape[1] // 3
    start = pl.program_id(0) * 128

    def columns(c):
        return pl.ds(pl.multiple_of(start + c * group, 128), 128)

    out_q = low(gain * (d_query - q_hat * (per_head(along, first) / 64.0)) * q_n)
    d_ref[:, columns(0)] = out_q
    d_key = dka[...]
    out_k = low(
        0.125 * (d_key - k_hat * (per_head(d_key * k_hat, first) / 64.0)) * k_n
    )
    out_v = low(dva[...])
    d_ref[:, columns(1)] = out_k
    d_ref[:, columns(2)] = out_v
    half = length // 2
    for rows, out_ref in ((slice(0, half), top_ref), (slice(half, length), bottom_ref)):
        part = sum_s[rows, :] + dot_nt(out_q[rows], wq_ref[...])
        part = part + dot_nt(out_k[rows], wk_ref[...]) + dot_nt(out_v[rows], wv_ref[...])
        sum_s[rows, :] = part

        @pl.when(pl.program_id(0) == pl.num_programs(0) - 1)
        def _():
            out_ref[...] = low(part)


def attend_back(qkv, gain, cq, sq, ck, lse, pieces, proj, w):
    length = qkv.shape[0]
    pairs = qkv.shape[1] // 384
    width = proj.shape[0]
    row = pl.BlockSpec((1, length), lambda p: (0, 0))

    def part(rows, number):
        return pl.BlockSpec((rows, 128), lambda p: (0, number * pairs + p))

    return call(
        functools.partial(attend_back_kernel, tile=256),
        (pairs,),
        [
            part(length, 0),
            part(length, 1),
            part(length, 2),
            pl.BlockSpec((1, 128), lambda p: (0, p)),
            row,
            row,
            pl.BlockSpec((length, 1), lambda p: (0, 0)),
            pl.BlockSpec((1, 2, length), lambda p: (p, 0, 0)),
        ]
        + [whole(pieces[0].shape)] * 4
        + [part(width, 0), part(width, 0), part(width, 1), part(width, 2)],
        [
            fixed((length, width)),
            fixed((length, 384 * pairs)),
            pl.BlockSpec((1, 1, 128), lambda p: (p, 0, 0)),
            fixed((length // 2, width)),
            fixed((length // 2, width)),
        ],
        [
            ((length, width), low_type),
            ((length, 384 * pairs), low_type),
            ((pairs, 1, 128), full_type),
            ((length // 2, width), low_type),
            ((length // 2, width), low_type),
        ],
        [pltpu.VMEM((length, 128), low_type)] * 4
        + [pltpu.VMEM((length, 128), full_type)] * 3
        + [pltpu.VMEM((length, width), full_type)],
        "attend_back",
    )(qkv, qkv, qkv, gain, cq[None, :], sq[None, :], ck[:, None], lse, *pieces, proj, w, w, w)


def body(
    vq_in, codes, segment, live, labels, level_weight, qkv_w, proj_w, fc1_w, fc2_w, head_w, ada_w,
    tables, head_scale, d_stats, qkv_stat, proj_stat, fc1_stat, fc2_stat, head_stat, ada_stat,
    tables_v, scale_v,
):
    g_count = lax.axis_size("g")
    dp_count = g_count * lax.axis_size("c")
    mp_count = lax.axis_size("h") * lax.axis_size("l")
    at_c, at_h, at_l = lax.axis_index("c"), lax.axis_index("h"), lax.axis_index("l")
    row_count, seq_len, code_dim = vq_in.shape
    item_count = labels.shape[1]
    level_count = level_weight.shape[0]
    slice_width = tables.shape[1]
    width = slice_width * dp_count
    half, quarter = seq_len // 2, seq_len // 4
    table_rows = tables.shape[0]
    lead = code_dim + level_count
    per_row = row_count * item_count
    note_rows = -(-(2 * per_row + 3) // slice_width)
    lead_pad = -(-(lead + note_rows) // 16) * 16

    def halves(a):
        n = a.shape[-1] // 2
        lower, upper = low(a[..., :n]), low(a[..., n:])
        return jnp.where(at_c == 0, lower, upper), jnp.where(at_c == 0, upper, lower)

    first_mine, first_other = halves(jnp.concatenate([qkv_w, proj_w.T[None]], 0))
    first_near = ordered(at_c, first_mine, over_c(first_other), 1)
    first_far = over_h(first_near)

    place, weight, weight_here = row_layout(level_weight, segment, live)
    weight_here = weight_here[0, 0]

    per_row = row_count * item_count
    note_rows = -(-(2 * per_row + 3) // slice_width)
    lead_pad = -(-(lead + note_rows) // 16) * 16
    tables_low = low(tables)
    label_flat = labels.reshape(-1)
    digits = jnp.stack([weight_here // 4096, (weight_here // 64) % 64, weight_here % 64])
    note = jnp.concatenate([label_flat // 32, label_flat % 32, digits])
    note = jnp.pad(low(note), (0, (lead_pad - lead) * slice_width - note.shape[0]))
    note = note.reshape(lead_pad - lead, slice_width)
    packed = tie(jnp.concatenate([tables_low[:lead], note], 0), first_near)
    gathered = lax.all_gather(packed, DP, axis=0)
    lead_table = jnp.transpose(gathered, (1, 0, 2)).reshape(lead_pad, width)
    notes = gathered[:, lead : lead + note_rows].reshape(dp_count, -1).astype(jnp.int32)
    labels_all = (notes[:, :per_row] * 32 + notes[:, per_row : 2 * per_row]).reshape(-1)
    weight_sum = full(
        jnp.sum(
            notes[:, 2 * per_row] * 4096
            + notes[:, 2 * per_row + 1] * 64
            + notes[:, 2 * per_row + 2]
        )
    )

    class_hot = (
        labels_all[:, None] + lead == jnp.arange(table_rows, dtype=jnp.int32)[None, :]
    )
    class_vec = dot_nn(low(class_hot), tables_low)
    sigma = jax.nn.sigmoid(class_vec)
    activated = low(class_vec * sigma)
    act_pairs = activated.reshape(g_count, 2, per_row, slice_width)
    act_mine = jnp.where(at_h == 0, act_pairs[:, 0], act_pairs[:, 1]).reshape(-1, slice_width)
    ada_low = low(ada_w)
    mod_part = dot_nn(act_mine, ada_low)
    mod_half = ada_w.shape[1] // 2
    left, right = mod_part[:, :mod_half], mod_part[:, mod_half:]
    mod_send = jnp.where(at_c == 0, right, left)
    mod_sum = jnp.where(at_c == 0, left, right) + over_c(mod_send)
    mod_sum = scatter_g(mod_sum)
    mod_items = ordered(at_c, mod_sum, over_c(mod_sum), 1).reshape(row_count, item_count, 8, width)
    mod_rows = jnp.transpose(mod_items, (0, 2, 1, 3))

    codes, place, live, weight, vq_in, head_gain = tie(
        (codes, place, live, weight, vq_in, head_scale), gathered
    )
    fc1_wide, fc2_wide, head_wide = tie((fc1_w, fc2_w, head_w), mod_send)
    qkv_piece = ordered(at_h, first_near[None], first_far[None], 0)
    qkv_pieces = [qkv_piece] + [over_g(qkv_piece, k) for k in range(1, 4)]

    def near_rows(w):
        kept, other = halves(w)
        return ordered(at_c, kept, over_c(other), 0)

    def gathered_weight(a):
        return lax.all_gather(a, ("h", "g"), axis=0, tiled=True).reshape(2, width, -1)

    feed_near = jnp.concatenate([near_rows(fc1_wide), near_rows(fc2_wide.T)], 1)
    head_near = near_rows(head_wide)

    mine = at_c == at_h
    info = jnp.stack([codes, place, live, weight])
    info = jnp.where(mine, info, over_c(info))
    vq_rows = jnp.where(mine, vq_in, over_c(vq_in))

    def relative(a, axis):
        shape = a.shape
        a = a.reshape(shape[:axis] + (2, 2, quarter) + shape[axis + 1 :])
        a = jnp.where(at_c == 0, a, jnp.flip(a, axis))
        return jnp.where(at_l == 0, a, jnp.flip(a, axis + 1)).reshape(shape)

    info = relative(info, 2)
    vq_rows = relative(vq_rows, 1)
    code_r, place_r, live_r, weight_r = info[0], info[1], info[2], info[3]
    seg_r, level_r = place_r // 16, place_r % 16
    base_r = seg_r * 16
    key_r = jnp.where(live_r > 0, place_r, 1 << 20)
    level_hot = low(
        level_r[..., None] == jnp.arange(lead_pad - code_dim, dtype=jnp.int32)
    )
    feats = jnp.concatenate([vq_rows, level_hot], 2)
    spot = jnp.arange(16, dtype=jnp.int32)
    hot = low((seg_r[..., None] == spot % 4) & (spot < 12))

    def window(*values):
        return lax.optimization_barrier(values)

    def far_part(r):
        return low(full(top[r][quarter:]) + full(moved[r][quarter:]))

    def await_head():
        return held[0]

    def turn(norm, kernel, filler=lambda: None, beside=None):
        moved[1] = over_c(bottom[1])
        first, moved[1] = window(norm(0, (top[0], moved[0], across[0])), moved[1])
        across[1] = over_l(far_part(1))
        pieces = [[first, over_l(first), over_c(first), None], None]
        done, across[1], pieces[0][2] = window(filler(), across[1], pieces[0][2])
        if done is not None and filler is await_head:
            held[0] = done
        second, pieces[0][1] = window(norm(1, (top[1], moved[1], across[1])), pieces[0][1])
        pieces[1] = [second, over_l(second), over_c(second), None]
        pieces[0][3] = over_c(pieces[0][1])
        kernel_out, pieces[1], beside = window(kernel(0, pieces[0]), pieces[1][:3], beside)
        return pieces, kernel_out, done, beside

    def launch():
        moved[0] = over_c(bottom[0])
        sent = far_part(0)
        across[0] = over_l(sent)
        return sent

    gain_own = jnp.where(at_c == 0, head_gain[:2], head_gain[2:])
    gains = jnp.exp(ordered(at_h, gain_own, over_h(gain_own), 0)) / 8.0
    gain_row = jnp.repeat(gains, 64)[None, :]
    inputs_one, qkv_rows, mixed_rows, lse_rows, top, bottom, stream_zero = ([None] * 2 for _ in range(7))
    if g_count == 4:
        inputs_one[0], qkv_rows[0], stream_zero[0], qkv_full, proj_full = enter_first(
            lax.axis_index("g"), feats[0], lead_table, hot[0], mod_rows[0], qkv_pieces
        )
    else:
        wide_piece = lax.all_gather(qkv_piece, "g", axis=0)
        wide_piece = jnp.transpose(wide_piece, (0, 3, 2, 1, 4)).reshape(width, -1)
        qkv_full, proj_full = wide_piece[:, :768], wide_piece[:, 768:]
        inputs_one[0], qkv_rows[0], stream_zero[0] = enter(feats[0], lead_table, hot[0], mod_rows[0], qkv_full)
    feed_full = gathered_weight(tie(feed_near, qkv_rows[0]))
    head_full = gathered_weight(tie(head_near, qkv_rows[0]))
    held = [head_full]

    moved, across = [None] * 2, [None] * 2

    def attention(r, given):
        mixed_rows[r], lse_rows[r], top[r], bottom[r] = attend(
            given, gain_row, place_r[r], base_r[r], key_r[r], proj_full
        )
        return top[r], bottom[r]

    attention(0, qkv_rows[0])
    moved[0] = over_c(bottom[0])
    (inputs_one[1], qkv_rows[1], stream_zero[1]), moved[0] = window(
        enter(tie(feats[1], bottom[0]), lead_table, hot[1], mod_rows[1], qkv_full), moved[0]
    )
    sent = far_part(0)
    across[0] = over_l(sent)
    (top[1], bottom[1]), across[0] = window(attention(1, tie(qkv_rows[1], sent)), across[0])

    branch_one, stream_one, acts, slopes, inputs_two = ([None] * 2 for _ in range(5))

    def norm_two(r, parts):
        branch_one[r], stream_one[r], given = onward(parts, stream_zero[r], hot[r], mod_rows[r], (2, 3, 4))
        return given

    def forward(r, pieces):
        inputs_two[r], acts[r], slopes[r], top[r], bottom[r] = feed(pieces, feed_full)
        return top[r], bottom[r]

    pieces_two, (top[0], bottom[0]), olds, _ = turn(
        norm_two,
        forward,
        lambda: old_stats(qkv_w, proj_w, fc1_w, fc2_w, head_w, ada_w, tables, head_scale[None]),
    )
    pieces_two[1].append(over_c(pieces_two[1][1]))
    sent = launch()
    (top[1], bottom[1]), across[0] = window(
        forward(1, [tie(pieces_two[1][0], sent)] + pieces_two[1][1:]), across[0]
    )

    block_codes = head_w.shape[1]
    half_codes = block_codes // 2
    column = jnp.arange(2 * half_codes, dtype=jnp.int32)
    block_here = (column // half_codes) * 2 + at_l
    column_code = (block_here * block_codes + at_c * half_codes + column % half_codes)[None, :]
    code_column = [code_r[r][:, None] for r in range(2)]
    branch_two, stream_two, logits, stats, d_logits, losses, others, inputs_out = ([None] * 2 for _ in range(8))

    def norm_out(r, parts):
        branch_two[r], stream_two[r], given = onward(parts, stream_one[r], hot[r], mod_rows[r], (5, 6, 7))
        return given

    def score(r, pieces):
        inputs_out[r], logits[r], stats[r] = head(pieces, held[0], code_column[r], column_code)
        return stats[r]

    def compare(r):
        return [over_c(stats[r]), over_l(stats[r]), over_cl(stats[r])]

    def score_back(r):
        lines, losses[r] = merge(weight_sum, stats[r], *others[r], full(weight_r[r])[None, :])
        d_logits[r], top[r], bottom[r] = head_back(logits[r], held[0], code_column[r], column_code, lines)
        return top[r], bottom[r]

    pieces_out, stats[0], _, _ = turn(norm_out, score, await_head)
    pieces_out[1].append(over_c(pieces_out[1][1]))
    stats[1], others[0] = window(score(1, pieces_out[1]), compare(0))
    (top[0], bottom[0]), others[1] = window(score_back(0), compare(1))
    sent = launch()
    logits[1] = tie(logits[1], sent)
    (top[1], bottom[1]), across[0] = window(score_back(1), across[0])

    def reduced(a):
        shape = a.shape[1:]
        a = lax.psum_scatter(a.reshape(-1, shape[2]), "g", scatter_dimension=0, tiled=True)
        return a.reshape(shape)

    def theirs(a):
        return jnp.where(at_h == 0, a[1], a[0])

    def settle(a, other):
        a = full(jnp.where(at_h == 0, a[0], a[1])) + full(other)
        rows = a.shape[0] // 2
        kept = jnp.where(at_c == 0, a[:rows], a[rows:])
        return kept, over_c(jnp.where(at_c == 0, a[rows:], a[:rows]))

    d_two, d_one, items_out, items_two, d_hidden, d_branch_two, d_branch_one = ([None] * 2 for _ in range(7))

    def back_out(r, parts):
        d_two[r], given, items_out[r] = back(
            parts, stream_two[r], hot[r], mod_rows[r], (7, 5), None, branch_two[r], None
        )
        return given

    def backward(r, pieces):
        d_branch_two[r], d_hidden[r], top[r], bottom[r] = feed_back(pieces, slopes[r], feed_full)
        return top[r], bottom[r]

    pieces_d_two, (top[0], bottom[0]), head_part, _ = turn(
        back_out, backward, lambda: head_grad_of(inputs_out, d_logits, g_count)
    )
    head_sum = reduced(head_part)
    pieces_d_two[1].append(over_c(pieces_d_two[1][1]))
    sent = launch()
    (top[1], bottom[1]), across[0], head_sum = window(
        backward(1, [tie(pieces_d_two[1][0], sent)] + pieces_d_two[1][1:]), across[0], head_sum
    )

    d_qkv, scale_rows = ([None] * 2 for _ in range(2))

    def back_two(r, parts):
        d_one[r], given, items_two[r] = back(
            parts, stream_one[r], hot[r], mod_rows[r], (4, 2), d_two[r], branch_one[r], None
        )
        return given

    def attention_back(r, pieces):
        d_branch_one[r], d_qkv[r], scale_rows[r], top[r], bottom[r] = attend_back(
            qkv_rows[r], gain_row, place_r[r], base_r[r], key_r[r], lse_rows[r], pieces, proj_full, qkv_full
        )
        return top[r], bottom[r]

    pieces_d_one, (top[0], bottom[0]), feed_part, head_other = turn(
        back_two,
        attention_back,
        lambda: feed_grad_of(inputs_two, d_hidden, d_branch_two, acts, g_count),
        over_h(theirs(head_sum)),
    )
    feed_sum = reduced(feed_part)
    pieces_d_one[1].append(over_c(pieces_d_one[1][1]))
    sent = launch()
    leaving = theirs(feed_sum)
    (top[1], bottom[1]), across[0], feed_other = window(
        attention_back(1, [tie(pieces_d_one[1][0], sent, leaving)] + pieces_d_one[1][1:]), across[0], over_h(leaving)
    )
    moved[1] = over_c(bottom[1])
    items_one, lead_parts = ([None] * 2 for _ in range(2))

    def back_one(r, parts):
        items_one[r], lead_parts[r] = back(
            parts, stream_zero[r], hot[r], mod_rows[r], (1,), d_one[r], None, feats[r]
        )
        return items_one[r]

    items_one[0], moved[1] = window(back_one(0, (top[0], moved[0], across[0])), moved[1])
    sent = far_part(1)
    across[1] = over_l(sent)
    first_part = first_grad_of(inputs_one, tie(d_qkv, sent), d_branch_one, mixed_rows, g_count)
    first_part, across[1] = window(first_part, across[1])
    first_sum = reduced(first_part)
    back_one(1, (top[1], moved[1], across[1]))
    lead_part = lead_parts[0] + lead_parts[1]

    def flat_items(items, number):
        return jnp.concatenate([items[r][number, :item_count] for r in range(2)], 0)

    d_items = jnp.concatenate(
        [flat_items(items_one, 0), flat_items(items_one, 1), flat_items(items_two, 2)]
        + [flat_items(items_two, 0), flat_items(items_two, 1), flat_items(items_out, 2)]
        + [flat_items(items_out, 0), flat_items(items_out, 1)],
        1,
    )
    left, right = d_items[:, :mod_half], d_items[:, mod_half:]
    d_items = jnp.where(at_c == 0, left, right) + over_c(jnp.where(at_c == 0, right, left))
    d_items = low(d_items + over_l(d_items))
    d_items = gather_g(ordered(at_h, d_items, over_h(d_items), 0))
    d_items = ordered(at_c, d_items, over_c(d_items), 1)
    ada_grad = dot_tn(activated, d_items)
    d_act_vec = dot_nt(d_items, ada_low)
    d_class = d_act_vec * (sigma * (1.0 + class_vec * (1.0 - sigma)))
    lead_part = jnp.transpose(lead_part.reshape(lead_pad, dp_count, slice_width), (1, 0, 2))
    lead_grad = jnp.sum(lax.all_to_all(lead_part, DP, 0, 0, tiled=True).reshape(dp_count, lead_pad, slice_width), 0)
    lead_grad = lead_grad + over_l(lead_grad)
    lead_grad = lead_grad + over_h(lead_grad)
    tables_grad = dot_tn(full(class_hot), d_class, highest)
    tables_grad = tables_grad + jnp.pad(lead_grad[:lead], ((0, table_rows - lead), (0, 0)))

    head_grad = ordered(at_c, *settle(tie(head_sum, items_one[0]), head_other), 1)
    kept, moved_half = settle(feed_sum, feed_other)
    n = kept.shape[1] // 2
    fc1_grad = ordered(at_c, kept[:, :n], moved_half[:, :n], 1)
    fc2_grad = ordered(at_c, kept[:, n:], moved_half[:, n:], 1)
    kept, moved_half = settle(first_sum, over_h(theirs(first_sum)))
    first_halves = jnp.stack([kept, moved_half])
    first_halves = jnp.where(at_c == 0, first_halves, first_halves[::-1])
    first_halves = jnp.transpose(first_halves.reshape(2, slice_width, 4, -1), (2, 1, 0, 3))
    first_halves = first_halves.reshape(4, slice_width, -1)
    qkv_grad, proj_grad = first_halves[:3], first_halves[3]

    decay = 1.0 - STEP ** (-0.8)
    grads = [qkv_grad, proj_grad, fc1_grad, fc2_grad, head_grad, ada_grad]
    masters = [qkv_w, proj_w.T, fc1_w, fc2_w.T, head_w, ada_w]
    wide = [g.size // slice_width * (mp_count if k < 5 else 1) for k, g in enumerate(grads)]
    sizes = [g.size // slice_width for g in grads]
    starts = [sum(sizes[:k]) for k in range(7)]

    def over_mp(a):
        a = a + over_l(a)
        return a + over_h(a)

    spots = jnp.arange(128, dtype=jnp.int32)[None, :]
    early_line = over_mp(tie(olds[:1] + jnp.where(spots == 22, losses[0] + losses[1], 0.0), lead_part))
    tail = early_line + olds[1:]
    rows_all = over_mp(row_stats(*grads[:5]))
    wide_column = jnp.array(wide[:5], full_type)[:, None]
    row_new = decay * d_stats[:5] + (1.0 - decay) * (rows_all[:5] / wide_column)
    tables_v_new = decay * tables_v + (1.0 - decay) * (tables_grad * tables_grad + eps_one)
    tables_step = tables_grad * lax.rsqrt(tables_v_new)
    tables_sum = jnp.sum(tables_step * tables_step)[None, None]
    scales = tie(scale_rows[0] + scale_rows[1], lead_part)
    scales = jnp.where(at_h == 0, scales[0], scales[1]) + over_h(
        jnp.where(at_h == 0, scales[1], scales[0])
    )
    flat, ada_row = column_stats(at_c, row_new, d_stats[5:6], tail, tables_sum, scales, grads, decay)
    d_stats_new = jnp.concatenate([row_new, ada_row[:1]], 0)
    if g_count == 4:
        flat = flat + over_c(flat)
        flat = flat + over_g(flat, 1)
        flat = flat + over_g(flat, 2)
    else:
        flat = lax.psum(flat, DP)
    col_old = jnp.concatenate(
        [qkv_stat.reshape(-1), proj_stat, fc1_stat, fc2_stat, head_stat, ada_stat]
    )[None, :]
    col_line, sum_line = finish(flat, col_old, decay, width, starts)
    col_new = [col_line[0, starts[k] : starts[k + 1]] for k in range(6)]
    line = flat[:1, starts[6] :]
    scale_grad = line[0, 11:15]
    loss_sum = line[0, 22]
    scale_v_new = decay * scale_v + (1.0 - decay) * (scale_grad * scale_grad + eps_one)
    scale_step = scale_grad * lax.rsqrt(scale_v_new)
    scale_spot = jnp.where(spots == 7, jnp.sum(scale_step * scale_step), 0.0)
    split = over_mp(jnp.where(spots == 5, 0.0, sum_line) + scale_spot)
    step_line = split + jnp.where(spots == 5, sum_line, 0.0)
    step_line = step_line + jnp.where(spots == 6, line[0, 10], 0.0)
    weight_line = jnp.zeros((1, 128), full_type)
    for k, value in enumerate([line[0, 16 + j] for j in range(5)] + [line[0, 8], line[0, 9], early_line[0, 21]]):
        weight_line = jnp.where(spots == k, value, weight_line)
    entries = [width * wide[k] for k in range(6)] + [table_rows * width, head_scale.shape[0] * mp_count]
    entry_line = jnp.array(entries + [1] * 120, full_type)[None, :]
    ratio = jnp.sqrt(step_line / entry_line) / clip_rms
    spread = jnp.maximum(eps_two, jnp.sqrt(weight_line / entry_line))
    factor = (rate_step * spread / jnp.maximum(1.0, ratio))[0]
    row_mean = line[0, :6] / width
    sides = [col_new[0].reshape(3, 1, -1)] + [c[None, :] for c in col_new[1:]]
    raw_steps = [
        grads[k] * lax.rsqrt(d_stats_new[k][:, None] * sides[k] / row_mean[k]) for k in range(6)
    ] + [tables_step, scale_step]
    parameters = masters + [tables, head_scale]
    news = [parameters[k] - factor[k] * raw_steps[k] for k in range(8)]
    return (
        loss_sum,
        weight_sum,
        qkv_grad,
        proj_grad.T,
        fc1_grad,
        fc2_grad.T,
        head_grad,
        ada_grad,
        tables_grad,
        scale_grad,
        d_stats_new,
        col_new[0].reshape(3, -1),
        col_new[1],
        col_new[2],
        col_new[3],
        col_new[4],
        col_new[5],
        tables_v_new,
        scale_v_new,
        news[0],
        news[1].T,
        news[2],
        news[3].T,
        news[4],
        news[5],
        news[6],
        news[7],
    )


def solution(mesh):
    inner = Mesh(
        mesh.devices.reshape(mesh.shape["dp"] // 2, 2, mesh.shape["mp"] // 2, 2),
        ("g", "c", "h", "l"),
    )
    return jax.shard_map(
        body,
        mesh=inner,
        in_specs=(
            P(DP, None, None),
            P(DP, None),
            P(DP, None),
            P(DP, None),
            P(DP, None),
            P(),
            P(None, DP, MP),
            P(MP, DP),
            P(DP, MP),
            P(MP, DP),
            P(DP, MP),
            P(DP, None),
            P(None, DP),
            P(MP),
            P(None, DP),
            P(None, MP),
            P(MP),
            P(MP),
            P(MP),
            P(MP),
            P(),
            P(None, DP),
            P(MP),
        ),
        out_specs=(
            P(),
            P(),
            P(None, DP, MP),
            P(MP, DP),
            P(DP, MP),
            P(MP, DP),
            P(DP, MP),
            P(DP, None),
            P(None, DP),
            P(MP),
            P(None, DP),
            P(None, MP),
            P(MP),
            P(MP),
            P(MP),
            P(MP),
            P(),
            P(None, DP),
            P(MP),
            P(None, DP, MP),
            P(MP, DP),
            P(DP, MP),
            P(MP, DP),
            P(DP, MP),
            P(DP, None),
            P(None, DP),
            P(MP),
        ),
        check_vma=False,
    )
```

```python
import functools
import math

import jax
import jax.numpy as jnp
from jax import lax
from jax.experimental import pallas as pl
from jax.experimental.pallas import tpu as pltpu
from jax.sharding import Mesh, PartitionSpec as P

STEP = 8
level_starts = (1, 5, 14, 30, 55, 91, 155, 255, 424)
eps_norm = 1e-06
eps_one = 1e-30
eps_two = 0.001
rate_step = 0.3
clip_rms = 1.0
low_type = jnp.bfloat16
full_type = jnp.float32
high = lax.Precision.HIGH
highest = lax.Precision.HIGHEST
swap_pairs = ((0, 1), (1, 0))
busy_us = {
    "row_layout": 2, "enter": 5, "enter_first": 6, "attend": 11, "onward": 4, "feed": 9, "head": 6, "merge": 2,
    "head_back": 5, "back": 5, "feed_back": 7, "attend_back": 16, "old_stats": 4, "row_stats": 3,
    "column_stats": 5, "finish": 2, "head_grad": 6, "feed_grad": 12, "first_grad": 6,
    "renew": 8, "arrange": 4,
}
DP = ("g", "c")
MP = ("h", "l")


def cost(name):
    return pl.CostEstimate(flops=busy_us[name] * 10**9, transcendentals=0, bytes_accessed=busy_us[name] * 10**6)


def low(a):
    return a.astype(low_type)


def full(a):
    return a.astype(full_type)


def dot_nn(a, b, precision=None):
    return jnp.dot(a, b, preferred_element_type=full_type, precision=precision)


def dot_nt(a, b, precision=None):
    return lax.dot_general(
        a, b, (((1,), (1,)), ((), ())), preferred_element_type=full_type, precision=precision
    )


def dot_tn(a, b, precision=None):
    return lax.dot_general(
        a, b, (((0,), (0,)), ((), ())), preferred_element_type=full_type, precision=precision
    )


def over_c(a):
    return lax.ppermute(a, "c", swap_pairs)


def over_l(a):
    return lax.ppermute(a, "l", swap_pairs)


def over_h(a):
    return lax.ppermute(a, "h", swap_pairs)


def over_cl(a):
    return lax.ppermute(a, ("c", "l"), [(i, i ^ 3) for i in range(4)])


def over_g(a, k):
    return lax.ppermute(a, "g", [(i, i ^ k) for i in range(lax.axis_size("g"))])


def ordered(flag, mine, other, axis):
    return jnp.where(
        flag == 0,
        jnp.concatenate([mine, other], axis),
        jnp.concatenate([other, mine], axis),
    )


def gather_g(a):
    count = lax.axis_size("g")
    if count != 4:
        return lax.all_gather(a, "g", axis=0, tiled=True)
    here = lax.axis_index("g")
    out = jnp.zeros((4,) + a.shape, a.dtype)
    for k in range(4):
        piece = a if k == 0 else over_g(a, k)
        out = lax.dynamic_update_index_in_dim(out, piece, here ^ k, 0)
    return out.reshape((4 * a.shape[0],) + a.shape[1:])


def scatter_g(a):
    count = lax.axis_size("g")
    if count != 4:
        return full(lax.psum_scatter(a, "g", scatter_dimension=0, tiled=True))
    here = lax.axis_index("g")
    blocks = a.reshape((4, a.shape[0] // 4) + a.shape[1:])
    total = full(lax.dynamic_index_in_dim(blocks, here, 0, False))
    for k in range(1, 4):
        total = total + full(over_g(lax.dynamic_index_in_dim(blocks, here ^ k, 0, False), k))
    return total


def tie(a, *others):
    return lax.optimization_barrier((a,) + others)[0]


def centre(values):
    centered = values - jnp.mean(values, -1, keepdims=True)
    scale = lax.rsqrt(jnp.mean(centered * centered, -1, keepdims=True) + eps_norm)
    return centered * scale, scale


def centre_back(normed, scale, incoming):
    return (
        incoming
        - jnp.mean(incoming, -1, keepdims=True)
        - normed * jnp.mean(incoming * normed, -1, keepdims=True)
    ) * scale


def gelu_parts(values):
    root = math.sqrt(2.0 / math.pi)
    square = values * values
    bent = jnp.tanh(values * (root + (root * 0.044715) * square))
    half = 0.5 + 0.5 * bent
    slope = half + values * (0.5 - 0.5 * (bent * bent)) * (root + (root * 3.0 * 0.044715) * square)
    return values * half, slope


def split_parts(a, count):
    parts = []
    for _ in range(count):
        parts.append(low(a))
        a = a - full(parts[-1])
    return parts


def item_parts(vectors):
    return jnp.concatenate(split_parts(vectors, 3) + [jnp.zeros(vectors.shape, low_type)], 0)


def item_sums(hot, values):
    upper, lower = split_parts(values, 2)
    return (dot_tn(hot, upper) + dot_tn(hot, lower))[:8]


def whole(shape):
    return pl.BlockSpec(shape, lambda i: (0,) * len(shape), pipeline_mode=pl.Buffered(1))


def tiled(tile, columns):
    return pl.BlockSpec((tile, columns), lambda i: (i, 0))


def call(kernel, grid, in_specs, out_specs, out_shape, scratch, name):
    return pl.pallas_call(
        kernel,
        grid=grid,
        in_specs=in_specs,
        out_specs=out_specs,
        out_shape=[jax.ShapeDtypeStruct(shape, dtype) for shape, dtype in out_shape],
        scratch_shapes=scratch,
        compiler_params=pltpu.CompilerParams(vmem_limit_bytes=48 * 2**20),
        cost_estimate=cost(name),
        name=name,
    )


def rows_kernel(lw_ref, seg_ref, live_ref, place_ref, weight_ref, sum_ref):
    seg, live = seg_ref[...], live_ref[...]
    at = lax.broadcasted_iota(jnp.int32, seg.shape, 1)
    first = jnp.zeros_like(seg)
    for item in range(1, 4):
        count = jnp.sum(full(jnp.where(seg < item, 1, 0)), 1, keepdims=True).astype(jnp.int32)
        first = jnp.where(seg == item, count, first)
    within = at - first
    level = jnp.zeros_like(seg)
    for start in level_starts:
        level = level + jnp.where(within >= start, 1, 0)
    weight = jnp.zeros_like(seg)
    for position in range(lw_ref.shape[0]):
        weight = jnp.where(level == position, lw_ref[position], weight)
    weight = weight * live
    place_ref[...] = seg * 16 + level
    weight_ref[...] = weight
    each = jnp.sum(full(weight), 1, keepdims=True)
    sum_ref[...] = jnp.sum(each, 0, keepdims=True).astype(jnp.int32)


def row_layout(level_weight, segment, live):
    shape = segment.shape
    return pl.pallas_call(
        rows_kernel,
        in_specs=[pl.BlockSpec(memory_space=pltpu.SMEM)] + [pl.BlockSpec(memory_space=pltpu.VMEM)] * 2,
        out_shape=[
            jax.ShapeDtypeStruct(shape, jnp.int32),
            jax.ShapeDtypeStruct(shape, jnp.int32),
            jax.ShapeDtypeStruct((1, 1), jnp.int32),
        ],
        cost_estimate=cost("row_layout"),
        name="row_layout",
    )(level_weight, segment, live)


def arrange_kernel(at_ref, mine_ref, other_ref, vq_ref, vq_other_ref, *refs):
    quarter = mine_ref.shape[2] // 4
    cols_s, vq_s = refs[-2:]
    use_mine, at_c, at_l = at_ref[0], at_ref[1], at_ref[2]
    n = 4 * quarter
    lane = lax.broadcasted_iota(jnp.int32, (n, 128), 1)
    for r in range(2):
        feat_ref, hot_ref, col_ref, row_ref = refs[4 * r : 4 * r + 4]
        info = jnp.where(use_mine == 1, mine_ref[r], other_ref[r])
        cols_s[...] = jnp.concatenate([info, jnp.zeros((124, n), full_type)], 0).T
        vq_s[...] = jnp.where(use_mine == 1, full(vq_ref[r]), full(vq_other_ref[r]))
        cols, vqs = [], []
        for k in range(4):
            start = jnp.bitwise_xor(at_c, k // 2) * 2 + jnp.bitwise_xor(at_l, k % 2)
            rows = pl.ds(pl.multiple_of(start * quarter, quarter), quarter)
            cols.append(cols_s[rows, :])
            vqs.append(vq_s[rows, :])
        cols = jnp.concatenate(cols, 0)
        code, place, live, weight = (cols[:, k : k + 1] for k in range(4))
        segment = jnp.floor(place * (1.0 / 16.0))
        base = segment * 16.0
        key = jnp.where(live > 0.0, place, 1048576.0)
        out = jnp.zeros((n, 128), full_type)
        for k, column in enumerate((place, base, key, code, weight)):
            out = jnp.where(lane == k, column, out)
        col_ref[...] = out
        row_ref[...] = out.T[0:8, :]
        spot = lax.broadcasted_iota(jnp.int32, (n, 16), 1)
        hit = (full(spot % 4) == segment) & (spot < 12)
        hot_ref[...] = low(jnp.where(hit, 1.0, 0.0))
        code_dim, padded = vq_ref.shape[2], feat_ref.shape[1]
        spread = lax.broadcasted_iota(jnp.int32, (code_dim, padded), 0) == lax.broadcasted_iota(
            jnp.int32, (code_dim, padded), 1
        )
        feats = dot_nn(low(jnp.concatenate(vqs, 0)), low(jnp.where(spread, 1.0, 0.0)))
        level = lax.broadcasted_iota(jnp.int32, (n, padded), 1) - code_dim
        feat_ref[...] = low(feats + jnp.where(full(level) == place - base, 1.0, 0.0))


def arrange(at, mine, other, vq, vq_other, padded):
    n, code_dim = vq.shape[1:]
    shapes = [((n, padded), low_type), ((n, 16), low_type), ((n, 128), full_type), ((8, n), full_type)] * 2
    return pl.pallas_call(
        arrange_kernel,
        in_specs=[pl.BlockSpec(memory_space=pltpu.SMEM)] + [pl.BlockSpec(memory_space=pltpu.VMEM)] * 4,
        out_shape=[jax.ShapeDtypeStruct(shape, dtype) for shape, dtype in shapes],
        scratch_shapes=[pltpu.VMEM((n, 128), full_type), pltpu.VMEM((n, code_dim), full_type)],
        compiler_params=pltpu.CompilerParams(vmem_limit_bytes=48 * 2**20),
        cost_estimate=cost("arrange"),
        name="arrange",
    )(at, mine, other, vq, vq_other)


def enter_tile(feat_ref, table_ref, hot_ref, w, in_ref, qkv_ref, stream_ref, parts_s):
    stream = dot_nn(feat_ref[...], table_ref[...])

    @pl.when(pl.program_id(0) == 0)
    def _():
        stream_ref[...] = stream[: stream_ref.shape[0]]

    normed, _ = centre(stream)
    hot = hot_ref[...]
    given = low(normed * (1.0 + dot_nn(hot, parts_s[1])) + dot_nn(hot, parts_s[0]))
    in_ref[...] = given
    qkv_ref[...] = dot_nn(given, w)


def enter_parts(mod_ref, parts_s):
    parts_s[0] = item_parts(mod_ref[0])
    parts_s[1] = item_parts(mod_ref[1])


def enter_kernel(feat_ref, table_ref, hot_ref, mod_ref, w_ref, in_ref, qkv_ref, stream_ref, parts_s):
    @pl.when(pl.program_id(0) == 0)
    def _():
        enter_parts(mod_ref, parts_s)

    enter_tile(feat_ref, table_ref, hot_ref, w_ref[...], in_ref, qkv_ref, stream_ref, parts_s)


def enter(feats, table, hot, mods, w):
    n, k = feats.shape
    width, columns = w.shape
    tile = n // 2
    return call(
        enter_kernel,
        (2,),
        [tiled(tile, k), whole((k, width)), tiled(tile, 16), whole(mods.shape), whole(w.shape)],
        [tiled(tile, width), tiled(tile, columns), fixed((tile // 2, width))],
        [((n, width), low_type), ((n, columns), full_type), ((tile // 2, width), full_type)],
        [pltpu.VMEM((2, 16, width), low_type)],
        "enter",
    )(feats, table, hot, mods, w)


def enter_first_kernel(
    at_ref, feat_ref, table_ref, hot_ref, mod_ref, a_ref, b_ref, c_ref, d_ref, in_ref, qkv_ref, stream_ref,
    w_ref, p_ref, parts_s
):
    @pl.when(pl.program_id(0) == 0)
    def _():
        enter_parts(mod_ref, parts_s)
        for k, ref in enumerate((a_ref, b_ref, c_ref, d_ref)):
            rows = ref.shape[2]
            start = pl.multiple_of(jnp.bitwise_xor(at_ref[0], k) * rows, rows)
            for j in range(2):
                for c in range(3):
                    w_ref[pl.ds(start, rows), (2 * c + j) * 128 : (2 * c + j + 1) * 128] = ref[j, c]
                p_ref[pl.ds(start, rows), j * 128 : (j + 1) * 128] = ref[j, 3]

    enter_tile(feat_ref, table_ref, hot_ref, w_ref[...], in_ref, qkv_ref, stream_ref, parts_s)


def enter_first(here, feats, table, hot, mods, pieces):
    n, k = feats.shape
    width = table.shape[1]
    columns = 768
    tile = n // 2
    shape = pieces[0].shape
    return call(
        enter_first_kernel,
        (n // tile,),
        [pl.BlockSpec(memory_space=pltpu.SMEM), tiled(tile, k), whole((k, width)), tiled(tile, 16), whole(mods.shape)]
        + [whole(shape)] * 4,
        [tiled(tile, width), tiled(tile, columns), fixed((tile // 2, width))]
        + [fixed((width, columns)), fixed((width, columns // 3))],
        [((n, width), low_type), ((n, columns), full_type), ((tile // 2, width), full_type)]
        + [((width, columns), low_type), ((width, columns // 3), low_type)],
        [pltpu.VMEM((2, 16, width), low_type)],
        "enter_first",
    )(here[None], feats, table, hot, mods, *pieces)


def onward_kernel(a_ref, b_ref, c_ref, x_ref, hot_ref, mod_ref, br_ref, y_ref, in_ref, parts_s, *, picks):
    @pl.when(pl.program_id(0) == 0)
    def _():
        for k, pick in enumerate(picks):
            parts_s[k] = item_parts(mod_ref[pick])

    branch = full(a_ref[...]) + full(b_ref[...]) + full(c_ref[...])
    br_ref[...] = branch
    hot = hot_ref[...]
    stream = x_ref[...] + dot_nn(hot, parts_s[0]) * branch
    y_ref[...] = stream
    normed, _ = centre(stream)
    in_ref[...] = low(normed * (1.0 + dot_nn(hot, parts_s[2])) + dot_nn(hot, parts_s[1]))


def onward(parts, stream, hot, mods, picks):
    n, width = parts[2].shape
    tile = n // 2
    return call(
        functools.partial(onward_kernel, picks=picks),
        (n // tile,),
        [tiled(tile, width)] * 4 + [tiled(tile, 16), whole(mods.shape)],
        [tiled(tile, width)] * 3,
        [((n, width), full_type), ((n, width), full_type), ((n, width), low_type)],
        [pltpu.VMEM((3, 16, width), low_type)],
        "onward",
    )(*parts, stream, hot, mods)


def back_kernel(*refs, gated, carried, picks):
    refs = list(refs)
    a_ref, b_ref, c_ref, x_ref, hot_ref, mod_ref = refs[:6]
    del refs[:6]
    res_ref = refs.pop(0) if carried else None
    br_ref = refs.pop(0) if gated else None
    feat_ref = None if gated else refs.pop(0)
    res_out = refs.pop(0) if gated else None
    d_ref = refs.pop(0) if gated else None
    items_ref = refs.pop(0)
    lead_ref = None if gated else refs.pop(0)
    parts_s = refs.pop(0)

    @pl.when(pl.program_id(0) == 0)
    def _():
        for k, pick in enumerate(picks):
            parts_s[k] = item_parts(mod_ref[pick])
        items_ref[...] = jnp.zeros_like(items_ref)
        if not gated:
            lead_ref[...] = jnp.zeros_like(lead_ref)

    hot = hot_ref[...]
    incoming = full(a_ref[...]) + full(b_ref[...]) + full(c_ref[...])
    normed, scale = centre(x_ref[...])
    items_ref[0] += item_sums(hot, incoming)
    items_ref[1] += item_sums(hot, incoming * normed)
    res = centre_back(normed, scale, incoming * (1.0 + dot_nn(hot, parts_s[0])))
    if carried:
        res = res + res_ref[...]
    if gated:
        res_out[...] = res
        items_ref[2] += item_sums(hot, res * br_ref[...])
        d_ref[...] = low(res * dot_nn(hot, parts_s[1]))
    else:
        upper, lower = split_parts(res, 2)
        feats = feat_ref[...]
        lead_ref[...] += dot_tn(feats, upper) + dot_tn(feats, lower)


def back(parts, stream, hot, mods, picks, carried, branch, feats):
    n, width = parts[2].shape
    tile = n // 2
    gated, has = branch is not None, carried is not None
    extra = ([carried] if has else []) + ([branch] if gated else [feats])
    specs = [tiled(tile, width)] * 4 + [tiled(tile, 16), whole(mods.shape)]
    specs += [tiled(tile, a.shape[1]) for a in extra]
    count = 3 if gated else 2
    out_specs, out_shape = [], []
    if gated:
        out_specs += [tiled(tile, width)] * 2
        out_shape += [((n, width), full_type), ((n, width), low_type)]
    out_specs.append(fixed((count, 8, width)))
    out_shape.append(((count, 8, width), full_type))
    if not gated:
        out_specs.append(fixed((feats.shape[1], width)))
        out_shape.append(((feats.shape[1], width), full_type))
    return call(
        functools.partial(back_kernel, gated=gated, carried=has, picks=picks),
        (n // tile,),
        specs,
        out_specs,
        out_shape,
        [pltpu.VMEM((2, 16, width), low_type)],
        "back",
    )(*parts, stream, hot, mods, *extra)


def either(a_ref, b_ref, c_ref, d_ref):
    top = jnp.concatenate([a_ref[...], b_ref[...]], 0)
    return jnp.where(pl.program_id(0) == 0, top, jnp.concatenate([c_ref[...], d_ref[...]], 0))


def put(value, top_ref, bottom_ref):
    @pl.when(pl.program_id(0) == 0)
    def _():
        top_ref[...] = value

    @pl.when(pl.program_id(0) == 1)
    def _():
        bottom_ref[...] = value


def fixed(shape):
    return pl.BlockSpec(shape, lambda i: (0,) * len(shape))


def column_half(shape, number):
    return pl.BlockSpec(
        shape[:3] + (shape[3] // 2,), lambda i: (0, 0, 0, number), pipeline_mode=pl.Buffered(1)
    )


def block_of(ref, h):
    return ref[:, h].reshape(-1, ref.shape[3])


def feed_kernel(a_ref, b_ref, c_ref, d_ref, one_ref, two_ref, row_ref, act_ref, slope_ref, top_ref, bottom_ref):
    given = either(a_ref, b_ref, c_ref, d_ref)
    row_ref[...] = given
    units = one_ref.shape[3]
    total = None
    for h in range(2):
        at = slice(h * units, (h + 1) * units)
        act, slope = gelu_parts(dot_nn(given, block_of(one_ref, h)))
        act = low(act)
        act_ref[:, at] = act
        slope_ref[:, at] = slope
        part = dot_nt(act, block_of(two_ref, h))
        total = part if total is None else total + part
    put(low(total), top_ref, bottom_ref)


def feed(pieces, both):
    tile, width = 2 * pieces[0].shape[0], pieces[0].shape[1]
    units = both.shape[3]
    return call(
        feed_kernel,
        (2,),
        [whole(pieces[0].shape)] * 4 + [column_half(both.shape, k) for k in range(2)],
        [tiled(tile, width), tiled(tile, units), tiled(tile, units), fixed((tile, width)), fixed((tile, width))],
        [((2 * tile, width), low_type), ((2 * tile, units), low_type), ((2 * tile, units), full_type)]
        + [((tile, width), low_type)] * 2,
        [],
        "feed",
    )(*pieces, both, both)


def feed_back_kernel(a_ref, b_ref, c_ref, d_ref, slope_ref, one_ref, two_ref, row_ref, dh_ref, top_ref, bottom_ref):
    given = either(a_ref, b_ref, c_ref, d_ref)
    row_ref[...] = given
    units = one_ref.shape[3]
    total = None
    for h in range(2):
        at = slice(h * units, (h + 1) * units)
        d_hidden = low(dot_nn(given, block_of(two_ref, h)) * slope_ref[:, at])
        dh_ref[:, at] = d_hidden
        part = dot_nt(d_hidden, block_of(one_ref, h))
        total = part if total is None else total + part
    put(low(total), top_ref, bottom_ref)


def feed_back(pieces, slope, both):
    tile, width = 2 * pieces[0].shape[0], pieces[0].shape[1]
    units = both.shape[3]
    return call(
        feed_back_kernel,
        (2,),
        [whole(pieces[0].shape)] * 4 + [tiled(tile, units)] + [column_half(both.shape, k) for k in range(2)],
        [tiled(tile, width), tiled(tile, units), fixed((tile, width)), fixed((tile, width))],
        [((2 * tile, width), low_type), ((2 * tile, units), low_type)] + [((tile, width), low_type)] * 2,
        [],
        "feed_back",
    )(*pieces, slope, both, both)


def head_kernel(a_ref, b_ref, c_ref, d_ref, w_ref, code_ref, column_ref, row_ref, logit_ref, stat_ref):
    given = either(a_ref, b_ref, c_ref, d_ref)
    row_ref[...] = given
    logits = jnp.concatenate([dot_nn(given, block_of(w_ref, h)) for h in range(2)], 1)
    logit_ref[...] = logits
    peak = jnp.max(logits, 1, keepdims=True)
    total = jnp.sum(jnp.exp(logits - peak), 1, keepdims=True)
    picked = jnp.sum(jnp.where(code_ref[:, 3:4] == column_ref[...], logits, 0.0), 1, keepdims=True)
    lane = lax.broadcasted_iota(jnp.int32, (logits.shape[0], 128), 1)
    turned = jnp.where(lane == 0, peak, jnp.where(lane == 1, total, picked)).T
    stat_ref[...] = turned[0:8, :]


def head(pieces, w, code, column):
    tile, width = 2 * pieces[0].shape[0], pieces[0].shape[1]
    units = 2 * w.shape[3]
    return call(
        head_kernel,
        (2,),
        [whole(pieces[0].shape)] * 4 + [whole(w.shape), tiled(tile, 128), whole((1, units))],
        [tiled(tile, width), tiled(tile, units), pl.BlockSpec((8, tile), lambda i: (0, i))],
        [((2 * tile, width), low_type), ((2 * tile, units), full_type), ((8, 2 * tile), full_type)],
        [],
        "head",
    )(*pieces, w, code, column)


def merge_kernel(sum_ref, here_ref, c_ref, l_ref, d_ref, weight_ref, out_ref, loss_ref):
    half = here_ref.shape[1] // 2

    def over_core(a):
        return jnp.concatenate([a[:, half:], a[:, :half]], 1)

    def over_line(a):
        return jnp.concatenate(
            [pltpu.roll(a[:, :half], half // 2, 1), pltpu.roll(a[:, half:], half // 2, 1)], 1
        )

    parts = (here_ref[...], over_core(c_ref[...]), over_line(l_ref[...]), over_core(over_line(d_ref[...])))
    peak = functools.reduce(jnp.maximum, [part[0:1] for part in parts])
    total = sum(part[1:2] * jnp.exp(part[0:1] - peak) for part in parts)
    picked = sum(part[2:3] for part in parts)
    log_total = peak + jnp.log(total)
    weight = weight_ref[4:5, :]
    spot = lax.broadcasted_iota(jnp.int32, (1, 2 * half), 1)
    loss = jnp.where(spot < half // 2, weight * (log_total - picked), 0.0)
    loss_ref[...] = jnp.broadcast_to(jnp.sum(loss, 1, keepdims=True), loss_ref.shape)
    blank = jnp.zeros((126, 2 * half), full_type)
    out_ref[...] = jnp.concatenate([log_total, weight / sum_ref[0], blank], 0).T


def merge(weight_sum, here, over_core, over_line, over_both, weights):
    n = here.shape[1]
    return pl.pallas_call(
        merge_kernel,
        in_specs=[pl.BlockSpec(memory_space=pltpu.SMEM)] + [pl.BlockSpec(memory_space=pltpu.VMEM)] * 5,
        out_shape=[jax.ShapeDtypeStruct((n, 128), full_type), jax.ShapeDtypeStruct((1, 128), full_type)],
        cost_estimate=cost("merge"),
        name="merge",
    )(weight_sum[None], here, over_core, over_line, over_both, weights)


def head_back_kernel(logit_ref, w_ref, code_ref, column_ref, line_ref, d_ref, top_ref, bottom_ref):
    hit = jnp.where(code_ref[:, 3:4] == column_ref[...], 1.0, 0.0)
    line = line_ref[...]
    d_logits = low(line[:, 1:2] * (jnp.exp(logit_ref[...] - line[:, 0:1]) - hit))
    d_ref[...] = d_logits
    units = w_ref.shape[3]
    total = dot_nt(d_logits[:, :units], block_of(w_ref, 0)) + dot_nt(d_logits[:, units:], block_of(w_ref, 1))
    put(low(total), top_ref, bottom_ref)


def head_back(logits, w, code, column, lines):
    n, units = logits.shape
    width = w.shape[0] * w.shape[2]
    tile = n // 2
    return call(
        head_back_kernel,
        (2,),
        [tiled(tile, units), whole(w.shape), tiled(tile, 128), whole((1, units)), tiled(tile, 128)],
        [tiled(tile, units), fixed((tile, width)), fixed((tile, width))],
        [((n, units), low_type)] + [((tile, width), low_type)] * 2,
        [],
        "head_back",
    )(logits, w, code, column, lines)


def old_stats_kernel(qkv_ref, proj_ref, one_ref, two_ref, head_ref, ada_ref, tab_ref, scale_ref, out_ref):
    def total(values):
        return jnp.sum(jnp.sum(values * values, 1, keepdims=True), 0, keepdims=True)

    spot = lax.broadcasted_iota(jnp.int32, (1, 128), 1)
    line = jnp.zeros((1, 128), full_type)
    sums = [sum(total(qkv_ref[c]) for c in range(3))]
    sums += [total(ref[...]) for ref in (proj_ref, one_ref, two_ref, head_ref, scale_ref)]
    for k, value in enumerate(sums):
        line = jnp.where(spot == 16 + k, value, line)
    out_ref[0:1, :] = line
    line = jnp.where(spot == 8, total(ada_ref[...]), 0.0)
    out_ref[1:2, :] = jnp.where(spot == 9, total(tab_ref[...]), line)


def old_stats(*olds):
    return pl.pallas_call(
        old_stats_kernel,
        out_shape=jax.ShapeDtypeStruct((2, 128), full_type),
        compiler_params=pltpu.CompilerParams(vmem_limit_bytes=48 * 2**20),
        cost_estimate=cost("old_stats"),
        name="old_stats",
    )(*olds)


def put_rows(out_ref, start, value):
    groups, _, rows, _ = out_ref.shape
    for g in range(groups):
        out_ref[g, 0, :, start : start + value.shape[1]] = value[g * rows : (g + 1) * rows]


def head_grad_kernel(a_ref, b_ref, c_ref, d_ref, out_ref):
    put_rows(out_ref, 0, low(dot_tn(a_ref[...], c_ref[...]) + dot_tn(b_ref[...], d_ref[...])))


def head_grad_of(inputs, wanted, groups):
    n, width = inputs[0].shape
    columns = wanted[0].shape[1] // 2
    block = pl.BlockSpec((n, columns), lambda i: (0, i))
    return call(
        head_grad_kernel,
        (2,),
        [whole((n, width))] * 2 + [block] * 2,
        [pl.BlockSpec((groups, 1, width // groups, columns), lambda i: (0, i, 0, 0))],
        [((groups, 2, width // groups, columns), low_type)],
        [],
        "head_grad",
    )(*inputs, *wanted)[0]


def feed_grad_kernel(a_ref, b_ref, c_ref, d_ref, e_ref, f_ref, g_ref, h_ref, out_ref):
    @pl.when(pl.program_id(0) < 2)
    def _():
        put_rows(out_ref, 0, low(dot_tn(a_ref[...], c_ref[...]) + dot_tn(b_ref[...], d_ref[...])))

    @pl.when(pl.program_id(0) >= 2)
    def _():
        put_rows(out_ref, 0, low(dot_tn(e_ref[...], g_ref[...]) + dot_tn(f_ref[...], h_ref[...])))


def feed_grad_of(inputs, d_hidden, d_branch, acts, groups):
    n, width = inputs[0].shape
    columns = acts[0].shape[1] // 2
    early = pl.BlockSpec((n, columns), lambda i: (0, jnp.minimum(i, 1)))
    late = pl.BlockSpec((n, columns), lambda i: (0, jnp.maximum(i - 2, 0)))
    return call(
        feed_grad_kernel,
        (4,),
        [whole((n, width))] * 2 + [early] * 2 + [whole((n, width))] * 2 + [late] * 2,
        [pl.BlockSpec((groups, 1, width // groups, columns), lambda i: (0, i % 2, 0, i // 2))],
        [((groups, 2, width // groups, 2 * columns), low_type)],
        [],
        "feed_grad",
    )(*inputs, *d_hidden, *d_branch, *acts)[0]


def first_grad_kernel(a_ref, b_ref, c_ref, d_ref, e_ref, f_ref, g_ref, h_ref, out_ref):
    group = c_ref.shape[1] // 3
    start = pl.program_id(0) * 128

    def columns(ref):
        return jnp.concatenate(
            [ref[:, pl.ds(pl.multiple_of(start + c * group, 128), 128)] for c in range(3)], 1
        )

    put_rows(out_ref, 0, low(dot_tn(a_ref[...], columns(c_ref)) + dot_tn(b_ref[...], columns(d_ref))))
    put_rows(out_ref, 384, low(dot_tn(e_ref[...], g_ref[...]) + dot_tn(f_ref[...], h_ref[...])))


def first_grad_of(inputs, d_qkv, d_branch, mixed, groups):
    n, width = inputs[0].shape
    return call(
        first_grad_kernel,
        (2,),
        [whole((n, width))] * 2 + [whole(d_qkv[0].shape)] * 2 + [whole((n, width))] * 2
        + [pl.BlockSpec((n, 128), lambda i: (0, i))] * 2,
        [pl.BlockSpec((groups, 1, width // groups, 512), lambda i: (0, i, 0, 0))],
        [((groups, 2, width // groups, 512), low_type)],
        [],
        "first_grad",
    )(*inputs, *d_qkv, *d_branch, *mixed)[0]


def row_stats_kernel(qkv_ref, proj_ref, one_ref, two_ref, head_ref, out_ref):
    n = out_ref.shape[1]
    lane = lax.broadcasted_iota(jnp.int32, (n, 128), 1)
    out = jnp.zeros((n, 128), full_type)
    qkv = sum(jnp.sum(qkv_ref[c] * qkv_ref[c], 1, keepdims=True) for c in range(3))
    sums = [qkv + 3 * qkv_ref.shape[2] * eps_one]
    for ref in (proj_ref, one_ref, two_ref, head_ref):
        values = ref[...]
        sums.append(jnp.sum(values * values, 1, keepdims=True) + ref.shape[1] * eps_one)
    for k, column in enumerate(sums):
        out = jnp.where(lane == k, column, out)
    out_ref[...] = out.T[0:8, :]


def row_stats(*gradients):
    n = gradients[1].shape[0]
    return pl.pallas_call(
        row_stats_kernel,
        out_shape=jax.ShapeDtypeStruct((8, n), full_type),
        compiler_params=pltpu.CompilerParams(vmem_limit_bytes=48 * 2**20),
        cost_estimate=cost("row_stats"),
        name="row_stats",
    )(*gradients)


def column_stats_kernel(
    at_ref, row_ref, old_ref, tail_ref, tables_ref, scale_ref, qkv_ref, proj_ref, one_ref, two_ref, head_ref, ada_ref, out_ref, new_ref, *, decay
):
    n = proj_ref.shape[0]
    rows = row_ref[...]
    padded = jnp.concatenate([rows, jnp.zeros((128 - rows.shape[0], n), full_type)], 0).T
    at = 0
    pieces = [(qkv_ref[c], 0) for c in range(3)]
    pieces += [(ref[...], k + 1) for k, ref in enumerate((proj_ref, one_ref, two_ref, head_ref))]
    for values, k in pieces:
        square = values * values
        columns = square.shape[1]
        out_ref[0:1, at : at + columns] = jnp.sum(square, 0, keepdims=True) + n * eps_one
        out_ref[1:2, at : at + columns] = jnp.sum(
            square * (1.0 / padded[:, k : k + 1]), 0, keepdims=True
        )
        at += columns
    columns = ada_ref.shape[1]
    step = 1024
    total = jnp.zeros((n, 1), full_type)
    for start in range(0, columns, step):
        values = ada_ref[:, start : start + step]
        total = total + jnp.sum(values * values, 1, keepdims=True)
    old = jnp.concatenate([old_ref[...], jnp.zeros((127, n), full_type)], 0).T[:, 0:1]
    row = decay * old + (1.0 - decay) * (total / columns + eps_one)
    lane = lax.broadcasted_iota(jnp.int32, (n, 128), 1)
    new_ref[...] = jnp.where(lane == 0, row, 0.0).T[0:8, :]
    for start in range(0, columns, step):
        values = ada_ref[:, start : start + step]
        square = values * values
        out_ref[0:1, at : at + step] = jnp.sum(square, 0, keepdims=True) + n * eps_one
        out_ref[1:2, at : at + step] = jnp.sum(square * (1.0 / row), 0, keepdims=True)
        at += step
    spots = lax.broadcasted_iota(jnp.int32, (1, 128), 1)
    line = tail_ref[...]
    for k in range(5):
        line = jnp.where(spots == k, jnp.sum(rows[k : k + 1, :], 1, keepdims=True), line)
    line = jnp.where(spots == 5, jnp.sum(row, 0, keepdims=True), line)
    line = jnp.where(spots == 10, tables_ref[...], line)
    scales = scale_ref[...]
    for k in range(2):
        value = jnp.sum(jnp.where((spots < 64) == (k == 0), scales, 0.0), 1, keepdims=True)
        line = jnp.where(spots == 11 + k + 2 * at_ref[0], value, line)
    out_ref[0:1, at : at + 128] = line
    out_ref[1:2, at : at + 128] = jnp.zeros_like(line)


def column_stats(at_c, row_new, old, tail, tables_sum, scales, gradients, decay):
    n = gradients[1].shape[0]
    columns = sum(g.size // n for g in gradients)
    return pl.pallas_call(
        functools.partial(column_stats_kernel, decay=decay),
        out_shape=[
            jax.ShapeDtypeStruct((2, columns + 128), full_type),
            jax.ShapeDtypeStruct((8, n), full_type),
        ],
        in_specs=[pl.BlockSpec(memory_space=pltpu.SMEM)]
        + [pl.BlockSpec(memory_space=pltpu.VMEM)] * (5 + len(gradients)),
        compiler_params=pltpu.CompilerParams(vmem_limit_bytes=48 * 2**20),
        cost_estimate=cost("column_stats"),
        name="column_stats",
    )(at_c[None], row_new, old, tail, tables_sum, scales, *gradients)


def spot_of(line, k):
    spots = lax.broadcasted_iota(jnp.int32, line.shape, 1)
    return jnp.sum(jnp.where(spots == k, line, 0.0), 1, keepdims=True)


def finish_kernel(
    flat_ref, old_ref, scale_ref, col_ref, part_ref, own_ref, second_ref, step_ref, *, decay, width, starts
):
    columns = old_ref.shape[1]
    line = flat_ref[0:1, columns:]
    new = decay * old_ref[...] + (1.0 - decay) * (flat_ref[0:1, :columns] / width)
    col_ref[...] = new
    ratio = flat_ref[1:2, :columns] / new
    spots = lax.broadcasted_iota(jnp.int32, (1, 128), 1)
    scales = (spots >= 11) & (spots < 15)
    gradient = jnp.where(scales, line, 0.0)
    second = decay * scale_ref[...] + (1.0 - decay) * (gradient * gradient + eps_one)
    step = gradient * lax.rsqrt(second)
    second_ref[...] = second
    step_ref[...] = step
    out = jnp.where(spots == 7, jnp.sum(step * step, 1, keepdims=True), 0.0)
    for k in range(6):
        value = jnp.sum(ratio[:, starts[k] : starts[k + 1]], 1, keepdims=True) * (spot_of(line, k) / width)
        if k == 5:
            own_ref[...] = jnp.where(spots == 5, value, 0.0)
        else:
            out = jnp.where(spots == k, value, out)
    part_ref[...] = out


def finish(flat, col_old, scale_line, decay, width, starts):
    return pl.pallas_call(
        functools.partial(finish_kernel, decay=decay, width=width, starts=starts),
        out_shape=[jax.ShapeDtypeStruct(col_old.shape, full_type)]
        + [jax.ShapeDtypeStruct((1, 128), full_type)] * 4,
        cost_estimate=cost("finish"),
        name="finish",
    )(flat, col_old, scale_line)


def renew_kernel(
    line_ref, part_ref, own_ref, early_ref, rows_ref, col_ref, ada_col_ref,
    qkv_g, proj_g, one_g, two_g, head_g, ada_g, step_ref, scale_step_ref,
    qkv_ref, proj_ref, one_ref, two_ref, head_ref, ada_ref, tab_ref, scale_ref,
    qkv_out, proj_out, one_out, two_out, head_out, ada_out, tab_out, scale_out, proj_turned, two_turned,
    *, width, entries, starts
):
    n = one_g.shape[0]
    line, part = line_ref[...], part_ref[...]

    def factor(k):
        step = spot_of(own_ref[...], 5) if k == 5 else spot_of(line, 10) if k == 6 else spot_of(part, k)
        weight = spot_of(early_ref[...], 21) if k == 7 else spot_of(line, {5: 8, 6: 9}.get(k, 16 + k))
        ratio = jnp.sqrt(step / entries[k]) / clip_rms
        spread = jnp.maximum(eps_two, jnp.sqrt(weight / entries[k]))
        return rate_step * spread / jnp.maximum(1.0, ratio)

    def row(k):
        rows = jnp.concatenate([rows_ref[k : k + 1, :], jnp.zeros((127, n), full_type)], 0)
        return rows.T[:, 0:1]

    def change(k, gradient, columns):
        mean = spot_of(line, k) / width
        return factor(k) * (gradient * lax.rsqrt(row(k) * columns / mean))

    ada_out[...] = ada_ref[...] - change(5, ada_g[...], ada_col_ref[...])
    at = pl.program_id(0)

    @pl.when(at == 0)
    def _():
        size = qkv_g.shape[2]
        for c in range(3):
            qkv_out[c] = qkv_ref[c] - change(0, qkv_g[c], col_ref[:, c * size : (c + 1) * size])

    @pl.when(at == 1)
    def _():
        gradient = proj_g[...]
        proj_turned[...] = gradient.T
        proj_out[...] = proj_ref[...] - change(1, gradient, col_ref[:, starts[1] : starts[2]]).T
        scale_out[...] = scale_ref[...] - factor(7) * scale_step_ref[...]

    @pl.when(at == 2)
    def _():
        one_out[...] = one_ref[...] - change(2, one_g[...], col_ref[:, starts[2] : starts[3]])

    @pl.when(at == 3)
    def _():
        gradient = two_g[...]
        two_turned[...] = gradient.T
        two_out[...] = two_ref[...] - change(3, gradient, col_ref[:, starts[3] : starts[4]]).T

    @pl.when(at == 4)
    def _():
        head_out[...] = head_ref[...] - change(4, head_g[...], col_ref[:, starts[4] : starts[5]])

    @pl.when(at == 5)
    def _():
        tab_out[...] = tab_ref[...] - factor(6) * step_ref[...]


def renew(lines, rows, columns, grads, steps, olds, width, entries, starts):
    n, tile = grads[2].shape[0], 1024
    ada = pl.BlockSpec((n, tile), lambda i: (0, i))
    first = starts[5] // tile

    def wholes(arrays):
        return [whole(a.shape) for a in arrays]

    outs = [a.shape for a in olds] + [olds[1].shape, olds[3].shape]
    out_specs = [ada if k == 5 else fixed(shape) for k, shape in enumerate(outs)]
    return call(
        functools.partial(renew_kernel, width=width, entries=entries, starts=starts),
        (olds[5].shape[1] // tile,),
        wholes(lines)
        + [whole(rows.shape), whole(columns.shape), pl.BlockSpec((1, tile), lambda i: (0, first + i))]
        + wholes(grads[:5])
        + [ada]
        + wholes(steps)
        + wholes(olds[:5])
        + [ada]
        + wholes(olds[6:]),
        out_specs,
        [(shape, full_type) for shape in outs],
        [],
        "renew",
    )(*lines, rows, columns, columns, *grads, *steps, *olds)


def head_lanes(shape):
    return lax.broadcasted_iota(jnp.int32, shape, len(shape) - 1) < 64


def per_head(values, first):
    left = jnp.sum(jnp.where(first, values, 0.0), -1, keepdims=True)
    right = jnp.sum(jnp.where(first, 0.0, values), -1, keepdims=True)
    return jnp.where(first, left, right)


def attend_kernel(
    q_ref, k_ref, v_ref, gain_ref, col_ref, row_ref, proj_ref,
    mix_ref, lse_ref, top_ref, bottom_ref, q_s, k_s, v_s, bias_s, sum_s
):
    length = q_ref.shape[0]
    tile = length // 2
    first = head_lanes((length, 128))
    query = q_ref[...]
    key = k_ref[...]
    q_s[...] = low(
        query * (lax.rsqrt(per_head(query * query, first) / 64.0 + eps_norm) * gain_ref[...])
    )
    k_s[...] = low(key * (lax.rsqrt(per_head(key * key, first) / 64.0 + eps_norm) * 0.125))
    v_s[...] = low(v_ref[...])
    first_t = head_lanes((tile, 128))

    @pl.when(pl.program_id(0) == 0)
    def _():
        ck = row_ref[2:3, :]
        for i in range(2):
            rows = slice(i * tile, (i + 1) * tile)
            shape = (tile, length)
            here = lax.broadcasted_iota(jnp.int32, shape, 1) - lax.broadcasted_iota(jnp.int32, shape, 0)
            keep = ((ck <= col_ref[rows, 0:1]) & (ck >= col_ref[rows, 1:2])) | (here == i * tile)
            bias_s[rows, :] = jnp.where(keep, 0.0, -1e30)
        sum_s[...] = jnp.zeros_like(sum_s)

    for i, out_ref in enumerate((top_ref, bottom_ref)):
        rows = slice(i * tile, (i + 1) * tile)
        query_t = q_s[rows, :]
        mixed, logs = [], []
        for head in range(2):
            chosen = first_t if head == 0 else ~first_t
            scores = dot_nt(jnp.where(chosen, query_t, jnp.zeros_like(query_t)), k_s[...]) + bias_s[rows, :]
            peak = jnp.max(scores, -1, keepdims=True)
            exponent = jnp.exp(scores - peak)
            total = jnp.sum(exponent, -1, keepdims=True)
            mixed.append(dot_nn(low(exponent * (1.0 / total)), v_s[...]))
            logs.append(peak + jnp.log(total))
        mixed = low(jnp.where(first_t, mixed[0], mixed[1]))
        mix_ref[rows, :] = mixed
        turned = jnp.where(first_t, logs[0], logs[1]).T
        lse_ref[0, 0:1, rows] = turned[0:1, :]
        lse_ref[0, 1:2, rows] = turned[64:65, :]
        part = sum_s[rows, :] + dot_nt(mixed, proj_ref[...])
        sum_s[rows, :] = part

        @pl.when(pl.program_id(0) == pl.num_programs(0) - 1)
        def _():
            out_ref[...] = low(part)


def attend(qkv, gain, cols, rows, proj):
    length = qkv.shape[0]
    pairs = qkv.shape[1] // 384
    width = proj.shape[0]
    block = pl.BlockSpec((length, 128), lambda p: (0, p))
    return call(
        attend_kernel,
        (pairs,),
        [
            block,
            pl.BlockSpec((length, 128), lambda p: (0, pairs + p)),
            pl.BlockSpec((length, 128), lambda p: (0, 2 * pairs + p)),
            pl.BlockSpec((1, 128), lambda p: (0, p)),
            whole((length, 128)),
            whole((8, length)),
            pl.BlockSpec((width, 128), lambda p: (0, p)),
        ],
        [block, pl.BlockSpec((1, 2, length), lambda p: (p, 0, 0))] + [fixed((length // 2, width))] * 2,
        [((length, 128 * pairs), low_type), ((pairs, 2, length), full_type)]
        + [((length // 2, width), low_type)] * 2,
        [pltpu.VMEM((length, 128), low_type)] * 3
        + [pltpu.VMEM((length, length), full_type), pltpu.VMEM((length, width), full_type)],
        "attend",
    )(qkv, qkv, qkv, gain, cols, rows, proj)


def attend_back_kernel(
    q_ref, k_ref, v_ref, gain_ref, col_ref, line_ref, lse_ref, pa_ref, pb_ref, pc_ref, pd_ref,
    proj_ref, wq_ref, wk_ref, wv_ref, row_ref, d_ref, ds_ref, top_ref, bottom_ref,
    q_s, k_s, v_s, dm_ref, dqa, dka, dva, sum_s, *, tile
):
    length = q_ref.shape[0]
    first = head_lanes((length, 128))
    query = q_ref[...]
    key = k_ref[...]
    gain = gain_ref[...]
    q_n = lax.rsqrt(per_head(query * query, first) / 64.0 + eps_norm)
    k_n = lax.rsqrt(per_head(key * key, first) / 64.0 + eps_norm)
    q_s[...] = low(query * (q_n * gain))
    k_s[...] = low(key * (k_n * 0.125))
    v_s[...] = low(v_ref[...])
    quarter = length // 4
    for k, ref in enumerate((pa_ref, pb_ref, pc_ref, pd_ref)):
        rows = slice(k * quarter, (k + 1) * quarter)
        dm_ref[rows, :] = low(dot_nn(ref[...], proj_ref[...]))

    @pl.when(pl.program_id(0) == 0)
    def _():
        sum_s[...] = jnp.zeros_like(sum_s)
        for k, ref in enumerate((pa_ref, pb_ref, pc_ref, pd_ref)):
            row_ref[k * quarter : (k + 1) * quarter, :] = ref[...]

    dka[...] = jnp.zeros_like(dka)
    dva[...] = jnp.zeros_like(dva)
    first_t = head_lanes((tile, 128))
    ck = col_ref[:, 2:3]

    def step(i, carry):
        rows = pl.ds(pl.multiple_of(i * tile, tile), tile)
        query_t = q_s[rows, :]
        dmix_t = dm_ref[rows, :]
        shape = (length, tile)
        here = lax.broadcasted_iota(jnp.int32, shape, 0) - lax.broadcasted_iota(jnp.int32, shape, 1)
        keep = ((ck <= line_ref[0:1, rows]) & (ck >= line_ref[1:2, rows])) | (here == i * tile)
        d_query = []
        for head in range(2):
            chosen = first_t if head == 0 else ~first_t
            zero = jnp.zeros_like(query_t)
            query_h = jnp.where(chosen, query_t, zero)
            dmix_h = jnp.where(chosen, dmix_t, zero)
            scores = dot_nt(k_s[...], query_h)
            attention = jnp.where(keep, jnp.exp(scores - lse_ref[0, head : head + 1, rows]), 0.0)
            dva[...] += dot_nn(low(attention), dmix_h)
            d_att = dot_nt(v_s[...], dmix_h)
            inner = jnp.sum(attention * d_att, 0, keepdims=True)
            d_scores = low(attention * (d_att - inner))
            dka[...] += dot_nn(d_scores, query_h)
            d_query.append(dot_tn(d_scores, k_s[...]))
        dqa[rows, :] = jnp.where(first_t, d_query[0], d_query[1])
        return carry

    lax.fori_loop(0, length // tile, step, 0)
    q_hat = query * q_n
    k_hat = key * k_n
    d_query = dqa[...]
    along = d_query * q_hat
    ds_ref[0] = jnp.sum(along, 0, keepdims=True) * gain
    group = d_ref.shape[1] // 3
    start = pl.program_id(0) * 128

    def columns(c):
        return pl.ds(pl.multiple_of(start + c * group, 128), 128)

    out_q = low(gain * (d_query - q_hat * (per_head(along, first) / 64.0)) * q_n)
    d_ref[:, columns(0)] = out_q
    d_key = dka[...]
    out_k = low(
        0.125 * (d_key - k_hat * (per_head(d_key * k_hat, first) / 64.0)) * k_n
    )
    out_v = low(dva[...])
    d_ref[:, columns(1)] = out_k
    d_ref[:, columns(2)] = out_v
    half = length // 2
    for rows, out_ref in ((slice(0, half), top_ref), (slice(half, length), bottom_ref)):
        part = sum_s[rows, :] + dot_nt(out_q[rows], wq_ref[...])
        part = part + dot_nt(out_k[rows], wk_ref[...]) + dot_nt(out_v[rows], wv_ref[...])
        sum_s[rows, :] = part

        @pl.when(pl.program_id(0) == pl.num_programs(0) - 1)
        def _():
            out_ref[...] = low(part)


def attend_back(qkv, gain, cols, rows, lse, pieces, proj, w):
    length = qkv.shape[0]
    pairs = qkv.shape[1] // 384
    width = proj.shape[0]

    def part(rows, number):
        return pl.BlockSpec((rows, 128), lambda p: (0, number * pairs + p))

    return call(
        functools.partial(attend_back_kernel, tile=256),
        (pairs,),
        [
            part(length, 0),
            part(length, 1),
            part(length, 2),
            pl.BlockSpec((1, 128), lambda p: (0, p)),
            whole((length, 128)),
            whole((8, length)),
            pl.BlockSpec((1, 2, length), lambda p: (p, 0, 0)),
        ]
        + [whole(pieces[0].shape)] * 4
        + [part(width, 0), part(width, 0), part(width, 1), part(width, 2)],
        [
            fixed((length, width)),
            fixed((length, 384 * pairs)),
            pl.BlockSpec((1, 1, 128), lambda p: (p, 0, 0)),
            fixed((length // 2, width)),
            fixed((length // 2, width)),
        ],
        [
            ((length, width), low_type),
            ((length, 384 * pairs), low_type),
            ((pairs, 1, 128), full_type),
            ((length // 2, width), low_type),
            ((length // 2, width), low_type),
        ],
        [pltpu.VMEM((length, 128), low_type)] * 4
        + [pltpu.VMEM((length, 128), full_type)] * 3
        + [pltpu.VMEM((length, width), full_type)],
        "attend_back",
    )(qkv, qkv, qkv, gain, cols, rows, lse, *pieces, proj, w, w, w)


def body(
    vq_in, codes, segment, live, labels, level_weight, qkv_w, proj_w, fc1_w, fc2_w, head_w, ada_w,
    tables, head_scale, d_stats, qkv_stat, proj_stat, fc1_stat, fc2_stat, head_stat, ada_stat,
    tables_v, scale_v,
):
    g_count = lax.axis_size("g")
    dp_count = g_count * lax.axis_size("c")
    mp_count = lax.axis_size("h") * lax.axis_size("l")
    at_c, at_h, at_l = lax.axis_index("c"), lax.axis_index("h"), lax.axis_index("l")
    row_count, seq_len, code_dim = vq_in.shape
    item_count = labels.shape[1]
    level_count = level_weight.shape[0]
    slice_width = tables.shape[1]
    width = slice_width * dp_count
    half, quarter = seq_len // 2, seq_len // 4
    table_rows = tables.shape[0]
    lead = code_dim + level_count
    per_row = row_count * item_count
    note_rows = -(-(2 * per_row + 3) // slice_width)
    lead_pad = -(-(lead + note_rows) // 16) * 16

    def halves(a):
        n = a.shape[-1] // 2
        lower, upper = low(a[..., :n]), low(a[..., n:])
        return jnp.where(at_c == 0, lower, upper), jnp.where(at_c == 0, upper, lower)

    first_mine, first_other = halves(jnp.concatenate([qkv_w, proj_w.T[None]], 0))
    first_near = ordered(at_c, first_mine, over_c(first_other), 1)

    place, weight, weight_here = row_layout(level_weight, segment, live)
    weight_here = weight_here[0, 0]

    per_row = row_count * item_count
    note_rows = -(-(2 * per_row + 3) // slice_width)
    lead_pad = -(-(lead + note_rows) // 16) * 16
    tables_low = low(tables)
    label_flat = labels.reshape(-1)
    digits = jnp.stack([weight_here // 4096, (weight_here // 64) % 64, weight_here % 64])
    note = jnp.concatenate([label_flat // 32, label_flat % 32, digits])
    note = jnp.pad(low(note), (0, (lead_pad - lead) * slice_width - note.shape[0]))
    note = note.reshape(lead_pad - lead, slice_width)
    packed = tie(jnp.concatenate([tables_low[:lead], note], 0), first_near)
    gathered, first_far = lax.optimization_barrier(
        (lax.all_gather(packed, DP, axis=0), over_h(first_near))
    )
    lead_table = jnp.transpose(gathered, (1, 0, 2)).reshape(lead_pad, width)
    notes = gathered[:, lead : lead + note_rows].reshape(dp_count, -1).astype(jnp.int32)
    labels_all = (notes[:, :per_row] * 32 + notes[:, per_row : 2 * per_row]).reshape(-1)
    weight_sum = full(
        jnp.sum(
            notes[:, 2 * per_row] * 4096
            + notes[:, 2 * per_row + 1] * 64
            + notes[:, 2 * per_row + 2]
        )
    )

    class_hot = (
        labels_all[:, None] + lead == jnp.arange(table_rows, dtype=jnp.int32)[None, :]
    )
    class_vec = dot_nn(low(class_hot), tables_low)
    sigma = jax.nn.sigmoid(class_vec)
    activated = low(class_vec * sigma)
    act_pairs = activated.reshape(g_count, 2, per_row, slice_width)
    act_mine = jnp.where(at_h == 0, act_pairs[:, 0], act_pairs[:, 1]).reshape(-1, slice_width)
    ada_low = low(ada_w)
    mod_part = dot_nn(act_mine, ada_low)
    mod_half = ada_w.shape[1] // 2
    left, right = mod_part[:, :mod_half], mod_part[:, mod_half:]
    mod_send = jnp.where(at_c == 0, right, left)
    mod_sum = jnp.where(at_c == 0, left, right) + over_c(mod_send)
    mod_first = mod_sum
    mod_sum = scatter_g(mod_sum)
    mod_items = ordered(at_c, mod_sum, over_c(mod_sum), 1).reshape(row_count, item_count, 8, width)
    mod_rows = jnp.transpose(mod_items, (0, 2, 1, 3))

    fc1_wide, fc2_wide = tie((fc1_w, fc2_w), mod_send)

    def near_rows(w):
        kept, other = halves(w)
        return ordered(at_c, kept, over_c(other), 0)

    def gathered_weight(a):
        wide = lax.all_gather(a.reshape(-1, a.shape[2]), "g", axis=0, tiled=True)
        return wide.reshape((g_count,) + a.shape)

    feed_near = jnp.concatenate([near_rows(fc1_wide), near_rows(fc2_wide.T)], 1)
    qkv_piece = ordered(at_h, first_near[None], first_far[None], 0)

    def window(*values):
        return lax.optimization_barrier(values)

    def far_part(r):
        return low(full(top[r][quarter:]) + full(moved[r][quarter:]))

    def turn(norm, kernel, filler=lambda: None, beside=None, keep=lambda done: None):
        moved[1] = over_c(bottom[1])
        first, moved[1] = window(norm(0, (top[0], moved[0], across[0])), moved[1])
        across[1] = over_l(far_part(1))
        pieces = [[first, over_l(first), over_c(first), None], None]
        done, across[1], pieces[0][2] = window(filler(), across[1], pieces[0][2])
        keep(done)
        second, pieces[0][1] = window(norm(1, (top[1], moved[1], across[1])), pieces[0][1])
        pieces[1] = [second, over_l(second), over_c(second), None]
        pieces[0][3] = over_c(pieces[0][1])
        kernel_out, pieces[1], beside = window(kernel(0, pieces[0]), pieces[1][:3], beside)
        return pieces, kernel_out, done, beside

    def launch():
        moved[0] = over_c(bottom[0])
        sent = far_part(0)
        across[0] = over_l(sent)
        return sent

    head_gain = tie(head_scale, gathered)
    gain_own = jnp.where(at_c == 0, head_gain[:2], head_gain[2:])
    gains = jnp.exp(ordered(at_h, gain_own, over_h(gain_own), 0)) / 8.0
    gain_row = jnp.repeat(gains, 64)[None, :]

    info = full(jnp.stack([codes, place, live, weight], 1))
    info_other, vq_other = over_c(info), over_c(vq_in)
    at = jnp.stack([full(at_c == at_h).astype(jnp.int32), at_c, at_l])
    arranged, olds, qkv_pieces, feed_far = window(
        arrange(at, tie(info, mod_first), info_other, vq_in, vq_other, lead_pad),
        old_stats(*tie((qkv_w, proj_w, fc1_w, fc2_w, head_w, ada_w, tables, head_scale[None]), mod_first)),
        [qkv_piece] + [over_g(qkv_piece, k) for k in range(1, 4)] if g_count == 4 else [],
        over_h(feed_near),
    )
    feats, hot, cols, rows = (arranged[k::4] for k in range(4))
    head_near = near_rows(tie(head_w, olds))
    feats_first = tie(feats[0], gain_row)
    inputs_one, qkv_rows, mixed_rows, lse_rows, top, bottom, stream_zero = ([None] * 2 for _ in range(7))
    if g_count == 4:
        inputs_one[0], qkv_rows[0], stream_zero[0], qkv_full, proj_full = enter_first(
            lax.axis_index("g"), feats_first, lead_table, hot[0], mod_rows[0], qkv_pieces
        )
    else:
        wide_piece = lax.all_gather(qkv_piece, "g", axis=0)
        wide_piece = jnp.transpose(wide_piece, (0, 3, 2, 1, 4)).reshape(width, -1)
        qkv_full, proj_full = wide_piece[:, :768], wide_piece[:, 768:]
        inputs_one[0], qkv_rows[0], stream_zero[0] = enter(feats_first, lead_table, hot[0], mod_rows[0], qkv_full)
    feed_full = gathered_weight(ordered(at_h, feed_near[None], feed_far[None], 0))

    moved, across = [None] * 2, [None] * 2

    def attention(r, given):
        mixed_rows[r], lse_rows[r], top[r], bottom[r] = attend(
            given, gain_row, cols[r], rows[r], proj_full
        )
        return top[r], bottom[r]

    (top[0], bottom[0]), head_far = window(attention(0, qkv_rows[0]), over_h(head_near))
    held = [gathered_weight(ordered(at_h, head_near[None], head_far[None], 0))]
    moved[0] = over_c(bottom[0])
    (inputs_one[1], qkv_rows[1], stream_zero[1]), moved[0] = window(
        enter(tie(feats[1], bottom[0]), lead_table, hot[1], mod_rows[1], qkv_full), moved[0]
    )
    sent = far_part(0)
    across[0] = over_l(sent)
    (top[1], bottom[1]), across[0] = window(attention(1, tie(qkv_rows[1], sent)), across[0])

    branch_one, stream_one, acts, slopes, inputs_two = ([None] * 2 for _ in range(5))

    def norm_two(r, parts):
        branch_one[r], stream_one[r], given = onward(parts, stream_zero[r], hot[r], mod_rows[r], (2, 3, 4))
        return given

    def forward(r, pieces):
        inputs_two[r], acts[r], slopes[r], top[r], bottom[r] = feed(pieces, feed_full)
        return top[r], bottom[r]

    pieces_two, (top[0], bottom[0]), _, _ = turn(norm_two, forward)
    pieces_two[1].append(over_c(pieces_two[1][1]))
    sent = launch()
    (top[1], bottom[1]), across[0] = window(
        forward(1, [tie(pieces_two[1][0], sent)] + pieces_two[1][1:]), across[0]
    )

    block_codes = head_w.shape[1]
    half_codes = block_codes // 2
    column = jnp.arange(2 * half_codes, dtype=jnp.int32)
    block_here = (column // half_codes) * 2 + at_l
    column_code = full(block_here * block_codes + at_c * half_codes + column % half_codes)[None, :]
    branch_two, stream_two, logits, stats, d_logits, losses, others, inputs_out = ([None] * 2 for _ in range(8))

    def norm_out(r, parts):
        branch_two[r], stream_two[r], given = onward(parts, stream_one[r], hot[r], mod_rows[r], (5, 6, 7))
        return given

    def score(r, pieces):
        inputs_out[r], logits[r], stats[r] = head(pieces, held[0], cols[r], column_code)
        return stats[r]

    def compare(r):
        return [over_c(stats[r]), over_l(stats[r]), over_cl(stats[r])]

    def score_back(r):
        lines, losses[r] = merge(weight_sum, stats[r], *others[r], rows[r])
        d_logits[r], top[r], bottom[r] = head_back(logits[r], held[0], cols[r], column_code, lines)
        return top[r], bottom[r]

    pieces_out, stats[0], _, _ = turn(
        norm_out, score, lambda: held[0], keep=lambda done: held.__setitem__(0, done)
    )
    pieces_out[1].append(over_c(pieces_out[1][1]))
    stats[1], others[0] = window(score(1, pieces_out[1]), compare(0))
    (top[0], bottom[0]), others[1] = window(score_back(0), compare(1))
    sent = launch()
    logits[1] = tie(logits[1], sent)
    (top[1], bottom[1]), across[0] = window(score_back(1), across[0])

    def reduced(a):
        shape = a.shape[1:]
        a = lax.psum_scatter(a.reshape(-1, shape[2]), "g", scatter_dimension=0, tiled=True)
        return a.reshape(shape)

    def theirs(a):
        return jnp.where(at_h == 0, a[1], a[0])

    def settle(a, other):
        a = full(jnp.where(at_h == 0, a[0], a[1])) + full(other)
        rows = a.shape[0] // 2
        kept = jnp.where(at_c == 0, a[:rows], a[rows:])
        return kept, over_c(jnp.where(at_c == 0, a[rows:], a[:rows]))

    d_two, d_one, items_out, items_two, d_hidden, d_branch_two, d_branch_one = ([None] * 2 for _ in range(7))

    def back_out(r, parts):
        d_two[r], given, items_out[r] = back(
            parts, stream_two[r], hot[r], mod_rows[r], (7, 5), None, branch_two[r], None
        )
        return given

    def backward(r, pieces):
        d_branch_two[r], d_hidden[r], top[r], bottom[r] = feed_back(pieces, slopes[r], feed_full)
        return top[r], bottom[r]

    pieces_d_two, (top[0], bottom[0]), head_part, _ = turn(
        back_out, backward, lambda: head_grad_of(inputs_out, d_logits, g_count)
    )
    head_sum = reduced(head_part)
    pieces_d_two[1].append(over_c(pieces_d_two[1][1]))
    sent = launch()
    (top[1], bottom[1]), across[0], head_sum = window(
        backward(1, [tie(pieces_d_two[1][0], sent)] + pieces_d_two[1][1:]), across[0], head_sum
    )

    d_qkv, scale_rows = ([None] * 2 for _ in range(2))

    def back_two(r, parts):
        d_one[r], given, items_two[r] = back(
            parts, stream_one[r], hot[r], mod_rows[r], (4, 2), d_two[r], branch_one[r], None
        )
        return given

    def attention_back(r, pieces):
        d_branch_one[r], d_qkv[r], scale_rows[r], top[r], bottom[r] = attend_back(
            qkv_rows[r], gain_row, cols[r], rows[r], lse_rows[r], pieces, proj_full, qkv_full
        )
        return top[r], bottom[r]

    pieces_d_one, (top[0], bottom[0]), feed_part, head_other = turn(
        back_two,
        attention_back,
        lambda: feed_grad_of(inputs_two, d_hidden, d_branch_two, acts, g_count),
        over_h(theirs(head_sum)),
    )
    feed_sum = reduced(feed_part)
    pieces_d_one[1].append(over_c(pieces_d_one[1][1]))
    sent = launch()
    leaving = theirs(feed_sum)
    (top[1], bottom[1]), across[0], feed_other = window(
        attention_back(1, [tie(pieces_d_one[1][0], sent, leaving)] + pieces_d_one[1][1:]), across[0], over_h(leaving)
    )
    moved[1] = over_c(bottom[1])
    items_one, lead_parts = ([None] * 2 for _ in range(2))

    def back_one(r, parts):
        items_one[r], lead_parts[r] = back(
            parts, stream_zero[r], hot[r], mod_rows[r], (1,), d_one[r], None, feats[r]
        )
        return items_one[r]

    items_one[0], moved[1] = window(back_one(0, (top[0], moved[0], across[0])), moved[1])
    sent = far_part(1)
    across[1] = over_l(sent)
    first_part = first_grad_of(inputs_one, tie(d_qkv, sent), d_branch_one, mixed_rows, g_count)
    first_part, across[1] = window(first_part, across[1])
    first_sum = reduced(first_part)
    back_one(1, (top[1], moved[1], across[1]))
    lead_part = lead_parts[0] + lead_parts[1]

    def flat_items(items, number):
        return jnp.concatenate([items[r][number, :item_count] for r in range(2)], 0)

    d_items = jnp.concatenate(
        [flat_items(items_one, 0), flat_items(items_one, 1), flat_items(items_two, 2)]
        + [flat_items(items_two, 0), flat_items(items_two, 1), flat_items(items_out, 2)]
        + [flat_items(items_out, 0), flat_items(items_out, 1)],
        1,
    )
    left, right = d_items[:, :mod_half], d_items[:, mod_half:]
    d_items = jnp.where(at_c == 0, left, right) + over_c(jnp.where(at_c == 0, right, left))
    d_items = low(d_items + over_l(d_items))
    d_items, first_sum = window(ordered(at_h, d_items, over_h(d_items), 0), first_sum)
    leaving = theirs(first_sum)
    d_items = gather_g(tie(d_items, leaving))
    d_items = ordered(at_c, d_items, over_c(d_items), 1)
    ada_grad = dot_tn(activated, d_items)
    d_act_vec = dot_nt(d_items, ada_low)
    d_class = d_act_vec * (sigma * (1.0 + class_vec * (1.0 - sigma)))
    lead_part = jnp.transpose(lead_part.reshape(lead_pad, dp_count, slice_width), (1, 0, 2))
    lead_grad = jnp.sum(lax.all_to_all(lead_part, DP, 0, 0, tiled=True).reshape(dp_count, lead_pad, slice_width), 0)
    lead_grad = lead_grad + over_l(lead_grad)
    lead_grad = lead_grad + over_h(lead_grad)
    tables_grad = dot_tn(full(class_hot), d_class, highest)
    tables_grad = tables_grad + jnp.pad(lead_grad[:lead], ((0, table_rows - lead), (0, 0)))

    head_grad = ordered(at_c, *settle(tie(head_sum, items_one[0]), head_other), 1)
    kept, moved_half = settle(feed_sum, feed_other)
    n = kept.shape[1] // 2
    fc1_grad = ordered(at_c, kept[:, :n], moved_half[:, :n], 1)
    fc2_grad = ordered(at_c, kept[:, n:], moved_half[:, n:], 1)
    ada_grad, tables_grad, first_other = window(ada_grad, tables_grad, over_h(leaving))
    kept, moved_half = settle(first_sum, first_other)
    first_halves = jnp.stack([kept, moved_half])
    first_halves = jnp.where(at_c == 0, first_halves, first_halves[::-1])
    first_halves = jnp.transpose(first_halves.reshape(2, slice_width, 4, -1), (2, 1, 0, 3))
    first_halves = first_halves.reshape(4, slice_width, -1)
    qkv_grad, proj_grad = first_halves[:3], first_halves[3]

    decay = 1.0 - STEP ** (-0.8)
    grads = [qkv_grad, proj_grad, fc1_grad, fc2_grad, head_grad, ada_grad]
    wide = [g.size // slice_width * (mp_count if k < 5 else 1) for k, g in enumerate(grads)]
    sizes = [g.size // slice_width for g in grads]
    starts = [sum(sizes[:k]) for k in range(7)]

    def over_mp(a):
        a = a + over_l(a)
        return a + over_h(a)

    spots = jnp.arange(128, dtype=jnp.int32)[None, :]
    early_line = over_mp(tie(olds[:1] + jnp.where(spots == 22, losses[0] + losses[1], 0.0), lead_part))
    tail = early_line + olds[1:]
    rows_all = over_mp(row_stats(*grads[:5]))
    wide_column = jnp.array(wide[:5], full_type)[:, None]
    row_new = decay * d_stats[:5] + (1.0 - decay) * (rows_all[:5] / wide_column)
    tables_v_new = decay * tables_v + (1.0 - decay) * (tables_grad * tables_grad + eps_one)
    tables_step = tables_grad * lax.rsqrt(tables_v_new)
    tables_sum = jnp.sum(tables_step * tables_step)[None, None]
    scales = tie(scale_rows[0] + scale_rows[1], lead_part)
    scales = jnp.where(at_h == 0, scales[0], scales[1]) + over_h(
        jnp.where(at_h == 0, scales[1], scales[0])
    )
    flat, ada_row = column_stats(at_c, row_new, d_stats[5:6], tail, tables_sum, scales, grads, decay)
    d_stats_new = jnp.concatenate([row_new, ada_row[:1]], 0)
    if g_count == 4:
        flat = flat + over_c(flat)
        flat = flat + over_g(flat, 1)
        flat = flat + over_g(flat, 2)
    else:
        flat = lax.psum(flat, DP)
    col_old = jnp.concatenate(
        [qkv_stat.reshape(-1), proj_stat, fc1_stat, fc2_stat, head_stat, ada_stat]
    )[None, :]
    heads = head_scale.shape[0]
    scale_line = jnp.pad(scale_v, (11, 128 - 11 - heads), constant_values=1.0)[None, :]
    col_line, part_line, own_line, second_line, scale_step = finish(
        flat, col_old, scale_line, decay, width, starts
    )
    col_new = [col_line[0, starts[k] : starts[k + 1]] for k in range(6)]
    line = flat[:1, starts[6] :]
    scale_grad = line[0, 11 : 11 + heads]
    loss_sum = line[0, 22]
    scale_v_new = second_line[0, 11 : 11 + heads]
    entries = [width * wide[k] for k in range(6)] + [table_rows * width, heads * mp_count]
    news = renew(
        (line, over_mp(part_line), own_line, early_line),
        d_stats_new,
        col_line,
        grads,
        (tables_step, scale_step),
        (
            qkv_w, proj_w, fc1_w, fc2_w, head_w, ada_w, tables,
            jnp.pad(head_scale, (11, 128 - 11 - heads))[None, :],
        ),
        width,
        entries,
        starts,
    )
    return (
        loss_sum,
        weight_sum,
        qkv_grad,
        news[8],
        fc1_grad,
        news[9],
        head_grad,
        ada_grad,
        tables_grad,
        scale_grad,
        d_stats_new,
        col_new[0].reshape(3, -1),
        col_new[1],
        col_new[2],
        col_new[3],
        col_new[4],
        col_new[5],
        tables_v_new,
        scale_v_new,
        news[0],
        news[1],
        news[2],
        news[3],
        news[4],
        news[5],
        news[6],
        news[7][0, 11 : 11 + heads],
    )


def solution(mesh):
    inner = Mesh(
        mesh.devices.reshape(mesh.shape["dp"] // 2, 2, mesh.shape["mp"] // 2, 2),
        ("g", "c", "h", "l"),
    )
    return jax.shard_map(
        body,
        mesh=inner,
        in_specs=(
            P(DP, None, None),
            P(DP, None),
            P(DP, None),
            P(DP, None),
            P(DP, None),
            P(),
            P(None, DP, MP),
            P(MP, DP),
            P(DP, MP),
            P(MP, DP),
            P(DP, MP),
            P(DP, None),
            P(None, DP),
            P(MP),
            P(None, DP),
            P(None, MP),
            P(MP),
            P(MP),
            P(MP),
            P(MP),
            P(),
            P(None, DP),
            P(MP),
        ),
        out_specs=(
            P(),
            P(),
            P(None, DP, MP),
            P(MP, DP),
            P(DP, MP),
            P(MP, DP),
            P(DP, MP),
            P(DP, None),
            P(None, DP),
            P(MP),
            P(None, DP),
            P(None, MP),
            P(MP),
            P(MP),
            P(MP),
            P(MP),
            P(),
            P(None, DP),
            P(MP),
            P(None, DP, MP),
            P(MP, DP),
            P(DP, MP),
            P(MP, DP),
            P(DP, MP),
            P(DP, None),
            P(None, DP),
            P(MP),
        ),
        check_vma=False,
    )
```

```python
import functools
import math

import jax
import jax.numpy as jnp
from jax import lax
from jax.experimental import pallas as pl
from jax.experimental.pallas import tpu as pltpu
from jax.sharding import Mesh, PartitionSpec as P

STEP = 8
level_starts = (1, 5, 14, 30, 55, 91, 155, 255, 424)
eps_norm = 1e-06
eps_one = 1e-30
eps_two = 0.001
rate_step = 0.3
clip_rms = 1.0
low_type = jnp.bfloat16
full_type = jnp.float32
high = lax.Precision.HIGH
highest = lax.Precision.HIGHEST
swap_pairs = ((0, 1), (1, 0))
busy_us = {
    "row_layout": 2, "enter": 5, "enter_first": 6, "attend": 11, "onward": 2, "feed": 5, "head": 6, "merge": 2,
    "head_back": 5, "back": 5, "feed_back": 7, "attend_back": 16, "old_stats": 4, "row_stats": 3,
    "column_stats": 5, "finish": 2, "head_grad": 6, "feed_grad": 12, "first_grad": 6,
    "renew": 8, "arrange": 4,
}
DP = ("g", "c")
MP = ("h", "l")


def cost(name):
    return pl.CostEstimate(flops=busy_us[name] * 10**9, transcendentals=0, bytes_accessed=busy_us[name] * 10**6)


def low(a):
    return a.astype(low_type)


def full(a):
    return a.astype(full_type)


def dot_nn(a, b, precision=None):
    return jnp.dot(a, b, preferred_element_type=full_type, precision=precision)


def dot_nt(a, b, precision=None):
    return lax.dot_general(
        a, b, (((1,), (1,)), ((), ())), preferred_element_type=full_type, precision=precision
    )


def dot_tn(a, b, precision=None):
    return lax.dot_general(
        a, b, (((0,), (0,)), ((), ())), preferred_element_type=full_type, precision=precision
    )


def over_c(a):
    return lax.ppermute(a, "c", swap_pairs)


def over_l(a):
    return lax.ppermute(a, "l", swap_pairs)


def over_h(a):
    return lax.ppermute(a, "h", swap_pairs)


def over_cl(a):
    return lax.ppermute(a, ("c", "l"), [(i, i ^ 3) for i in range(4)])


def over_g(a, k):
    return lax.ppermute(a, "g", [(i, i ^ k) for i in range(lax.axis_size("g"))])


def ordered(flag, mine, other, axis):
    return jnp.where(
        flag == 0,
        jnp.concatenate([mine, other], axis),
        jnp.concatenate([other, mine], axis),
    )


def gather_g(a):
    count = lax.axis_size("g")
    if count != 4:
        return lax.all_gather(a, "g", axis=0, tiled=True)
    here = lax.axis_index("g")
    out = jnp.zeros((4,) + a.shape, a.dtype)
    for k in range(4):
        piece = a if k == 0 else over_g(a, k)
        out = lax.dynamic_update_index_in_dim(out, piece, here ^ k, 0)
    return out.reshape((4 * a.shape[0],) + a.shape[1:])


def scatter_g(a):
    count = lax.axis_size("g")
    if count != 4:
        return full(lax.psum_scatter(a, "g", scatter_dimension=0, tiled=True))
    here = lax.axis_index("g")
    blocks = a.reshape((4, a.shape[0] // 4) + a.shape[1:])
    total = full(lax.dynamic_index_in_dim(blocks, here, 0, False))
    for k in range(1, 4):
        total = total + full(over_g(lax.dynamic_index_in_dim(blocks, here ^ k, 0, False), k))
    return total


def tie(a, *others):
    return lax.optimization_barrier((a,) + others)[0]


def centre(values):
    centered = values - jnp.mean(values, -1, keepdims=True)
    scale = lax.rsqrt(jnp.mean(centered * centered, -1, keepdims=True) + eps_norm)
    return centered * scale, scale


def centre_back(normed, scale, incoming):
    return (
        incoming
        - jnp.mean(incoming, -1, keepdims=True)
        - normed * jnp.mean(incoming * normed, -1, keepdims=True)
    ) * scale


def gelu_parts(values):
    root = math.sqrt(2.0 / math.pi)
    square = values * values
    bent = jnp.tanh(values * (root + (root * 0.044715) * square))
    half = 0.5 + 0.5 * bent
    slope = half + values * (0.5 - 0.5 * (bent * bent)) * (root + (root * 3.0 * 0.044715) * square)
    return values * half, slope


def split_parts(a, count):
    parts = []
    for _ in range(count):
        parts.append(low(a))
        a = a - full(parts[-1])
    return parts


def item_parts(vectors):
    return jnp.concatenate(split_parts(vectors, 3) + [jnp.zeros(vectors.shape, low_type)], 0)


def item_sums(hot, values):
    upper, lower = split_parts(values, 2)
    return (dot_tn(hot, upper) + dot_tn(hot, lower))[:8]


def whole(shape):
    return pl.BlockSpec(shape, lambda i: (0,) * len(shape), pipeline_mode=pl.Buffered(1))


def tiled(tile, columns):
    return pl.BlockSpec((tile, columns), lambda i: (i, 0))


def call(kernel, grid, in_specs, out_specs, out_shape, scratch, name):
    return pl.pallas_call(
        kernel,
        grid=grid,
        in_specs=in_specs,
        out_specs=out_specs,
        out_shape=[jax.ShapeDtypeStruct(shape, dtype) for shape, dtype in out_shape],
        scratch_shapes=scratch,
        compiler_params=pltpu.CompilerParams(vmem_limit_bytes=62 * 2**20),
        cost_estimate=cost(name),
        name=name,
    )


def rows_kernel(lw_ref, seg_ref, live_ref, place_ref, weight_ref, sum_ref):
    seg, live = seg_ref[...], live_ref[...]
    at = lax.broadcasted_iota(jnp.int32, seg.shape, 1)
    first = jnp.zeros_like(seg)
    for item in range(1, 4):
        count = jnp.sum(full(jnp.where(seg < item, 1, 0)), 1, keepdims=True).astype(jnp.int32)
        first = jnp.where(seg == item, count, first)
    within = at - first
    level = jnp.zeros_like(seg)
    for start in level_starts:
        level = level + jnp.where(within >= start, 1, 0)
    weight = jnp.zeros_like(seg)
    for position in range(lw_ref.shape[0]):
        weight = jnp.where(level == position, lw_ref[position], weight)
    weight = weight * live
    place_ref[...] = seg * 16 + level
    weight_ref[...] = weight
    each = jnp.sum(full(weight), 1, keepdims=True)
    sum_ref[...] = jnp.sum(each, 0, keepdims=True).astype(jnp.int32)


def row_layout(level_weight, segment, live):
    shape = segment.shape
    return pl.pallas_call(
        rows_kernel,
        in_specs=[pl.BlockSpec(memory_space=pltpu.SMEM)] + [pl.BlockSpec(memory_space=pltpu.VMEM)] * 2,
        out_shape=[
            jax.ShapeDtypeStruct(shape, jnp.int32),
            jax.ShapeDtypeStruct(shape, jnp.int32),
            jax.ShapeDtypeStruct((1, 1), jnp.int32),
        ],
        compiler_params=pltpu.CompilerParams(vmem_limit_bytes=62 * 2**20),
        cost_estimate=cost("row_layout"),
        name="row_layout",
    )(level_weight, segment, live)


def arrange_kernel(at_ref, mine_ref, other_ref, vq_ref, vq_other_ref, *refs):
    quarter = mine_ref.shape[2] // 4
    cols_s, vq_s = refs[-2:]
    use_mine, at_c, at_l = at_ref[0], at_ref[1], at_ref[2]
    n = 4 * quarter
    lane = lax.broadcasted_iota(jnp.int32, (n, 128), 1)
    for r in range(2):
        feat_ref, hot_ref, col_ref, row_ref = refs[4 * r : 4 * r + 4]
        info = jnp.where(use_mine == 1, mine_ref[r], other_ref[r])
        cols_s[...] = jnp.concatenate([info, jnp.zeros((124, n), full_type)], 0).T
        vq_s[...] = jnp.where(use_mine == 1, full(vq_ref[r]), full(vq_other_ref[r]))
        cols, vqs = [], []
        for k in range(4):
            start = jnp.bitwise_xor(at_c, k // 2) * 2 + jnp.bitwise_xor(at_l, k % 2)
            rows = pl.ds(pl.multiple_of(start * quarter, quarter), quarter)
            cols.append(cols_s[rows, :])
            vqs.append(vq_s[rows, :])
        cols = jnp.concatenate(cols, 0)
        code, place, live, weight = (cols[:, k : k + 1] for k in range(4))
        segment = jnp.floor(place * (1.0 / 16.0))
        base = segment * 16.0
        key = jnp.where(live > 0.0, place, 1048576.0)
        out = jnp.zeros((n, 128), full_type)
        for k, column in enumerate((place, base, key, code, weight)):
            out = jnp.where(lane == k, column, out)
        col_ref[...] = out
        row_ref[...] = out.T[0:8, :]
        spot = lax.broadcasted_iota(jnp.int32, (n, 16), 1)
        hit = (full(spot % 4) == segment) & (spot < 12)
        hot_ref[...] = low(jnp.where(hit, 1.0, 0.0))
        code_dim, padded = vq_ref.shape[2], feat_ref.shape[1]
        spread = lax.broadcasted_iota(jnp.int32, (code_dim, padded), 0) == lax.broadcasted_iota(
            jnp.int32, (code_dim, padded), 1
        )
        feats = dot_nn(low(jnp.concatenate(vqs, 0)), low(jnp.where(spread, 1.0, 0.0)))
        level = lax.broadcasted_iota(jnp.int32, (n, padded), 1) - code_dim
        feat_ref[...] = low(feats + jnp.where(full(level) == place - base, 1.0, 0.0))


def arrange(at, mine, other, vq, vq_other, padded):
    n, code_dim = vq.shape[1:]
    shapes = [((n, padded), low_type), ((n, 16), low_type), ((n, 128), full_type), ((8, n), full_type)] * 2
    return pl.pallas_call(
        arrange_kernel,
        in_specs=[pl.BlockSpec(memory_space=pltpu.SMEM)] + [pl.BlockSpec(memory_space=pltpu.VMEM)] * 4,
        out_shape=[jax.ShapeDtypeStruct(shape, dtype) for shape, dtype in shapes],
        scratch_shapes=[pltpu.VMEM((n, 128), full_type), pltpu.VMEM((n, code_dim), full_type)],
        compiler_params=pltpu.CompilerParams(vmem_limit_bytes=62 * 2**20),
        cost_estimate=cost("arrange"),
        name="arrange",
    )(at, mine, other, vq, vq_other)


def enter_tile(feat_ref, table_ref, hot_ref, w, in_ref, qkv_ref, stream_ref, parts_s):
    stream = dot_nn(feat_ref[...], table_ref[...])

    @pl.when(pl.program_id(0) == 0)
    def _():
        stream_ref[...] = stream[: stream_ref.shape[0]]

    normed, _ = centre(stream)
    hot = hot_ref[...]
    given = low(normed * (1.0 + dot_nn(hot, parts_s[1])) + dot_nn(hot, parts_s[0]))
    in_ref[...] = given
    qkv_ref[...] = dot_nn(given, w)


def enter_parts(mod_ref, parts_s):
    parts_s[0] = item_parts(mod_ref[0])
    parts_s[1] = item_parts(mod_ref[1])


def enter_kernel(feat_ref, table_ref, hot_ref, mod_ref, w_ref, in_ref, qkv_ref, stream_ref, parts_s):
    @pl.when(pl.program_id(0) == 0)
    def _():
        enter_parts(mod_ref, parts_s)

    enter_tile(feat_ref, table_ref, hot_ref, w_ref[...], in_ref, qkv_ref, stream_ref, parts_s)


def enter(feats, table, hot, mods, w):
    n, k = feats.shape
    width, columns = w.shape
    tile = n // 2
    return call(
        enter_kernel,
        (2,),
        [tiled(tile, k), whole((k, width)), tiled(tile, 16), whole(mods.shape), whole(w.shape)],
        [tiled(tile, width), tiled(tile, columns), fixed((tile // 2, width))],
        [((n, width), low_type), ((n, columns), full_type), ((tile // 2, width), full_type)],
        [pltpu.VMEM((2, 16, width), low_type)],
        "enter",
    )(feats, table, hot, mods, w)


def enter_first_kernel(
    at_ref, feat_ref, table_ref, hot_ref, mod_ref, a_ref, b_ref, c_ref, d_ref, in_ref, qkv_ref, stream_ref,
    w_ref, p_ref, parts_s
):
    @pl.when(pl.program_id(0) == 0)
    def _():
        enter_parts(mod_ref, parts_s)
        for k, ref in enumerate((a_ref, b_ref, c_ref, d_ref)):
            rows = ref.shape[2]
            start = pl.multiple_of(jnp.bitwise_xor(at_ref[0], k) * rows, rows)
            for j in range(2):
                for c in range(3):
                    w_ref[pl.ds(start, rows), (2 * c + j) * 128 : (2 * c + j + 1) * 128] = ref[j, c]
                p_ref[pl.ds(start, rows), j * 128 : (j + 1) * 128] = ref[j, 3]

    enter_tile(feat_ref, table_ref, hot_ref, w_ref[...], in_ref, qkv_ref, stream_ref, parts_s)


def enter_first(here, feats, table, hot, mods, pieces):
    n, k = feats.shape
    width = table.shape[1]
    columns = 768
    tile = n // 2
    shape = pieces[0].shape
    return call(
        enter_first_kernel,
        (n // tile,),
        [pl.BlockSpec(memory_space=pltpu.SMEM), tiled(tile, k), whole((k, width)), tiled(tile, 16), whole(mods.shape)]
        + [whole(shape)] * 4,
        [tiled(tile, width), tiled(tile, columns), fixed((tile // 2, width))]
        + [fixed((width, columns)), fixed((width, columns // 3))],
        [((n, width), low_type), ((n, columns), full_type), ((tile // 2, width), full_type)]
        + [((width, columns), low_type), ((width, columns // 3), low_type)],
        [pltpu.VMEM((2, 16, width), low_type)],
        "enter_first",
    )(here[None], feats, table, hot, mods, *pieces)


def onward_kernel(a_ref, b_ref, c_ref, x_ref, hot_ref, mod_ref, br_ref, y_ref, in_ref, parts_s, *, picks):
    @pl.when(pl.program_id(0) == 0)
    def _():
        for k, pick in enumerate(picks):
            parts_s[k] = item_parts(mod_ref[pick])

    branch = full(a_ref[...]) + full(b_ref[...]) + full(c_ref[...])
    br_ref[...] = branch
    hot = hot_ref[...]
    stream = x_ref[...] + dot_nn(hot, parts_s[0]) * branch
    y_ref[...] = stream
    normed, _ = centre(stream)
    in_ref[...] = low(normed * (1.0 + dot_nn(hot, parts_s[2])) + dot_nn(hot, parts_s[1]))


def onward(parts, stream, hot, mods, picks):
    n, width = parts[2].shape
    tile = n // 2
    return call(
        functools.partial(onward_kernel, picks=picks),
        (n // tile,),
        [tiled(tile, width)] * 4 + [tiled(tile, 16), whole(mods.shape)],
        [tiled(tile, width)] * 3,
        [((n, width), full_type), ((n, width), full_type), ((n, width), low_type)],
        [pltpu.VMEM((3, 16, width), low_type)],
        "onward",
    )(*parts, stream, hot, mods)


def back_kernel(*refs, gated, carried, picks):
    refs = list(refs)
    a_ref, b_ref, c_ref, x_ref, hot_ref, mod_ref = refs[:6]
    del refs[:6]
    res_ref = refs.pop(0) if carried else None
    br_ref = refs.pop(0) if gated else None
    feat_ref = None if gated else refs.pop(0)
    res_out = refs.pop(0) if gated else None
    d_ref = refs.pop(0) if gated else None
    items_ref = refs.pop(0)
    lead_ref = None if gated else refs.pop(0)
    parts_s = refs.pop(0)

    @pl.when(pl.program_id(0) == 0)
    def _():
        for k, pick in enumerate(picks):
            parts_s[k] = item_parts(mod_ref[pick])
        items_ref[...] = jnp.zeros_like(items_ref)
        if not gated:
            lead_ref[...] = jnp.zeros_like(lead_ref)

    hot = hot_ref[...]
    incoming = full(a_ref[...]) + full(b_ref[...]) + full(c_ref[...])
    normed, scale = centre(x_ref[...])
    items_ref[0] += item_sums(hot, incoming)
    items_ref[1] += item_sums(hot, incoming * normed)
    res = centre_back(normed, scale, incoming * (1.0 + dot_nn(hot, parts_s[0])))
    if carried:
        res = res + res_ref[...]
    if gated:
        res_out[...] = res
        items_ref[2] += item_sums(hot, res * br_ref[...])
        d_ref[...] = low(res * dot_nn(hot, parts_s[1]))
    else:
        upper, lower = split_parts(res, 2)
        feats = feat_ref[...]
        lead_ref[...] += dot_tn(feats, upper) + dot_tn(feats, lower)


def back(parts, stream, hot, mods, picks, carried, branch, feats):
    n, width = parts[2].shape
    tile = n // 2
    gated, has = branch is not None, carried is not None
    extra = ([carried] if has else []) + ([branch] if gated else [feats])
    specs = [tiled(tile, width)] * 4 + [tiled(tile, 16), whole(mods.shape)]
    specs += [tiled(tile, a.shape[1]) for a in extra]
    count = 3 if gated else 2
    out_specs, out_shape = [], []
    if gated:
        out_specs += [tiled(tile, width)] * 2
        out_shape += [((n, width), full_type), ((n, width), low_type)]
    out_specs.append(fixed((count, 8, width)))
    out_shape.append(((count, 8, width), full_type))
    if not gated:
        out_specs.append(fixed((feats.shape[1], width)))
        out_shape.append(((feats.shape[1], width), full_type))
    return call(
        functools.partial(back_kernel, gated=gated, carried=has, picks=picks),
        (n // tile,),
        specs,
        out_specs,
        out_shape,
        [pltpu.VMEM((2, 16, width), low_type)],
        "back",
    )(*parts, stream, hot, mods, *extra)


def either(a_ref, b_ref, c_ref, d_ref):
    top = jnp.concatenate([a_ref[...], b_ref[...]], 0)
    return jnp.where(pl.program_id(0) == 0, top, jnp.concatenate([c_ref[...], d_ref[...]], 0))


def put(value, top_ref, bottom_ref):
    @pl.when(pl.program_id(0) == 0)
    def _():
        top_ref[...] = value

    @pl.when(pl.program_id(0) == 1)
    def _():
        bottom_ref[...] = value


def fixed(shape):
    return pl.BlockSpec(shape, lambda i: (0,) * len(shape))


def column_half(shape, number):
    return pl.BlockSpec(
        shape[:3] + (shape[3] // 2,), lambda i: (0, 0, 0, number), pipeline_mode=pl.Buffered(1)
    )


def block_of(ref, h):
    return ref[:, h].reshape(-1, ref.shape[3])


def feed_kernel(a_ref, b_ref, c_ref, d_ref, one_ref, two_ref, row_ref, act_ref, slope_ref, top_ref, bottom_ref):
    given = either(a_ref, b_ref, c_ref, d_ref)
    row_ref[...] = given
    units = one_ref.shape[3]
    total = None
    for h in range(2):
        at = slice(h * units, (h + 1) * units)
        act, slope = gelu_parts(dot_nn(given, block_of(one_ref, h)))
        act = low(act)
        act_ref[:, at] = act
        slope_ref[:, at] = slope
        part = dot_nt(act, block_of(two_ref, h))
        total = part if total is None else total + part
    put(low(total), top_ref, bottom_ref)


def feed(pieces, both):
    tile, width = 2 * pieces[0].shape[0], pieces[0].shape[1]
    units = both.shape[3]
    return call(
        feed_kernel,
        (2,),
        [whole(pieces[0].shape)] * 4 + [column_half(both.shape, k) for k in range(2)],
        [tiled(tile, width), tiled(tile, units), tiled(tile, units), fixed((tile, width)), fixed((tile, width))],
        [((2 * tile, width), low_type), ((2 * tile, units), low_type), ((2 * tile, units), full_type)]
        + [((tile, width), low_type)] * 2,
        [],
        "feed",
    )(*pieces, both, both)


def feed_back_kernel(a_ref, b_ref, c_ref, d_ref, slope_ref, one_ref, two_ref, row_ref, dh_ref, top_ref, bottom_ref):
    given = either(a_ref, b_ref, c_ref, d_ref)
    row_ref[...] = given
    units = one_ref.shape[3]
    total = None
    for h in range(2):
        at = slice(h * units, (h + 1) * units)
        d_hidden = low(dot_nn(given, block_of(two_ref, h)) * slope_ref[:, at])
        dh_ref[:, at] = d_hidden
        part = dot_nt(d_hidden, block_of(one_ref, h))
        total = part if total is None else total + part
    put(low(total), top_ref, bottom_ref)


def feed_back(pieces, slope, both):
    tile, width = 2 * pieces[0].shape[0], pieces[0].shape[1]
    units = both.shape[3]
    return call(
        feed_back_kernel,
        (2,),
        [whole(pieces[0].shape)] * 4 + [tiled(tile, units)] + [column_half(both.shape, k) for k in range(2)],
        [tiled(tile, width), tiled(tile, units), fixed((tile, width)), fixed((tile, width))],
        [((2 * tile, width), low_type), ((2 * tile, units), low_type)] + [((tile, width), low_type)] * 2,
        [],
        "feed_back",
    )(*pieces, slope, both, both)


def head_kernel(a_ref, b_ref, c_ref, d_ref, w_ref, code_ref, column_ref, row_ref, logit_ref, stat_ref):
    given = either(a_ref, b_ref, c_ref, d_ref)
    row_ref[...] = given
    logits = jnp.concatenate([dot_nn(given, block_of(w_ref, h)) for h in range(2)], 1)
    logit_ref[...] = logits
    peak = jnp.max(logits, 1, keepdims=True)
    total = jnp.sum(jnp.exp(logits - peak), 1, keepdims=True)
    picked = jnp.sum(jnp.where(code_ref[:, 3:4] == column_ref[...], logits, 0.0), 1, keepdims=True)
    lane = lax.broadcasted_iota(jnp.int32, (logits.shape[0], 128), 1)
    turned = jnp.where(lane == 0, peak, jnp.where(lane == 1, total, picked)).T
    stat_ref[...] = turned[0:8, :]


def head(pieces, w, code, column):
    tile, width = 2 * pieces[0].shape[0], pieces[0].shape[1]
    units = 2 * w.shape[3]
    return call(
        head_kernel,
        (2,),
        [whole(pieces[0].shape)] * 4 + [whole(w.shape), tiled(tile, 128), whole((1, units))],
        [tiled(tile, width), tiled(tile, units), pl.BlockSpec((8, tile), lambda i: (0, i))],
        [((2 * tile, width), low_type), ((2 * tile, units), full_type), ((8, 2 * tile), full_type)],
        [],
        "head",
    )(*pieces, w, code, column)


def merge_kernel(sum_ref, here_ref, c_ref, l_ref, d_ref, weight_ref, out_ref, loss_ref):
    half = here_ref.shape[1] // 2

    def over_core(a):
        return jnp.concatenate([a[:, half:], a[:, :half]], 1)

    def over_line(a):
        return jnp.concatenate(
            [pltpu.roll(a[:, :half], half // 2, 1), pltpu.roll(a[:, half:], half // 2, 1)], 1
        )

    parts = (here_ref[...], over_core(c_ref[...]), over_line(l_ref[...]), over_core(over_line(d_ref[...])))
    peak = functools.reduce(jnp.maximum, [part[0:1] for part in parts])
    total = sum(part[1:2] * jnp.exp(part[0:1] - peak) for part in parts)
    picked = sum(part[2:3] for part in parts)
    log_total = peak + jnp.log(total)
    weight = weight_ref[4:5, :]
    spot = lax.broadcasted_iota(jnp.int32, (1, 2 * half), 1)
    loss = jnp.where(spot < half // 2, weight * (log_total - picked), 0.0)
    loss_ref[...] = jnp.broadcast_to(jnp.sum(loss, 1, keepdims=True), loss_ref.shape)
    blank = jnp.zeros((126, 2 * half), full_type)
    out_ref[...] = jnp.concatenate([log_total, weight / sum_ref[0], blank], 0).T


def merge(weight_sum, here, over_core, over_line, over_both, weights):
    n = here.shape[1]
    return pl.pallas_call(
        merge_kernel,
        in_specs=[pl.BlockSpec(memory_space=pltpu.SMEM)] + [pl.BlockSpec(memory_space=pltpu.VMEM)] * 5,
        out_shape=[jax.ShapeDtypeStruct((n, 128), full_type), jax.ShapeDtypeStruct((1, 128), full_type)],
        compiler_params=pltpu.CompilerParams(vmem_limit_bytes=62 * 2**20),
        cost_estimate=cost("merge"),
        name="merge",
    )(weight_sum[None], here, over_core, over_line, over_both, weights)


def head_back_kernel(logit_ref, w_ref, code_ref, column_ref, line_ref, d_ref, top_ref, bottom_ref):
    hit = jnp.where(code_ref[:, 3:4] == column_ref[...], 1.0, 0.0)
    line = line_ref[...]
    d_logits = low(line[:, 1:2] * (jnp.exp(logit_ref[...] - line[:, 0:1]) - hit))
    d_ref[...] = d_logits
    units = w_ref.shape[3]
    total = dot_nt(d_logits[:, :units], block_of(w_ref, 0)) + dot_nt(d_logits[:, units:], block_of(w_ref, 1))
    put(low(total), top_ref, bottom_ref)


def head_back(logits, w, code, column, lines):
    n, units = logits.shape
    width = w.shape[0] * w.shape[2]
    tile = n // 2
    return call(
        head_back_kernel,
        (2,),
        [tiled(tile, units), whole(w.shape), tiled(tile, 128), whole((1, units)), tiled(tile, 128)],
        [tiled(tile, units), fixed((tile, width)), fixed((tile, width))],
        [((n, units), low_type)] + [((tile, width), low_type)] * 2,
        [],
        "head_back",
    )(logits, w, code, column, lines)


def old_stats_kernel(qkv_ref, proj_ref, one_ref, two_ref, head_ref, ada_ref, tab_ref, scale_ref, out_ref):
    def total(values):
        return jnp.sum(jnp.sum(values * values, 1, keepdims=True), 0, keepdims=True)

    spot = lax.broadcasted_iota(jnp.int32, (1, 128), 1)
    line = jnp.zeros((1, 128), full_type)
    sums = [sum(total(qkv_ref[c]) for c in range(3))]
    sums += [total(ref[...]) for ref in (proj_ref, one_ref, two_ref, head_ref, scale_ref)]
    for k, value in enumerate(sums):
        line = jnp.where(spot == 16 + k, value, line)
    out_ref[0:1, :] = line
    line = jnp.where(spot == 8, total(ada_ref[...]), 0.0)
    out_ref[1:2, :] = jnp.where(spot == 9, total(tab_ref[...]), line)


def old_stats(*olds):
    return pl.pallas_call(
        old_stats_kernel,
        out_shape=jax.ShapeDtypeStruct((2, 128), full_type),
        compiler_params=pltpu.CompilerParams(vmem_limit_bytes=62 * 2**20),
        cost_estimate=cost("old_stats"),
        name="old_stats",
    )(*olds)


def put_rows(out_ref, start, value):
    groups, _, rows, _ = out_ref.shape
    for g in range(groups):
        out_ref[g, 0, :, start : start + value.shape[1]] = value[g * rows : (g + 1) * rows]


def head_grad_kernel(a_ref, b_ref, c_ref, d_ref, out_ref):
    put_rows(out_ref, 0, low(dot_tn(a_ref[...], c_ref[...]) + dot_tn(b_ref[...], d_ref[...])))


def head_grad_of(inputs, wanted, groups):
    n, width = inputs[0].shape
    columns = wanted[0].shape[1] // 2
    block = pl.BlockSpec((n, columns), lambda i: (0, i))
    return call(
        head_grad_kernel,
        (2,),
        [whole((n, width))] * 2 + [block] * 2,
        [pl.BlockSpec((groups, 1, width // groups, columns), lambda i: (0, i, 0, 0))],
        [((groups, 2, width // groups, columns), low_type)],
        [],
        "head_grad",
    )(*inputs, *wanted)[0]


def feed_grad_kernel(a_ref, b_ref, c_ref, d_ref, e_ref, f_ref, g_ref, h_ref, out_ref):
    @pl.when(pl.program_id(0) < 2)
    def _():
        put_rows(out_ref, 0, low(dot_tn(a_ref[...], c_ref[...]) + dot_tn(b_ref[...], d_ref[...])))

    @pl.when(pl.program_id(0) >= 2)
    def _():
        put_rows(out_ref, 0, low(dot_tn(e_ref[...], g_ref[...]) + dot_tn(f_ref[...], h_ref[...])))


def feed_grad_of(inputs, d_hidden, d_branch, acts, groups):
    n, width = inputs[0].shape
    columns = acts[0].shape[1] // 2
    early = pl.BlockSpec((n, columns), lambda i: (0, jnp.minimum(i, 1)))
    late = pl.BlockSpec((n, columns), lambda i: (0, jnp.maximum(i - 2, 0)))
    return call(
        feed_grad_kernel,
        (4,),
        [whole((n, width))] * 2 + [early] * 2 + [whole((n, width))] * 2 + [late] * 2,
        [pl.BlockSpec((groups, 1, width // groups, columns), lambda i: (0, i % 2, 0, i // 2))],
        [((groups, 2, width // groups, 2 * columns), low_type)],
        [],
        "feed_grad",
    )(*inputs, *d_hidden, *d_branch, *acts)[0]


def first_grad_kernel(a_ref, b_ref, c_ref, d_ref, e_ref, f_ref, g_ref, h_ref, out_ref):
    group = c_ref.shape[1] // 3
    start = pl.program_id(0) * 128

    def columns(ref):
        return jnp.concatenate(
            [ref[:, pl.ds(pl.multiple_of(start + c * group, 128), 128)] for c in range(3)], 1
        )

    put_rows(out_ref, 0, low(dot_tn(a_ref[...], columns(c_ref)) + dot_tn(b_ref[...], columns(d_ref))))
    put_rows(out_ref, 384, low(dot_tn(e_ref[...], g_ref[...]) + dot_tn(f_ref[...], h_ref[...])))


def first_grad_of(inputs, d_qkv, d_branch, mixed, groups):
    n, width = inputs[0].shape
    return call(
        first_grad_kernel,
        (2,),
        [whole((n, width))] * 2 + [whole(d_qkv[0].shape)] * 2 + [whole((n, width))] * 2
        + [pl.BlockSpec((n, 128), lambda i: (0, i))] * 2,
        [pl.BlockSpec((groups, 1, width // groups, 512), lambda i: (0, i, 0, 0))],
        [((groups, 2, width // groups, 512), low_type)],
        [],
        "first_grad",
    )(*inputs, *d_qkv, *d_branch, *mixed)[0]


def row_stats_kernel(qkv_ref, proj_ref, one_ref, two_ref, head_ref, out_ref):
    n = out_ref.shape[1]
    lane = lax.broadcasted_iota(jnp.int32, (n, 128), 1)
    out = jnp.zeros((n, 128), full_type)
    qkv = sum(jnp.sum(qkv_ref[c] * qkv_ref[c], 1, keepdims=True) for c in range(3))
    sums = [qkv + 3 * qkv_ref.shape[2] * eps_one]
    for ref in (proj_ref, one_ref, two_ref, head_ref):
        values = ref[...]
        sums.append(jnp.sum(values * values, 1, keepdims=True) + ref.shape[1] * eps_one)
    for k, column in enumerate(sums):
        out = jnp.where(lane == k, column, out)
    out_ref[...] = out.T[0:8, :]


def row_stats(*gradients):
    n = gradients[1].shape[0]
    return pl.pallas_call(
        row_stats_kernel,
        out_shape=jax.ShapeDtypeStruct((8, n), full_type),
        compiler_params=pltpu.CompilerParams(vmem_limit_bytes=62 * 2**20),
        cost_estimate=cost("row_stats"),
        name="row_stats",
    )(*gradients)


def column_stats_kernel(
    at_ref, row_ref, old_ref, tail_ref, tables_ref, scale_ref, qkv_ref, proj_ref, one_ref, two_ref, head_ref, ada_ref, out_ref, new_ref, *, decay
):
    n = proj_ref.shape[0]
    rows = row_ref[...]
    padded = jnp.concatenate([rows, jnp.zeros((128 - rows.shape[0], n), full_type)], 0).T
    at = 0
    pieces = [(qkv_ref[c], 0) for c in range(3)]
    pieces += [(ref[...], k + 1) for k, ref in enumerate((proj_ref, one_ref, two_ref, head_ref))]
    for values, k in pieces:
        square = values * values
        columns = square.shape[1]
        out_ref[0:1, at : at + columns] = jnp.sum(square, 0, keepdims=True) + n * eps_one
        out_ref[1:2, at : at + columns] = jnp.sum(
            square * (1.0 / padded[:, k : k + 1]), 0, keepdims=True
        )
        at += columns
    columns = ada_ref.shape[1]
    step = 1024
    total = jnp.zeros((n, 1), full_type)
    for start in range(0, columns, step):
        values = ada_ref[:, start : start + step]
        total = total + jnp.sum(values * values, 1, keepdims=True)
    old = jnp.concatenate([old_ref[...], jnp.zeros((127, n), full_type)], 0).T[:, 0:1]
    row = decay * old + (1.0 - decay) * (total / columns + eps_one)
    lane = lax.broadcasted_iota(jnp.int32, (n, 128), 1)
    new_ref[...] = jnp.where(lane == 0, row, 0.0).T[0:8, :]
    for start in range(0, columns, step):
        values = ada_ref[:, start : start + step]
        square = values * values
        out_ref[0:1, at : at + step] = jnp.sum(square, 0, keepdims=True) + n * eps_one
        out_ref[1:2, at : at + step] = jnp.sum(square * (1.0 / row), 0, keepdims=True)
        at += step
    spots = lax.broadcasted_iota(jnp.int32, (1, 128), 1)
    line = tail_ref[...]
    for k in range(5):
        line = jnp.where(spots == k, jnp.sum(rows[k : k + 1, :], 1, keepdims=True), line)
    line = jnp.where(spots == 5, jnp.sum(row, 0, keepdims=True), line)
    line = jnp.where(spots == 10, tables_ref[...], line)
    scales = scale_ref[...]
    for k in range(2):
        value = jnp.sum(jnp.where((spots < 64) == (k == 0), scales, 0.0), 1, keepdims=True)
        line = jnp.where(spots == 11 + k + 2 * at_ref[0], value, line)
    out_ref[0:1, at : at + 128] = line
    out_ref[1:2, at : at + 128] = jnp.zeros_like(line)


def column_stats(at_c, row_new, old, tail, tables_sum, scales, gradients, decay):
    n = gradients[1].shape[0]
    columns = sum(g.size // n for g in gradients)
    return pl.pallas_call(
        functools.partial(column_stats_kernel, decay=decay),
        out_shape=[
            jax.ShapeDtypeStruct((2, columns + 128), full_type),
            jax.ShapeDtypeStruct((8, n), full_type),
        ],
        in_specs=[pl.BlockSpec(memory_space=pltpu.SMEM)]
        + [pl.BlockSpec(memory_space=pltpu.VMEM)] * (5 + len(gradients)),
        compiler_params=pltpu.CompilerParams(vmem_limit_bytes=62 * 2**20),
        cost_estimate=cost("column_stats"),
        name="column_stats",
    )(at_c[None], row_new, old, tail, tables_sum, scales, *gradients)


def spot_of(line, k):
    spots = lax.broadcasted_iota(jnp.int32, line.shape, 1)
    return jnp.sum(jnp.where(spots == k, line, 0.0), 1, keepdims=True)


def finish_kernel(
    flat_ref, old_ref, scale_ref, col_ref, part_ref, own_ref, second_ref, step_ref, *, decay, width, starts
):
    columns = old_ref.shape[1]
    line = flat_ref[0:1, columns:]
    new = decay * old_ref[...] + (1.0 - decay) * (flat_ref[0:1, :columns] / width)
    col_ref[...] = new
    ratio = flat_ref[1:2, :columns] / new
    spots = lax.broadcasted_iota(jnp.int32, (1, 128), 1)
    scales = (spots >= 11) & (spots < 15)
    gradient = jnp.where(scales, line, 0.0)
    second = decay * scale_ref[...] + (1.0 - decay) * (gradient * gradient + eps_one)
    step = gradient * lax.rsqrt(second)
    second_ref[...] = second
    step_ref[...] = step
    out = jnp.where(spots == 7, jnp.sum(step * step, 1, keepdims=True), 0.0)
    for k in range(6):
        value = jnp.sum(ratio[:, starts[k] : starts[k + 1]], 1, keepdims=True) * (spot_of(line, k) / width)
        if k == 5:
            own_ref[...] = jnp.where(spots == 5, value, 0.0)
        else:
            out = jnp.where(spots == k, value, out)
    part_ref[...] = out


def finish(flat, col_old, scale_line, decay, width, starts):
    return pl.pallas_call(
        functools.partial(finish_kernel, decay=decay, width=width, starts=starts),
        out_shape=[jax.ShapeDtypeStruct(col_old.shape, full_type)]
        + [jax.ShapeDtypeStruct((1, 128), full_type)] * 4,
        compiler_params=pltpu.CompilerParams(vmem_limit_bytes=62 * 2**20),
        cost_estimate=cost("finish"),
        name="finish",
    )(flat, col_old, scale_line)


def renew_kernel(
    line_ref, part_ref, own_ref, early_ref, rows_ref, col_ref, ada_col_ref,
    qkv_g, proj_g, one_g, two_g, head_g, ada_g, step_ref, scale_step_ref,
    qkv_ref, proj_ref, one_ref, two_ref, head_ref, ada_ref, tab_ref, scale_ref,
    qkv_out, proj_out, one_out, two_out, head_out, ada_out, tab_out, scale_out, proj_turned, two_turned,
    *, width, entries, starts
):
    n = one_g.shape[0]
    line, part = line_ref[...], part_ref[...]

    def factor(k):
        step = spot_of(own_ref[...], 5) if k == 5 else spot_of(line, 10) if k == 6 else spot_of(part, k)
        weight = spot_of(early_ref[...], 21) if k == 7 else spot_of(line, {5: 8, 6: 9}.get(k, 16 + k))
        ratio = jnp.sqrt(step / entries[k]) / clip_rms
        spread = jnp.maximum(eps_two, jnp.sqrt(weight / entries[k]))
        return rate_step * spread / jnp.maximum(1.0, ratio)

    def row(k):
        rows = jnp.concatenate([rows_ref[k : k + 1, :], jnp.zeros((127, n), full_type)], 0)
        return rows.T[:, 0:1]

    def change(k, gradient, columns):
        mean = spot_of(line, k) / width
        return factor(k) * (gradient * lax.rsqrt(row(k) * columns / mean))

    ada_out[...] = ada_ref[...] - change(5, ada_g[...], ada_col_ref[...])
    at = pl.program_id(0)

    @pl.when(at == 0)
    def _():
        size = qkv_g.shape[2]
        for c in range(3):
            qkv_out[c] = qkv_ref[c] - change(0, qkv_g[c], col_ref[:, c * size : (c + 1) * size])

    @pl.when(at == 1)
    def _():
        gradient = proj_g[...]
        proj_turned[...] = gradient.T
        proj_out[...] = proj_ref[...] - change(1, gradient, col_ref[:, starts[1] : starts[2]]).T
        scale_out[...] = scale_ref[...] - factor(7) * scale_step_ref[...]

    @pl.when(at == 2)
    def _():
        one_out[...] = one_ref[...] - change(2, one_g[...], col_ref[:, starts[2] : starts[3]])

    @pl.when(at == 3)
    def _():
        gradient = two_g[...]
        two_turned[...] = gradient.T
        two_out[...] = two_ref[...] - change(3, gradient, col_ref[:, starts[3] : starts[4]]).T

    @pl.when(at == 4)
    def _():
        head_out[...] = head_ref[...] - change(4, head_g[...], col_ref[:, starts[4] : starts[5]])

    @pl.when(at == 5)
    def _():
        tab_out[...] = tab_ref[...] - factor(6) * step_ref[...]


def renew(lines, rows, columns, grads, steps, olds, width, entries, starts):
    n, tile = grads[2].shape[0], 1024
    ada = pl.BlockSpec((n, tile), lambda i: (0, i))
    first = starts[5] // tile

    def wholes(arrays):
        return [whole(a.shape) for a in arrays]

    outs = [a.shape for a in olds] + [olds[1].shape, olds[3].shape]
    out_specs = [ada if k == 5 else fixed(shape) for k, shape in enumerate(outs)]
    return call(
        functools.partial(renew_kernel, width=width, entries=entries, starts=starts),
        (olds[5].shape[1] // tile,),
        wholes(lines)
        + [whole(rows.shape), whole(columns.shape), pl.BlockSpec((1, tile), lambda i: (0, first + i))]
        + wholes(grads[:5])
        + [ada]
        + wholes(steps)
        + wholes(olds[:5])
        + [ada]
        + wholes(olds[6:]),
        out_specs,
        [(shape, full_type) for shape in outs],
        [],
        "renew",
    )(*lines, rows, columns, columns, *grads, *steps, *olds)


def head_lanes(shape):
    return lax.broadcasted_iota(jnp.int32, shape, len(shape) - 1) < 64


def per_head(values, first):
    left = jnp.sum(jnp.where(first, values, 0.0), -1, keepdims=True)
    right = jnp.sum(jnp.where(first, 0.0, values), -1, keepdims=True)
    return jnp.where(first, left, right)


def attend_kernel(
    q_ref, k_ref, v_ref, gain_ref, col_ref, row_ref, proj_ref,
    mix_ref, lse_ref, top_ref, bottom_ref, q_s, k_s, v_s, bias_s, sum_s
):
    length = q_ref.shape[0]
    tile = length // 2
    first = head_lanes((length, 128))
    query = q_ref[...]
    key = k_ref[...]
    q_s[...] = low(
        query * (lax.rsqrt(per_head(query * query, first) / 64.0 + eps_norm) * gain_ref[...])
    )
    k_s[...] = low(key * (lax.rsqrt(per_head(key * key, first) / 64.0 + eps_norm) * 0.125))
    v_s[...] = low(v_ref[...])
    first_t = head_lanes((tile, 128))

    @pl.when(pl.program_id(0) == 0)
    def _():
        ck = row_ref[2:3, :]
        for i in range(2):
            rows = slice(i * tile, (i + 1) * tile)
            shape = (tile, length)
            here = lax.broadcasted_iota(jnp.int32, shape, 1) - lax.broadcasted_iota(jnp.int32, shape, 0)
            keep = ((ck <= col_ref[rows, 0:1]) & (ck >= col_ref[rows, 1:2])) | (here == i * tile)
            bias_s[rows, :] = jnp.where(keep, 0.0, -1e30)
        sum_s[...] = jnp.zeros_like(sum_s)

    for i, out_ref in enumerate((top_ref, bottom_ref)):
        rows = slice(i * tile, (i + 1) * tile)
        query_t = q_s[rows, :]
        mixed, logs = [], []
        for head in range(2):
            chosen = first_t if head == 0 else ~first_t
            scores = dot_nt(jnp.where(chosen, query_t, jnp.zeros_like(query_t)), k_s[...]) + bias_s[rows, :]
            peak = jnp.max(scores, -1, keepdims=True)
            exponent = jnp.exp(scores - peak)
            total = jnp.sum(exponent, -1, keepdims=True)
            mixed.append(dot_nn(low(exponent * (1.0 / total)), v_s[...]))
            logs.append(peak + jnp.log(total))
        mixed = low(jnp.where(first_t, mixed[0], mixed[1]))
        mix_ref[rows, :] = mixed
        turned = jnp.where(first_t, logs[0], logs[1]).T
        lse_ref[0, 0:1, rows] = turned[0:1, :]
        lse_ref[0, 1:2, rows] = turned[64:65, :]
        part = sum_s[rows, :] + dot_nt(mixed, proj_ref[...])
        sum_s[rows, :] = part

        @pl.when(pl.program_id(0) == pl.num_programs(0) - 1)
        def _():
            out_ref[...] = low(part)


def attend(qkv, gain, cols, rows, proj):
    length = qkv.shape[0]
    pairs = qkv.shape[1] // 384
    width = proj.shape[0]
    block = pl.BlockSpec((length, 128), lambda p: (0, p))
    return call(
        attend_kernel,
        (pairs,),
        [
            block,
            pl.BlockSpec((length, 128), lambda p: (0, pairs + p)),
            pl.BlockSpec((length, 128), lambda p: (0, 2 * pairs + p)),
            pl.BlockSpec((1, 128), lambda p: (0, p)),
            whole((length, 128)),
            whole((8, length)),
            pl.BlockSpec((width, 128), lambda p: (0, p)),
        ],
        [block, pl.BlockSpec((1, 2, length), lambda p: (p, 0, 0))] + [fixed((length // 2, width))] * 2,
        [((length, 128 * pairs), low_type), ((pairs, 2, length), full_type)]
        + [((length // 2, width), low_type)] * 2,
        [pltpu.VMEM((length, 128), low_type)] * 3
        + [pltpu.VMEM((length, length), full_type), pltpu.VMEM((length, width), full_type)],
        "attend",
    )(qkv, qkv, qkv, gain, cols, rows, proj)


def attend_back_kernel(
    q_ref, k_ref, v_ref, gain_ref, col_ref, line_ref, lse_ref, pa_ref, pb_ref, pc_ref, pd_ref,
    proj_ref, wq_ref, wk_ref, wv_ref, row_ref, d_ref, ds_ref, top_ref, bottom_ref,
    q_s, k_s, v_s, dm_ref, dqa, dka, dva, bias_s, sum_s
):
    length = q_ref.shape[0]
    first = head_lanes((length, 128))
    query = q_ref[...]
    key = k_ref[...]
    gain = gain_ref[...]
    q_n = lax.rsqrt(per_head(query * query, first) / 64.0 + eps_norm)
    k_n = lax.rsqrt(per_head(key * key, first) / 64.0 + eps_norm)
    q_s[...] = low(query * (q_n * gain))
    k_s[...] = low(key * (k_n * 0.125))
    v_s[...] = low(v_ref[...])
    quarter = length // 4
    for k, ref in enumerate((pa_ref, pb_ref, pc_ref, pd_ref)):
        rows = slice(k * quarter, (k + 1) * quarter)
        dm_ref[rows, :] = low(dot_nn(ref[...], proj_ref[...]))

    @pl.when(pl.program_id(0) == 0)
    def _():
        sum_s[...] = jnp.zeros_like(sum_s)
        for k, ref in enumerate((pa_ref, pb_ref, pc_ref, pd_ref)):
            row_ref[k * quarter : (k + 1) * quarter, :] = ref[...]

    tile = length // 2
    first_t = head_lanes((tile, 128))

    @pl.when(pl.program_id(0) == 0)
    def _():
        ck = col_ref[:, 2:3]
        for i in range(2):
            rows = slice(i * tile, (i + 1) * tile)
            shape = (length, tile)
            here = lax.broadcasted_iota(jnp.int32, shape, 0) - lax.broadcasted_iota(jnp.int32, shape, 1)
            keep = ((ck <= line_ref[0:1, rows]) & (ck >= line_ref[1:2, rows])) | (here == i * tile)
            bias_s[:, rows] = jnp.where(keep, 0.0, -1e30)

    d_keys, d_values = None, None
    for i in range(2):
        rows = slice(i * tile, (i + 1) * tile)
        query_t = q_s[rows, :]
        dmix_t = dm_ref[rows, :]
        d_query = []
        for head in range(2):
            chosen = first_t if head == 0 else ~first_t
            zero = jnp.zeros_like(query_t)
            query_h = jnp.where(chosen, query_t, zero)
            dmix_h = jnp.where(chosen, dmix_t, zero)
            scores = dot_nt(k_s[...], query_h) + bias_s[:, rows]
            attention = jnp.exp(scores - lse_ref[0, head : head + 1, rows])
            part = dot_nn(low(attention), dmix_h)
            d_values = part if d_values is None else d_values + part
            d_att = dot_nt(v_s[...], dmix_h)
            inner = jnp.sum(attention * d_att, 0, keepdims=True)
            d_scores = low(attention * (d_att - inner))
            part = dot_nn(d_scores, query_h)
            d_keys = part if d_keys is None else d_keys + part
            d_query.append(dot_tn(d_scores, k_s[...]))
        dqa[rows, :] = jnp.where(first_t, d_query[0], d_query[1])
    dka[...] = d_keys
    dva[...] = d_values
    q_hat = query * q_n
    k_hat = key * k_n
    d_query = dqa[...]
    along = d_query * q_hat
    ds_ref[0] = jnp.sum(along, 0, keepdims=True) * gain
    group = d_ref.shape[1] // 3
    start = pl.program_id(0) * 128

    def columns(c):
        return pl.ds(pl.multiple_of(start + c * group, 128), 128)

    out_q = low(gain * (d_query - q_hat * (per_head(along, first) / 64.0)) * q_n)
    d_ref[:, columns(0)] = out_q
    d_key = dka[...]
    out_k = low(
        0.125 * (d_key - k_hat * (per_head(d_key * k_hat, first) / 64.0)) * k_n
    )
    out_v = low(dva[...])
    d_ref[:, columns(1)] = out_k
    d_ref[:, columns(2)] = out_v
    half = length // 2
    for rows, out_ref in ((slice(0, half), top_ref), (slice(half, length), bottom_ref)):
        part = sum_s[rows, :] + dot_nt(out_q[rows], wq_ref[...])
        part = part + dot_nt(out_k[rows], wk_ref[...]) + dot_nt(out_v[rows], wv_ref[...])
        sum_s[rows, :] = part

        @pl.when(pl.program_id(0) == pl.num_programs(0) - 1)
        def _():
            out_ref[...] = low(part)


def attend_back(qkv, gain, cols, rows, lse, pieces, proj, w):
    length = qkv.shape[0]
    pairs = qkv.shape[1] // 384
    width = proj.shape[0]

    def part(rows, number):
        return pl.BlockSpec((rows, 128), lambda p: (0, number * pairs + p))

    return call(
        attend_back_kernel,
        (pairs,),
        [
            part(length, 0),
            part(length, 1),
            part(length, 2),
            pl.BlockSpec((1, 128), lambda p: (0, p)),
            whole((length, 128)),
            whole((8, length)),
            pl.BlockSpec((1, 2, length), lambda p: (p, 0, 0)),
        ]
        + [whole(pieces[0].shape)] * 4
        + [part(width, 0), part(width, 0), part(width, 1), part(width, 2)],
        [
            fixed((length, width)),
            fixed((length, 384 * pairs)),
            pl.BlockSpec((1, 1, 128), lambda p: (p, 0, 0)),
            fixed((length // 2, width)),
            fixed((length // 2, width)),
        ],
        [
            ((length, width), low_type),
            ((length, 384 * pairs), low_type),
            ((pairs, 1, 128), full_type),
            ((length // 2, width), low_type),
            ((length // 2, width), low_type),
        ],
        [pltpu.VMEM((length, 128), low_type)] * 4
        + [pltpu.VMEM((length, 128), full_type)] * 3
        + [pltpu.VMEM((length, length), full_type), pltpu.VMEM((length, width), full_type)],
        "attend_back",
    )(qkv, qkv, qkv, gain, cols, rows, lse, *pieces, proj, w, w, w)


def body(
    vq_in, codes, segment, live, labels, level_weight, qkv_w, proj_w, fc1_w, fc2_w, head_w, ada_w,
    tables, head_scale, d_stats, qkv_stat, proj_stat, fc1_stat, fc2_stat, head_stat, ada_stat,
    tables_v, scale_v,
):
    g_count = lax.axis_size("g")
    dp_count = g_count * lax.axis_size("c")
    mp_count = lax.axis_size("h") * lax.axis_size("l")
    at_c, at_h, at_l = lax.axis_index("c"), lax.axis_index("h"), lax.axis_index("l")
    row_count, seq_len, code_dim = vq_in.shape
    item_count = labels.shape[1]
    level_count = level_weight.shape[0]
    slice_width = tables.shape[1]
    width = slice_width * dp_count
    half, quarter = seq_len // 2, seq_len // 4
    table_rows = tables.shape[0]
    lead = code_dim + level_count
    per_row = row_count * item_count
    note_rows = -(-(2 * per_row + 3) // slice_width)
    lead_pad = -(-(lead + note_rows) // 16) * 16

    def halves(a):
        n = a.shape[-1] // 2
        lower, upper = low(a[..., :n]), low(a[..., n:])
        return jnp.where(at_c == 0, lower, upper), jnp.where(at_c == 0, upper, lower)

    first_mine, first_other = halves(jnp.concatenate([qkv_w, proj_w.T[None]], 0))
    first_near = ordered(at_c, first_mine, over_c(first_other), 1)

    place, weight, weight_here = row_layout(level_weight, segment, live)
    weight_here = weight_here[0, 0]

    per_row = row_count * item_count
    note_rows = -(-(2 * per_row + 3) // slice_width)
    lead_pad = -(-(lead + note_rows) // 16) * 16
    tables_low = low(tables)
    label_flat = labels.reshape(-1)
    digits = jnp.stack([weight_here // 4096, (weight_here // 64) % 64, weight_here % 64])
    note = jnp.concatenate([label_flat // 32, label_flat % 32, digits])
    note = jnp.pad(low(note), (0, (lead_pad - lead) * slice_width - note.shape[0]))
    note = note.reshape(lead_pad - lead, slice_width)
    packed = tie(jnp.concatenate([tables_low[:lead], note], 0), first_near)
    gathered, first_far = lax.optimization_barrier(
        (lax.all_gather(packed, DP, axis=0), over_h(first_near))
    )
    lead_table = jnp.transpose(gathered, (1, 0, 2)).reshape(lead_pad, width)
    notes = gathered[:, lead : lead + note_rows].reshape(dp_count, -1).astype(jnp.int32)
    labels_all = (notes[:, :per_row] * 32 + notes[:, per_row : 2 * per_row]).reshape(-1)
    weight_sum = full(
        jnp.sum(
            notes[:, 2 * per_row] * 4096
            + notes[:, 2 * per_row + 1] * 64
            + notes[:, 2 * per_row + 2]
        )
    )

    class_hot = (
        labels_all[:, None] + lead == jnp.arange(table_rows, dtype=jnp.int32)[None, :]
    )
    class_vec = dot_nn(low(class_hot), tables_low)
    sigma = jax.nn.sigmoid(class_vec)
    activated = low(class_vec * sigma)
    act_pairs = activated.reshape(g_count, 2, per_row, slice_width)
    act_mine = jnp.where(at_h == 0, act_pairs[:, 0], act_pairs[:, 1]).reshape(-1, slice_width)
    ada_low = low(ada_w)
    mod_part = dot_nn(act_mine, ada_low)
    mod_half = ada_w.shape[1] // 2
    left, right = mod_part[:, :mod_half], mod_part[:, mod_half:]
    mod_send = jnp.where(at_c == 0, right, left)
    mod_sum = jnp.where(at_c == 0, left, right) + over_c(mod_send)
    mod_first = mod_sum
    mod_sum = scatter_g(mod_sum)
    mod_items = ordered(at_c, mod_sum, over_c(mod_sum), 1).reshape(row_count, item_count, 8, width)
    mod_rows = jnp.transpose(mod_items, (0, 2, 1, 3))

    fc1_wide, fc2_wide = tie((fc1_w, fc2_w), mod_send)

    def near_rows(w):
        kept, other = halves(w)
        return ordered(at_c, kept, over_c(other), 0)

    def gathered_weight(a):
        wide = lax.all_gather(a.reshape(-1, a.shape[2]), "g", axis=0, tiled=True)
        return wide.reshape((g_count,) + a.shape)

    feed_near = jnp.concatenate([near_rows(fc1_wide), near_rows(fc2_wide.T)], 1)
    qkv_piece = ordered(at_h, first_near[None], first_far[None], 0)

    def window(*values):
        return lax.optimization_barrier(values)

    def far_part(r):
        return low(full(top[r][quarter:]) + full(moved[r][quarter:]))

    def turn(norm, kernel, filler=lambda: None, beside=None, keep=lambda done: None):
        moved[1] = over_c(bottom[1])
        first, moved[1] = window(norm(0, (top[0], moved[0], across[0])), moved[1])
        across[1] = over_l(far_part(1))
        pieces = [[first, over_l(first), over_c(first), None], None]
        done, across[1], pieces[0][2] = window(filler(), across[1], pieces[0][2])
        keep(done)
        second, pieces[0][1] = window(norm(1, (top[1], moved[1], across[1])), pieces[0][1])
        pieces[1] = [second, over_l(second), over_c(second), None]
        pieces[0][3] = over_c(pieces[0][1])
        kernel_out, pieces[1], beside = window(kernel(0, pieces[0]), pieces[1][:3], beside)
        return pieces, kernel_out, done, beside

    def launch():
        moved[0] = over_c(bottom[0])
        sent = far_part(0)
        across[0] = over_l(sent)
        return sent

    head_gain = tie(head_scale, gathered)
    gain_own = jnp.where(at_c == 0, head_gain[:2], head_gain[2:])
    gains = jnp.exp(ordered(at_h, gain_own, over_h(gain_own), 0)) / 8.0
    gain_row = jnp.repeat(gains, 64)[None, :]

    info = full(jnp.stack([codes, place, live, weight], 1))
    info_other, vq_other = over_c(info), over_c(vq_in)
    at = jnp.stack([full(at_c == at_h).astype(jnp.int32), at_c, at_l])
    arranged, olds, qkv_pieces, feed_far = window(
        arrange(at, tie(info, mod_first), info_other, vq_in, vq_other, lead_pad),
        old_stats(*tie((qkv_w, proj_w, fc1_w, fc2_w, head_w, ada_w, tables, head_scale[None]), mod_first)),
        [qkv_piece] + [over_g(qkv_piece, k) for k in range(1, 4)] if g_count == 4 else [],
        over_h(feed_near),
    )
    feats, hot, cols, rows = (arranged[k::4] for k in range(4))
    head_near = near_rows(tie(head_w, olds))
    feats_first = tie(feats[0], gain_row)
    inputs_one, qkv_rows, mixed_rows, lse_rows, top, bottom, stream_zero = ([None] * 2 for _ in range(7))
    if g_count == 4:
        inputs_one[0], qkv_rows[0], stream_zero[0], qkv_full, proj_full = enter_first(
            lax.axis_index("g"), feats_first, lead_table, hot[0], mod_rows[0], qkv_pieces
        )
    else:
        wide_piece = lax.all_gather(qkv_piece, "g", axis=0)
        wide_piece = jnp.transpose(wide_piece, (0, 3, 2, 1, 4)).reshape(width, -1)
        qkv_full, proj_full = wide_piece[:, :768], wide_piece[:, 768:]
        inputs_one[0], qkv_rows[0], stream_zero[0] = enter(feats_first, lead_table, hot[0], mod_rows[0], qkv_full)
    feed_full = gathered_weight(ordered(at_h, feed_near[None], feed_far[None], 0))

    moved, across = [None] * 2, [None] * 2

    def attention(r, given):
        mixed_rows[r], lse_rows[r], top[r], bottom[r] = attend(
            given, gain_row, cols[r], rows[r], proj_full
        )
        return top[r], bottom[r]

    (top[0], bottom[0]), head_far = window(attention(0, qkv_rows[0]), over_h(head_near))
    held = [gathered_weight(ordered(at_h, head_near[None], head_far[None], 0))]
    moved[0] = over_c(bottom[0])
    (inputs_one[1], qkv_rows[1], stream_zero[1]), moved[0] = window(
        enter(tie(feats[1], bottom[0]), lead_table, hot[1], mod_rows[1], qkv_full), moved[0]
    )
    sent = far_part(0)
    across[0] = over_l(sent)
    (top[1], bottom[1]), across[0] = window(attention(1, tie(qkv_rows[1], sent)), across[0])

    branch_one, stream_one, acts, slopes, inputs_two = ([None] * 2 for _ in range(5))

    def norm_two(r, parts):
        branch_one[r], stream_one[r], given = onward(parts, stream_zero[r], hot[r], mod_rows[r], (2, 3, 4))
        return given

    def forward(r, pieces):
        inputs_two[r], acts[r], slopes[r], top[r], bottom[r] = feed(pieces, feed_full)
        return top[r], bottom[r]

    pieces_two, (top[0], bottom[0]), _, _ = turn(norm_two, forward)
    pieces_two[1].append(over_c(pieces_two[1][1]))
    sent = launch()
    (top[1], bottom[1]), across[0] = window(
        forward(1, [tie(pieces_two[1][0], sent)] + pieces_two[1][1:]), across[0]
    )

    block_codes = head_w.shape[1]
    half_codes = block_codes // 2
    column = jnp.arange(2 * half_codes, dtype=jnp.int32)
    block_here = (column // half_codes) * 2 + at_l
    column_code = full(block_here * block_codes + at_c * half_codes + column % half_codes)[None, :]
    branch_two, stream_two, logits, stats, d_logits, losses, others, inputs_out = ([None] * 2 for _ in range(8))

    def norm_out(r, parts):
        branch_two[r], stream_two[r], given = onward(parts, stream_one[r], hot[r], mod_rows[r], (5, 6, 7))
        return given

    def score(r, pieces):
        inputs_out[r], logits[r], stats[r] = head(pieces, held[0], cols[r], column_code)
        return stats[r]

    def compare(r):
        return [over_c(stats[r]), over_l(stats[r]), over_cl(stats[r])]

    def score_back(r):
        lines, losses[r] = merge(weight_sum, stats[r], *others[r], rows[r])
        d_logits[r], top[r], bottom[r] = head_back(logits[r], held[0], cols[r], column_code, lines)
        return top[r], bottom[r]

    pieces_out, stats[0], _, _ = turn(
        norm_out, score, lambda: held[0], keep=lambda done: held.__setitem__(0, done)
    )
    pieces_out[1].append(over_c(pieces_out[1][1]))
    stats[1], others[0] = window(score(1, pieces_out[1]), compare(0))
    (top[0], bottom[0]), others[1] = window(score_back(0), compare(1))
    sent = launch()
    logits[1] = tie(logits[1], sent)
    (top[1], bottom[1]), across[0] = window(score_back(1), across[0])

    def reduced(a):
        shape = a.shape[1:]
        a = lax.psum_scatter(a.reshape(-1, shape[2]), "g", scatter_dimension=0, tiled=True)
        return a.reshape(shape)

    def theirs(a):
        return jnp.where(at_h == 0, a[1], a[0])

    def settle(a, other):
        a = full(jnp.where(at_h == 0, a[0], a[1])) + full(other)
        rows = a.shape[0] // 2
        kept = jnp.where(at_c == 0, a[:rows], a[rows:])
        return kept, over_c(jnp.where(at_c == 0, a[rows:], a[:rows]))

    d_two, d_one, items_out, items_two, d_hidden, d_branch_two, d_branch_one = ([None] * 2 for _ in range(7))

    def back_out(r, parts):
        d_two[r], given, items_out[r] = back(
            parts, stream_two[r], hot[r], mod_rows[r], (7, 5), None, branch_two[r], None
        )
        return given

    def backward(r, pieces):
        d_branch_two[r], d_hidden[r], top[r], bottom[r] = feed_back(pieces, slopes[r], feed_full)
        return top[r], bottom[r]

    pieces_d_two, (top[0], bottom[0]), head_part, _ = turn(
        back_out, backward, lambda: head_grad_of(inputs_out, d_logits, g_count)
    )
    head_sum = reduced(head_part)
    pieces_d_two[1].append(over_c(pieces_d_two[1][1]))
    sent = launch()
    (top[1], bottom[1]), across[0], head_sum = window(
        backward(1, [tie(pieces_d_two[1][0], sent)] + pieces_d_two[1][1:]), across[0], head_sum
    )

    d_qkv, scale_rows = ([None] * 2 for _ in range(2))

    def back_two(r, parts):
        d_one[r], given, items_two[r] = back(
            parts, stream_one[r], hot[r], mod_rows[r], (4, 2), d_two[r], branch_one[r], None
        )
        return given

    def attention_back(r, pieces):
        d_branch_one[r], d_qkv[r], scale_rows[r], top[r], bottom[r] = attend_back(
            qkv_rows[r], gain_row, cols[r], rows[r], lse_rows[r], pieces, proj_full, qkv_full
        )
        return top[r], bottom[r]

    pieces_d_one, (top[0], bottom[0]), feed_part, head_other = turn(
        back_two,
        attention_back,
        lambda: feed_grad_of(inputs_two, d_hidden, d_branch_two, acts, g_count),
        over_h(theirs(head_sum)),
    )
    feed_sum = reduced(feed_part)
    pieces_d_one[1].append(over_c(pieces_d_one[1][1]))
    sent = launch()
    leaving = theirs(feed_sum)
    (top[1], bottom[1]), across[0], feed_other = window(
        attention_back(1, [tie(pieces_d_one[1][0], sent, leaving)] + pieces_d_one[1][1:]), across[0], over_h(leaving)
    )
    moved[1] = over_c(bottom[1])
    items_one, lead_parts = ([None] * 2 for _ in range(2))

    def back_one(r, parts):
        items_one[r], lead_parts[r] = back(
            parts, stream_zero[r], hot[r], mod_rows[r], (1,), d_one[r], None, feats[r]
        )
        return items_one[r]

    items_one[0], moved[1] = window(back_one(0, (top[0], moved[0], across[0])), moved[1])
    sent = far_part(1)
    across[1] = over_l(sent)
    first_part = first_grad_of(inputs_one, tie(d_qkv, sent), d_branch_one, mixed_rows, g_count)
    first_part, across[1] = window(first_part, across[1])
    first_sum = reduced(first_part)
    back_one(1, (top[1], moved[1], across[1]))
    lead_part = lead_parts[0] + lead_parts[1]

    def flat_items(items, number):
        return jnp.concatenate([items[r][number, :item_count] for r in range(2)], 0)

    d_items = jnp.concatenate(
        [flat_items(items_one, 0), flat_items(items_one, 1), flat_items(items_two, 2)]
        + [flat_items(items_two, 0), flat_items(items_two, 1), flat_items(items_out, 2)]
        + [flat_items(items_out, 0), flat_items(items_out, 1)],
        1,
    )
    left, right = d_items[:, :mod_half], d_items[:, mod_half:]
    d_items = jnp.where(at_c == 0, left, right) + over_c(jnp.where(at_c == 0, right, left))
    d_items = low(d_items + over_l(d_items))
    d_items, first_sum = window(ordered(at_h, d_items, over_h(d_items), 0), first_sum)
    leaving = theirs(first_sum)
    d_items = gather_g(tie(d_items, leaving))
    d_items = ordered(at_c, d_items, over_c(d_items), 1)
    ada_grad = dot_tn(activated, d_items)
    d_act_vec = dot_nt(d_items, ada_low)
    d_class = d_act_vec * (sigma * (1.0 + class_vec * (1.0 - sigma)))
    lead_part = jnp.transpose(lead_part.reshape(lead_pad, dp_count, slice_width), (1, 0, 2))
    lead_grad = jnp.sum(lax.all_to_all(lead_part, DP, 0, 0, tiled=True).reshape(dp_count, lead_pad, slice_width), 0)
    lead_grad = lead_grad + over_l(lead_grad)
    lead_grad = lead_grad + over_h(lead_grad)
    tables_grad = dot_tn(full(class_hot), d_class, highest)
    tables_grad = tables_grad + jnp.pad(lead_grad[:lead], ((0, table_rows - lead), (0, 0)))

    head_grad = ordered(at_c, *settle(tie(head_sum, items_one[0]), head_other), 1)
    kept, moved_half = settle(feed_sum, feed_other)
    n = kept.shape[1] // 2
    fc1_grad = ordered(at_c, kept[:, :n], moved_half[:, :n], 1)
    fc2_grad = ordered(at_c, kept[:, n:], moved_half[:, n:], 1)
    ada_grad, tables_grad, first_other = window(ada_grad, tables_grad, over_h(leaving))
    kept, moved_half = settle(first_sum, first_other)
    first_halves = jnp.stack([kept, moved_half])
    first_halves = jnp.where(at_c == 0, first_halves, first_halves[::-1])
    first_halves = jnp.transpose(first_halves.reshape(2, slice_width, 4, -1), (2, 1, 0, 3))
    first_halves = first_halves.reshape(4, slice_width, -1)
    qkv_grad, proj_grad = first_halves[:3], first_halves[3]

    decay = 1.0 - STEP ** (-0.8)
    grads = [qkv_grad, proj_grad, fc1_grad, fc2_grad, head_grad, ada_grad]
    wide = [g.size // slice_width * (mp_count if k < 5 else 1) for k, g in enumerate(grads)]
    sizes = [g.size // slice_width for g in grads]
    starts = [sum(sizes[:k]) for k in range(7)]

    def over_mp(a):
        a = a + over_l(a)
        return a + over_h(a)

    spots = jnp.arange(128, dtype=jnp.int32)[None, :]
    early_line = over_mp(tie(olds[:1] + jnp.where(spots == 22, losses[0] + losses[1], 0.0), lead_part))
    tail = early_line + olds[1:]
    rows_all = over_mp(row_stats(*grads[:5]))
    wide_column = jnp.array(wide[:5], full_type)[:, None]
    row_new = decay * d_stats[:5] + (1.0 - decay) * (rows_all[:5] / wide_column)
    tables_v_new = decay * tables_v + (1.0 - decay) * (tables_grad * tables_grad + eps_one)
    tables_step = tables_grad * lax.rsqrt(tables_v_new)
    tables_sum = jnp.sum(tables_step * tables_step)[None, None]
    scales = tie(scale_rows[0] + scale_rows[1], lead_part)
    scales = jnp.where(at_h == 0, scales[0], scales[1]) + over_h(
        jnp.where(at_h == 0, scales[1], scales[0])
    )
    flat, ada_row = column_stats(at_c, row_new, d_stats[5:6], tail, tables_sum, scales, grads, decay)
    d_stats_new = jnp.concatenate([row_new, ada_row[:1]], 0)
    if g_count == 4:
        flat = flat + over_c(flat)
        flat = flat + over_g(flat, 1)
        flat = flat + over_g(flat, 2)
    else:
        flat = lax.psum(flat, DP)
    col_old = jnp.concatenate(
        [qkv_stat.reshape(-1), proj_stat, fc1_stat, fc2_stat, head_stat, ada_stat]
    )[None, :]
    heads = head_scale.shape[0]
    scale_line = jnp.pad(scale_v, (11, 128 - 11 - heads), constant_values=1.0)[None, :]
    col_line, part_line, own_line, second_line, scale_step = finish(
        flat, col_old, scale_line, decay, width, starts
    )
    col_new = [col_line[0, starts[k] : starts[k + 1]] for k in range(6)]
    line = flat[:1, starts[6] :]
    scale_grad = line[0, 11 : 11 + heads]
    loss_sum = line[0, 22]
    scale_v_new = second_line[0, 11 : 11 + heads]
    entries = [width * wide[k] for k in range(6)] + [table_rows * width, heads * mp_count]
    news = renew(
        (line, over_mp(part_line), own_line, early_line),
        d_stats_new,
        col_line,
        grads,
        (tables_step, scale_step),
        (
            qkv_w, proj_w, fc1_w, fc2_w, head_w, ada_w, tables,
            jnp.pad(head_scale, (11, 128 - 11 - heads))[None, :],
        ),
        width,
        entries,
        starts,
    )
    return (
        loss_sum,
        weight_sum,
        qkv_grad,
        news[8],
        fc1_grad,
        news[9],
        head_grad,
        ada_grad,
        tables_grad,
        scale_grad,
        d_stats_new,
        col_new[0].reshape(3, -1),
        col_new[1],
        col_new[2],
        col_new[3],
        col_new[4],
        col_new[5],
        tables_v_new,
        scale_v_new,
        news[0],
        news[1],
        news[2],
        news[3],
        news[4],
        news[5],
        news[6],
        news[7][0, 11 : 11 + heads],
    )


def solution(mesh):
    inner = Mesh(
        mesh.devices.reshape(mesh.shape["dp"] // 2, 2, mesh.shape["mp"] // 2, 2),
        ("g", "c", "h", "l"),
    )
    return jax.shard_map(
        body,
        mesh=inner,
        in_specs=(
            P(DP, None, None),
            P(DP, None),
            P(DP, None),
            P(DP, None),
            P(DP, None),
            P(),
            P(None, DP, MP),
            P(MP, DP),
            P(DP, MP),
            P(MP, DP),
            P(DP, MP),
            P(DP, None),
            P(None, DP),
            P(MP),
            P(None, DP),
            P(None, MP),
            P(MP),
            P(MP),
            P(MP),
            P(MP),
            P(),
            P(None, DP),
            P(MP),
        ),
        out_specs=(
            P(),
            P(),
            P(None, DP, MP),
            P(MP, DP),
            P(DP, MP),
            P(MP, DP),
            P(DP, MP),
            P(DP, None),
            P(None, DP),
            P(MP),
            P(None, DP),
            P(None, MP),
            P(MP),
            P(MP),
            P(MP),
            P(MP),
            P(),
            P(None, DP),
            P(MP),
            P(None, DP, MP),
            P(MP, DP),
            P(DP, MP),
            P(MP, DP),
            P(DP, MP),
            P(DP, None),
            P(None, DP),
            P(MP),
        ),
        check_vma=False,
    )
```

```python
import functools
import math

import jax
import jax.numpy as jnp
from jax import lax
from jax.experimental import pallas as pl
from jax.experimental.pallas import tpu as pltpu
from jax.sharding import Mesh, PartitionSpec as P

STEP = 8
level_starts = (1, 5, 14, 30, 55, 91, 155, 255, 424)
eps_norm = 1e-06
eps_one = 1e-30
eps_two = 0.001
rate_step = 0.3
clip_rms = 1.0
low_type = jnp.bfloat16
full_type = jnp.float32
high = lax.Precision.HIGH
highest = lax.Precision.HIGHEST
swap_pairs = ((0, 1), (1, 0))
busy_us = {
    "row_layout": 2, "enter": 5, "enter_first": 6, "attend": 11, "onward": 2, "feed": 5, "head": 6, "merge": 2,
    "head_back": 5, "back": 5, "feed_back": 7, "attend_back": 16, "old_stats": 4, "row_stats": 3,
    "column_stats": 5, "finish": 2, "head_grad": 6, "feed_grad": 12, "first_grad": 6,
    "renew": 8, "arrange": 4,
}
DP = ("g", "c")
MP = ("h", "l")


def cost(name):
    return pl.CostEstimate(flops=busy_us[name] * 10**9, transcendentals=0, bytes_accessed=busy_us[name] * 10**6)


def low(a):
    return a.astype(low_type)


def full(a):
    return a.astype(full_type)


def dot_nn(a, b, precision=None):
    return jnp.dot(a, b, preferred_element_type=full_type, precision=precision)


def dot_nt(a, b, precision=None):
    return lax.dot_general(
        a, b, (((1,), (1,)), ((), ())), preferred_element_type=full_type, precision=precision
    )


def dot_tn(a, b, precision=None):
    return lax.dot_general(
        a, b, (((0,), (0,)), ((), ())), preferred_element_type=full_type, precision=precision
    )


def over_c(a):
    return lax.ppermute(a, "c", swap_pairs)


def over_l(a):
    return lax.ppermute(a, "l", swap_pairs)


def over_h(a):
    return lax.ppermute(a, "h", swap_pairs)


def over_cl(a):
    return lax.ppermute(a, ("c", "l"), [(i, i ^ 3) for i in range(4)])


def over_g(a, k):
    return lax.ppermute(a, "g", [(i, i ^ k) for i in range(lax.axis_size("g"))])


def ordered(flag, mine, other, axis):
    return jnp.where(
        flag == 0,
        jnp.concatenate([mine, other], axis),
        jnp.concatenate([other, mine], axis),
    )


def gather_g(a):
    count = lax.axis_size("g")
    if count != 4:
        return lax.all_gather(a, "g", axis=0, tiled=True)
    here = lax.axis_index("g")
    out = jnp.zeros((4,) + a.shape, a.dtype)
    for k in range(4):
        piece = a if k == 0 else over_g(a, k)
        out = lax.dynamic_update_index_in_dim(out, piece, here ^ k, 0)
    return out.reshape((4 * a.shape[0],) + a.shape[1:])


def scatter_g(a):
    count = lax.axis_size("g")
    if count != 4:
        return full(lax.psum_scatter(a, "g", scatter_dimension=0, tiled=True))
    here = lax.axis_index("g")
    blocks = a.reshape((4, a.shape[0] // 4) + a.shape[1:])
    total = full(lax.dynamic_index_in_dim(blocks, here, 0, False))
    for k in range(1, 4):
        total = total + full(over_g(lax.dynamic_index_in_dim(blocks, here ^ k, 0, False), k))
    return total


def tie(a, *others):
    return lax.optimization_barrier((a,) + others)[0]


def centre(values):
    centered = values - jnp.mean(values, -1, keepdims=True)
    scale = lax.rsqrt(jnp.mean(centered * centered, -1, keepdims=True) + eps_norm)
    return centered * scale, scale


def centre_back(normed, scale, incoming):
    return (
        incoming
        - jnp.mean(incoming, -1, keepdims=True)
        - normed * jnp.mean(incoming * normed, -1, keepdims=True)
    ) * scale


def gelu_parts(values):
    root = math.sqrt(2.0 / math.pi)
    square = values * values
    bent = jnp.tanh(values * (root + (root * 0.044715) * square))
    half = 0.5 + 0.5 * bent
    slope = half + values * (0.5 - 0.5 * (bent * bent)) * (root + (root * 3.0 * 0.044715) * square)
    return values * half, slope


def split_parts(a, count):
    parts = []
    for _ in range(count):
        parts.append(low(a))
        a = a - full(parts[-1])
    return parts


def item_parts(vectors):
    return jnp.concatenate(split_parts(vectors, 3) + [jnp.zeros(vectors.shape, low_type)], 0)


def item_sums(hot, values):
    upper, lower = split_parts(values, 2)
    return (dot_tn(hot, upper) + dot_tn(hot, lower))[:8]


def whole(shape):
    return pl.BlockSpec(shape, lambda i: (0,) * len(shape), pipeline_mode=pl.Buffered(1))


def tiled(tile, columns):
    return pl.BlockSpec((tile, columns), lambda i: (i, 0))


def call(kernel, grid, in_specs, out_specs, out_shape, scratch, name):
    return pl.pallas_call(
        kernel,
        grid=grid,
        in_specs=in_specs,
        out_specs=out_specs,
        out_shape=[jax.ShapeDtypeStruct(shape, dtype) for shape, dtype in out_shape],
        scratch_shapes=scratch,
        compiler_params=pltpu.CompilerParams(vmem_limit_bytes=62 * 2**20),
        cost_estimate=cost(name),
        name=name,
    )


def rows_kernel(lw_ref, seg_ref, live_ref, place_ref, weight_ref, sum_ref):
    seg, live = seg_ref[...], live_ref[...]
    at = lax.broadcasted_iota(jnp.int32, seg.shape, 1)
    first = jnp.zeros_like(seg)
    for item in range(1, 4):
        count = jnp.sum(full(jnp.where(seg < item, 1, 0)), 1, keepdims=True).astype(jnp.int32)
        first = jnp.where(seg == item, count, first)
    within = at - first
    level = jnp.zeros_like(seg)
    for start in level_starts:
        level = level + jnp.where(within >= start, 1, 0)
    weight = jnp.zeros_like(seg)
    for position in range(lw_ref.shape[0]):
        weight = jnp.where(level == position, lw_ref[position], weight)
    weight = weight * live
    place_ref[...] = seg * 16 + level
    weight_ref[...] = weight
    each = jnp.sum(full(weight), 1, keepdims=True)
    sum_ref[...] = jnp.sum(each, 0, keepdims=True).astype(jnp.int32)


def row_layout(level_weight, segment, live):
    shape = segment.shape
    return pl.pallas_call(
        rows_kernel,
        in_specs=[pl.BlockSpec(memory_space=pltpu.SMEM)] + [pl.BlockSpec(memory_space=pltpu.VMEM)] * 2,
        out_shape=[
            jax.ShapeDtypeStruct(shape, jnp.int32),
            jax.ShapeDtypeStruct(shape, jnp.int32),
            jax.ShapeDtypeStruct((1, 1), jnp.int32),
        ],
        compiler_params=pltpu.CompilerParams(vmem_limit_bytes=62 * 2**20),
        cost_estimate=cost("row_layout"),
        name="row_layout",
    )(level_weight, segment, live)


def arrange_kernel(at_ref, mine_ref, other_ref, vq_ref, vq_other_ref, *refs):
    quarter = mine_ref.shape[2] // 4
    cols_s, vq_s = refs[-2:]
    use_mine, at_c, at_l = at_ref[0], at_ref[1], at_ref[2]
    n = 4 * quarter
    lane = lax.broadcasted_iota(jnp.int32, (n, 128), 1)
    for r in range(2):
        feat_ref, hot_ref, col_ref, row_ref = refs[4 * r : 4 * r + 4]
        info = jnp.where(use_mine == 1, mine_ref[r], other_ref[r])
        cols_s[...] = jnp.concatenate([info, jnp.zeros((124, n), full_type)], 0).T
        vq_s[...] = jnp.where(use_mine == 1, full(vq_ref[r]), full(vq_other_ref[r]))
        cols, vqs = [], []
        for k in range(4):
            start = jnp.bitwise_xor(at_c, k // 2) * 2 + jnp.bitwise_xor(at_l, k % 2)
            rows = pl.ds(pl.multiple_of(start * quarter, quarter), quarter)
            cols.append(cols_s[rows, :])
            vqs.append(vq_s[rows, :])
        cols = jnp.concatenate(cols, 0)
        code, place, live, weight = (cols[:, k : k + 1] for k in range(4))
        segment = jnp.floor(place * (1.0 / 16.0))
        base = segment * 16.0
        key = jnp.where(live > 0.0, place, 1048576.0)
        out = jnp.zeros((n, 128), full_type)
        for k, column in enumerate((place, base, key, code, weight)):
            out = jnp.where(lane == k, column, out)
        col_ref[...] = out
        row_ref[...] = out.T[0:8, :]
        spot = lax.broadcasted_iota(jnp.int32, (n, 16), 1)
        hit = (full(spot % 4) == segment) & (spot < 12)
        hot_ref[...] = low(jnp.where(hit, 1.0, 0.0))
        code_dim, padded = vq_ref.shape[2], feat_ref.shape[1]
        spread = lax.broadcasted_iota(jnp.int32, (code_dim, padded), 0) == lax.broadcasted_iota(
            jnp.int32, (code_dim, padded), 1
        )
        feats = dot_nn(low(jnp.concatenate(vqs, 0)), low(jnp.where(spread, 1.0, 0.0)))
        level = lax.broadcasted_iota(jnp.int32, (n, padded), 1) - code_dim
        feat_ref[...] = low(feats + jnp.where(full(level) == place - base, 1.0, 0.0))


def arrange(at, mine, other, vq, vq_other, padded):
    n, code_dim = vq.shape[1:]
    shapes = [((n, padded), low_type), ((n, 16), low_type), ((n, 128), full_type), ((8, n), full_type)] * 2
    return pl.pallas_call(
        arrange_kernel,
        in_specs=[pl.BlockSpec(memory_space=pltpu.SMEM)] + [pl.BlockSpec(memory_space=pltpu.VMEM)] * 4,
        out_shape=[jax.ShapeDtypeStruct(shape, dtype) for shape, dtype in shapes],
        scratch_shapes=[pltpu.VMEM((n, 128), full_type), pltpu.VMEM((n, code_dim), full_type)],
        compiler_params=pltpu.CompilerParams(vmem_limit_bytes=62 * 2**20),
        cost_estimate=cost("arrange"),
        name="arrange",
    )(at, mine, other, vq, vq_other)


def enter_tile(feat_ref, table_ref, hot_ref, w, in_ref, qkv_ref, stream_ref, parts_s):
    stream = dot_nn(feat_ref[...], table_ref[...])

    @pl.when(pl.program_id(0) == 0)
    def _():
        stream_ref[...] = stream[: stream_ref.shape[0]]

    normed, _ = centre(stream)
    hot = hot_ref[...]
    given = low(normed * (1.0 + dot_nn(hot, parts_s[1])) + dot_nn(hot, parts_s[0]))
    in_ref[...] = given
    qkv_ref[...] = dot_nn(given, w)


def enter_parts(mod_ref, parts_s):
    parts_s[0] = item_parts(mod_ref[0])
    parts_s[1] = item_parts(mod_ref[1])


def enter_kernel(feat_ref, table_ref, hot_ref, mod_ref, w_ref, in_ref, qkv_ref, stream_ref, parts_s):
    @pl.when(pl.program_id(0) == 0)
    def _():
        enter_parts(mod_ref, parts_s)

    enter_tile(feat_ref, table_ref, hot_ref, w_ref[...], in_ref, qkv_ref, stream_ref, parts_s)


def enter(feats, table, hot, mods, w):
    n, k = feats.shape
    width, columns = w.shape
    tile = n // 2
    return call(
        enter_kernel,
        (2,),
        [tiled(tile, k), whole((k, width)), tiled(tile, 16), whole(mods.shape), whole(w.shape)],
        [tiled(tile, width), tiled(tile, columns), fixed((tile // 2, width))],
        [((n, width), low_type), ((n, columns), full_type), ((tile // 2, width), full_type)],
        [pltpu.VMEM((2, 16, width), low_type)],
        "enter",
    )(feats, table, hot, mods, w)


def enter_first_kernel(
    at_ref, feat_ref, table_ref, hot_ref, mod_ref, a_ref, b_ref, c_ref, d_ref, in_ref, qkv_ref, stream_ref,
    w_ref, p_ref, parts_s
):
    @pl.when(pl.program_id(0) == 0)
    def _():
        enter_parts(mod_ref, parts_s)
        for k, ref in enumerate((a_ref, b_ref, c_ref, d_ref)):
            rows = ref.shape[2]
            start = pl.multiple_of(jnp.bitwise_xor(at_ref[0], k) * rows, rows)
            for j in range(2):
                for c in range(3):
                    w_ref[pl.ds(start, rows), (2 * c + j) * 128 : (2 * c + j + 1) * 128] = ref[j, c]
                p_ref[pl.ds(start, rows), j * 128 : (j + 1) * 128] = ref[j, 3]

    enter_tile(feat_ref, table_ref, hot_ref, w_ref[...], in_ref, qkv_ref, stream_ref, parts_s)


def enter_first(here, feats, table, hot, mods, pieces):
    n, k = feats.shape
    width = table.shape[1]
    columns = 768
    tile = n // 2
    shape = pieces[0].shape
    return call(
        enter_first_kernel,
        (n // tile,),
        [pl.BlockSpec(memory_space=pltpu.SMEM), tiled(tile, k), whole((k, width)), tiled(tile, 16), whole(mods.shape)]
        + [whole(shape)] * 4,
        [tiled(tile, width), tiled(tile, columns), fixed((tile // 2, width))]
        + [fixed((width, columns)), fixed((width, columns // 3))],
        [((n, width), low_type), ((n, columns), full_type), ((tile // 2, width), full_type)]
        + [((width, columns), low_type), ((width, columns // 3), low_type)],
        [pltpu.VMEM((2, 16, width), low_type)],
        "enter_first",
    )(here[None], feats, table, hot, mods, *pieces)


def onward_kernel(a_ref, b_ref, c_ref, x_ref, hot_ref, mod_ref, br_ref, y_ref, in_ref, parts_s, *, picks):
    @pl.when(pl.program_id(0) == 0)
    def _():
        for k, pick in enumerate(picks):
            parts_s[k] = item_parts(mod_ref[pick])

    branch = full(a_ref[...]) + full(b_ref[...]) + full(c_ref[...])
    br_ref[...] = branch
    hot = hot_ref[...]
    stream = x_ref[...] + dot_nn(hot, parts_s[0]) * branch
    y_ref[...] = stream
    normed, _ = centre(stream)
    in_ref[...] = low(normed * (1.0 + dot_nn(hot, parts_s[2])) + dot_nn(hot, parts_s[1]))


def onward(parts, stream, hot, mods, picks):
    n, width = parts[2].shape
    tile = n
    return call(
        functools.partial(onward_kernel, picks=picks),
        (n // tile,),
        [tiled(tile, width)] * 4 + [tiled(tile, 16), whole(mods.shape)],
        [tiled(tile, width)] * 3,
        [((n, width), full_type), ((n, width), full_type), ((n, width), low_type)],
        [pltpu.VMEM((3, 16, width), low_type)],
        "onward",
    )(*parts, stream, hot, mods)


def back_kernel(*refs, gated, carried, picks):
    refs = list(refs)
    a_ref, b_ref, c_ref, x_ref, hot_ref, mod_ref = refs[:6]
    del refs[:6]
    res_ref = refs.pop(0) if carried else None
    br_ref = refs.pop(0) if gated else None
    feat_ref = None if gated else refs.pop(0)
    res_out = refs.pop(0) if gated else None
    d_ref = refs.pop(0) if gated else None
    items_ref = refs.pop(0)
    lead_ref = None if gated else refs.pop(0)
    parts_s = refs.pop(0)

    @pl.when(pl.program_id(0) == 0)
    def _():
        for k, pick in enumerate(picks):
            parts_s[k] = item_parts(mod_ref[pick])
        items_ref[...] = jnp.zeros_like(items_ref)
        if not gated:
            lead_ref[...] = jnp.zeros_like(lead_ref)

    hot = hot_ref[...]
    incoming = full(a_ref[...]) + full(b_ref[...]) + full(c_ref[...])
    normed, scale = centre(x_ref[...])
    items_ref[0] += item_sums(hot, incoming)
    items_ref[1] += item_sums(hot, incoming * normed)
    res = centre_back(normed, scale, incoming * (1.0 + dot_nn(hot, parts_s[0])))
    if carried:
        res = res + res_ref[...]
    if gated:
        res_out[...] = res
        items_ref[2] += item_sums(hot, res * br_ref[...])
        d_ref[...] = low(res * dot_nn(hot, parts_s[1]))
    else:
        upper, lower = split_parts(res, 2)
        feats = feat_ref[...]
        lead_ref[...] += dot_tn(feats, upper) + dot_tn(feats, lower)


def back(parts, stream, hot, mods, picks, carried, branch, feats):
    n, width = parts[2].shape
    tile = n
    gated, has = branch is not None, carried is not None
    extra = ([carried] if has else []) + ([branch] if gated else [feats])
    specs = [tiled(tile, width)] * 4 + [tiled(tile, 16), whole(mods.shape)]
    specs += [tiled(tile, a.shape[1]) for a in extra]
    count = 3 if gated else 2
    out_specs, out_shape = [], []
    if gated:
        out_specs += [tiled(tile, width)] * 2
        out_shape += [((n, width), full_type), ((n, width), low_type)]
    out_specs.append(fixed((count, 8, width)))
    out_shape.append(((count, 8, width), full_type))
    if not gated:
        out_specs.append(fixed((feats.shape[1], width)))
        out_shape.append(((feats.shape[1], width), full_type))
    return call(
        functools.partial(back_kernel, gated=gated, carried=has, picks=picks),
        (n // tile,),
        specs,
        out_specs,
        out_shape,
        [pltpu.VMEM((2, 16, width), low_type)],
        "back",
    )(*parts, stream, hot, mods, *extra)


def either(a_ref, b_ref, c_ref, d_ref):
    top = jnp.concatenate([a_ref[...], b_ref[...]], 0)
    return jnp.where(pl.program_id(0) == 0, top, jnp.concatenate([c_ref[...], d_ref[...]], 0))


def put(value, top_ref, bottom_ref):
    @pl.when(pl.program_id(0) == 0)
    def _():
        top_ref[...] = value

    @pl.when(pl.program_id(0) == 1)
    def _():
        bottom_ref[...] = value


def fixed(shape):
    return pl.BlockSpec(shape, lambda i: (0,) * len(shape))


def column_half(shape, number):
    return pl.BlockSpec(
        shape[:3] + (shape[3] // 2,), lambda i: (0, 0, 0, number), pipeline_mode=pl.Buffered(1)
    )


def block_of(ref, h):
    return ref[:, h].reshape(-1, ref.shape[3])


def feed_kernel(a_ref, b_ref, c_ref, d_ref, one_ref, two_ref, row_ref, act_ref, slope_ref, top_ref, bottom_ref):
    given = either(a_ref, b_ref, c_ref, d_ref)
    row_ref[...] = given
    units = one_ref.shape[3]
    total = None
    for h in range(2):
        at = slice(h * units, (h + 1) * units)
        act, slope = gelu_parts(dot_nn(given, block_of(one_ref, h)))
        act = low(act)
        act_ref[:, at] = act
        slope_ref[:, at] = slope
        part = dot_nt(act, block_of(two_ref, h))
        total = part if total is None else total + part
    put(low(total), top_ref, bottom_ref)


def feed(pieces, both):
    tile, width = 2 * pieces[0].shape[0], pieces[0].shape[1]
    units = both.shape[3]
    return call(
        feed_kernel,
        (2,),
        [whole(pieces[0].shape)] * 4 + [column_half(both.shape, k) for k in range(2)],
        [tiled(tile, width), tiled(tile, units), tiled(tile, units), fixed((tile, width)), fixed((tile, width))],
        [((2 * tile, width), low_type), ((2 * tile, units), low_type), ((2 * tile, units), full_type)]
        + [((tile, width), low_type)] * 2,
        [],
        "feed",
    )(*pieces, both, both)


def feed_back_kernel(a_ref, b_ref, c_ref, d_ref, slope_ref, one_ref, two_ref, row_ref, dh_ref, top_ref, bottom_ref):
    given = either(a_ref, b_ref, c_ref, d_ref)
    row_ref[...] = given
    units = one_ref.shape[3]
    total = None
    for h in range(2):
        at = slice(h * units, (h + 1) * units)
        d_hidden = low(dot_nn(given, block_of(two_ref, h)) * slope_ref[:, at])
        dh_ref[:, at] = d_hidden
        part = dot_nt(d_hidden, block_of(one_ref, h))
        total = part if total is None else total + part
    put(low(total), top_ref, bottom_ref)


def feed_back(pieces, slope, both):
    tile, width = 2 * pieces[0].shape[0], pieces[0].shape[1]
    units = both.shape[3]
    return call(
        feed_back_kernel,
        (2,),
        [whole(pieces[0].shape)] * 4 + [tiled(tile, units)] + [column_half(both.shape, k) for k in range(2)],
        [tiled(tile, width), tiled(tile, units), fixed((tile, width)), fixed((tile, width))],
        [((2 * tile, width), low_type), ((2 * tile, units), low_type)] + [((tile, width), low_type)] * 2,
        [],
        "feed_back",
    )(*pieces, slope, both, both)


def head_kernel(a_ref, b_ref, c_ref, d_ref, w_ref, code_ref, column_ref, row_ref, logit_ref, stat_ref):
    given = either(a_ref, b_ref, c_ref, d_ref)
    row_ref[...] = given
    logits = jnp.concatenate([dot_nn(given, block_of(w_ref, h)) for h in range(2)], 1)
    logit_ref[...] = logits
    peak = jnp.max(logits, 1, keepdims=True)
    total = jnp.sum(jnp.exp(logits - peak), 1, keepdims=True)
    picked = jnp.sum(jnp.where(code_ref[:, 3:4] == column_ref[...], logits, 0.0), 1, keepdims=True)
    lane = lax.broadcasted_iota(jnp.int32, (logits.shape[0], 128), 1)
    turned = jnp.where(lane == 0, peak, jnp.where(lane == 1, total, picked)).T
    stat_ref[...] = turned[0:8, :]


def head(pieces, w, code, column):
    tile, width = 2 * pieces[0].shape[0], pieces[0].shape[1]
    units = 2 * w.shape[3]
    return call(
        head_kernel,
        (2,),
        [whole(pieces[0].shape)] * 4 + [whole(w.shape), tiled(tile, 128), whole((1, units))],
        [tiled(tile, width), tiled(tile, units), pl.BlockSpec((8, tile), lambda i: (0, i))],
        [((2 * tile, width), low_type), ((2 * tile, units), full_type), ((8, 2 * tile), full_type)],
        [],
        "head",
    )(*pieces, w, code, column)


def merge_kernel(sum_ref, here_ref, c_ref, l_ref, d_ref, weight_ref, out_ref, loss_ref):
    half = here_ref.shape[1] // 2

    def over_core(a):
        return jnp.concatenate([a[:, half:], a[:, :half]], 1)

    def over_line(a):
        return jnp.concatenate(
            [pltpu.roll(a[:, :half], half // 2, 1), pltpu.roll(a[:, half:], half // 2, 1)], 1
        )

    parts = (here_ref[...], over_core(c_ref[...]), over_line(l_ref[...]), over_core(over_line(d_ref[...])))
    peak = functools.reduce(jnp.maximum, [part[0:1] for part in parts])
    total = sum(part[1:2] * jnp.exp(part[0:1] - peak) for part in parts)
    picked = sum(part[2:3] for part in parts)
    log_total = peak + jnp.log(total)
    weight = weight_ref[4:5, :]
    spot = lax.broadcasted_iota(jnp.int32, (1, 2 * half), 1)
    loss = jnp.where(spot < half // 2, weight * (log_total - picked), 0.0)
    loss_ref[...] = jnp.broadcast_to(jnp.sum(loss, 1, keepdims=True), loss_ref.shape)
    blank = jnp.zeros((126, 2 * half), full_type)
    out_ref[...] = jnp.concatenate([log_total, weight / sum_ref[0], blank], 0).T


def merge(weight_sum, here, over_core, over_line, over_both, weights):
    n = here.shape[1]
    return pl.pallas_call(
        merge_kernel,
        in_specs=[pl.BlockSpec(memory_space=pltpu.SMEM)] + [pl.BlockSpec(memory_space=pltpu.VMEM)] * 5,
        out_shape=[jax.ShapeDtypeStruct((n, 128), full_type), jax.ShapeDtypeStruct((1, 128), full_type)],
        compiler_params=pltpu.CompilerParams(vmem_limit_bytes=62 * 2**20),
        cost_estimate=cost("merge"),
        name="merge",
    )(weight_sum[None], here, over_core, over_line, over_both, weights)


def head_back_kernel(logit_ref, w_ref, code_ref, column_ref, line_ref, d_ref, top_ref, bottom_ref):
    hit = jnp.where(code_ref[:, 3:4] == column_ref[...], 1.0, 0.0)
    line = line_ref[...]
    d_logits = low(line[:, 1:2] * (jnp.exp(logit_ref[...] - line[:, 0:1]) - hit))
    d_ref[...] = d_logits
    units = w_ref.shape[3]
    total = dot_nt(d_logits[:, :units], block_of(w_ref, 0)) + dot_nt(d_logits[:, units:], block_of(w_ref, 1))
    put(low(total), top_ref, bottom_ref)


def head_back(logits, w, code, column, lines):
    n, units = logits.shape
    width = w.shape[0] * w.shape[2]
    tile = n // 2
    return call(
        head_back_kernel,
        (2,),
        [tiled(tile, units), whole(w.shape), tiled(tile, 128), whole((1, units)), tiled(tile, 128)],
        [tiled(tile, units), fixed((tile, width)), fixed((tile, width))],
        [((n, units), low_type)] + [((tile, width), low_type)] * 2,
        [],
        "head_back",
    )(logits, w, code, column, lines)


def old_stats_kernel(qkv_ref, proj_ref, one_ref, two_ref, head_ref, ada_ref, tab_ref, scale_ref, out_ref):
    def total(values):
        return jnp.sum(jnp.sum(values * values, 1, keepdims=True), 0, keepdims=True)

    spot = lax.broadcasted_iota(jnp.int32, (1, 128), 1)
    line = jnp.zeros((1, 128), full_type)
    sums = [sum(total(qkv_ref[c]) for c in range(3))]
    sums += [total(ref[...]) for ref in (proj_ref, one_ref, two_ref, head_ref, scale_ref)]
    for k, value in enumerate(sums):
        line = jnp.where(spot == 16 + k, value, line)
    out_ref[0:1, :] = line
    line = jnp.where(spot == 8, total(ada_ref[...]), 0.0)
    out_ref[1:2, :] = jnp.where(spot == 9, total(tab_ref[...]), line)


def old_stats(*olds):
    return pl.pallas_call(
        old_stats_kernel,
        out_shape=jax.ShapeDtypeStruct((2, 128), full_type),
        compiler_params=pltpu.CompilerParams(vmem_limit_bytes=62 * 2**20),
        cost_estimate=cost("old_stats"),
        name="old_stats",
    )(*olds)


def put_rows(out_ref, start, value):
    groups, _, rows, _ = out_ref.shape
    for g in range(groups):
        out_ref[g, 0, :, start : start + value.shape[1]] = value[g * rows : (g + 1) * rows]


def head_grad_kernel(a_ref, b_ref, c_ref, d_ref, out_ref):
    put_rows(out_ref, 0, low(dot_tn(a_ref[...], c_ref[...]) + dot_tn(b_ref[...], d_ref[...])))


def head_grad_of(inputs, wanted, groups):
    n, width = inputs[0].shape
    columns = wanted[0].shape[1] // 2
    block = pl.BlockSpec((n, columns), lambda i: (0, i))
    return call(
        head_grad_kernel,
        (2,),
        [whole((n, width))] * 2 + [block] * 2,
        [pl.BlockSpec((groups, 1, width // groups, columns), lambda i: (0, i, 0, 0))],
        [((groups, 2, width // groups, columns), low_type)],
        [],
        "head_grad",
    )(*inputs, *wanted)[0]


def feed_grad_kernel(a_ref, b_ref, c_ref, d_ref, e_ref, f_ref, g_ref, h_ref, out_ref):
    @pl.when(pl.program_id(0) < 2)
    def _():
        put_rows(out_ref, 0, low(dot_tn(a_ref[...], c_ref[...]) + dot_tn(b_ref[...], d_ref[...])))

    @pl.when(pl.program_id(0) >= 2)
    def _():
        put_rows(out_ref, 0, low(dot_tn(e_ref[...], g_ref[...]) + dot_tn(f_ref[...], h_ref[...])))


def feed_grad_of(inputs, d_hidden, d_branch, acts, groups):
    n, width = inputs[0].shape
    columns = acts[0].shape[1] // 2
    early = pl.BlockSpec((n, columns), lambda i: (0, jnp.minimum(i, 1)))
    late = pl.BlockSpec((n, columns), lambda i: (0, jnp.maximum(i - 2, 0)))
    return call(
        feed_grad_kernel,
        (4,),
        [whole((n, width))] * 2 + [early] * 2 + [whole((n, width))] * 2 + [late] * 2,
        [pl.BlockSpec((groups, 1, width // groups, columns), lambda i: (0, i % 2, 0, i // 2))],
        [((groups, 2, width // groups, 2 * columns), low_type)],
        [],
        "feed_grad",
    )(*inputs, *d_hidden, *d_branch, *acts)[0]


def first_grad_kernel(a_ref, b_ref, c_ref, d_ref, e_ref, f_ref, g_ref, h_ref, out_ref):
    group = c_ref.shape[1] // 3
    start = pl.program_id(0) * 128

    def columns(ref):
        return jnp.concatenate(
            [ref[:, pl.ds(pl.multiple_of(start + c * group, 128), 128)] for c in range(3)], 1
        )

    put_rows(out_ref, 0, low(dot_tn(a_ref[...], columns(c_ref)) + dot_tn(b_ref[...], columns(d_ref))))
    put_rows(out_ref, 384, low(dot_tn(e_ref[...], g_ref[...]) + dot_tn(f_ref[...], h_ref[...])))


def first_grad_of(inputs, d_qkv, d_branch, mixed, groups):
    n, width = inputs[0].shape
    return call(
        first_grad_kernel,
        (2,),
        [whole((n, width))] * 2 + [whole(d_qkv[0].shape)] * 2 + [whole((n, width))] * 2
        + [pl.BlockSpec((n, 128), lambda i: (0, i))] * 2,
        [pl.BlockSpec((groups, 1, width // groups, 512), lambda i: (0, i, 0, 0))],
        [((groups, 2, width // groups, 512), low_type)],
        [],
        "first_grad",
    )(*inputs, *d_qkv, *d_branch, *mixed)[0]


def row_stats_kernel(qkv_ref, proj_ref, one_ref, two_ref, head_ref, out_ref):
    n = out_ref.shape[1]
    lane = lax.broadcasted_iota(jnp.int32, (n, 128), 1)
    out = jnp.zeros((n, 128), full_type)
    qkv = sum(jnp.sum(qkv_ref[c] * qkv_ref[c], 1, keepdims=True) for c in range(3))
    sums = [qkv + 3 * qkv_ref.shape[2] * eps_one]
    for ref in (proj_ref, one_ref, two_ref, head_ref):
        values = ref[...]
        sums.append(jnp.sum(values * values, 1, keepdims=True) + ref.shape[1] * eps_one)
    for k, column in enumerate(sums):
        out = jnp.where(lane == k, column, out)
    out_ref[...] = out.T[0:8, :]


def row_stats(*gradients):
    n = gradients[1].shape[0]
    return pl.pallas_call(
        row_stats_kernel,
        out_shape=jax.ShapeDtypeStruct((8, n), full_type),
        compiler_params=pltpu.CompilerParams(vmem_limit_bytes=62 * 2**20),
        cost_estimate=cost("row_stats"),
        name="row_stats",
    )(*gradients)


def column_stats_kernel(
    at_ref, row_ref, old_ref, tail_ref, tables_ref, scale_ref, qkv_ref, proj_ref, one_ref, two_ref, head_ref, ada_ref, out_ref, new_ref, *, decay
):
    n = proj_ref.shape[0]
    rows = row_ref[...]
    padded = jnp.concatenate([rows, jnp.zeros((128 - rows.shape[0], n), full_type)], 0).T
    at = 0
    pieces = [(qkv_ref[c], 0) for c in range(3)]
    pieces += [(ref[...], k + 1) for k, ref in enumerate((proj_ref, one_ref, two_ref, head_ref))]
    for values, k in pieces:
        square = values * values
        columns = square.shape[1]
        out_ref[0:1, at : at + columns] = jnp.sum(square, 0, keepdims=True) + n * eps_one
        out_ref[1:2, at : at + columns] = jnp.sum(
            square * (1.0 / padded[:, k : k + 1]), 0, keepdims=True
        )
        at += columns
    columns = ada_ref.shape[1]
    step = 1024
    total = jnp.zeros((n, 1), full_type)
    for start in range(0, columns, step):
        values = ada_ref[:, start : start + step]
        total = total + jnp.sum(values * values, 1, keepdims=True)
    old = jnp.concatenate([old_ref[...], jnp.zeros((127, n), full_type)], 0).T[:, 0:1]
    row = decay * old + (1.0 - decay) * (total / columns + eps_one)
    lane = lax.broadcasted_iota(jnp.int32, (n, 128), 1)
    new_ref[...] = jnp.where(lane == 0, row, 0.0).T[0:8, :]
    for start in range(0, columns, step):
        values = ada_ref[:, start : start + step]
        square = values * values
        out_ref[0:1, at : at + step] = jnp.sum(square, 0, keepdims=True) + n * eps_one
        out_ref[1:2, at : at + step] = jnp.sum(square * (1.0 / row), 0, keepdims=True)
        at += step
    spots = lax.broadcasted_iota(jnp.int32, (1, 128), 1)
    line = tail_ref[...]
    for k in range(5):
        line = jnp.where(spots == k, jnp.sum(rows[k : k + 1, :], 1, keepdims=True), line)
    line = jnp.where(spots == 5, jnp.sum(row, 0, keepdims=True), line)
    line = jnp.where(spots == 10, tables_ref[...], line)
    scales = scale_ref[...]
    for k in range(2):
        value = jnp.sum(jnp.where((spots < 64) == (k == 0), scales, 0.0), 1, keepdims=True)
        line = jnp.where(spots == 11 + k + 2 * at_ref[0], value, line)
    out_ref[0:1, at : at + 128] = line
    out_ref[1:2, at : at + 128] = jnp.zeros_like(line)


def column_stats(at_c, row_new, old, tail, tables_sum, scales, gradients, decay):
    n = gradients[1].shape[0]
    columns = sum(g.size // n for g in gradients)
    return pl.pallas_call(
        functools.partial(column_stats_kernel, decay=decay),
        out_shape=[
            jax.ShapeDtypeStruct((2, columns + 128), full_type),
            jax.ShapeDtypeStruct((8, n), full_type),
        ],
        in_specs=[pl.BlockSpec(memory_space=pltpu.SMEM)]
        + [pl.BlockSpec(memory_space=pltpu.VMEM)] * (5 + len(gradients)),
        compiler_params=pltpu.CompilerParams(vmem_limit_bytes=62 * 2**20),
        cost_estimate=cost("column_stats"),
        name="column_stats",
    )(at_c[None], row_new, old, tail, tables_sum, scales, *gradients)


def spot_of(line, k):
    spots = lax.broadcasted_iota(jnp.int32, line.shape, 1)
    return jnp.sum(jnp.where(spots == k, line, 0.0), 1, keepdims=True)


def finish_kernel(
    flat_ref, old_ref, scale_ref, col_ref, part_ref, own_ref, second_ref, step_ref, *, decay, width, starts
):
    columns = old_ref.shape[1]
    line = flat_ref[0:1, columns:]
    new = decay * old_ref[...] + (1.0 - decay) * (flat_ref[0:1, :columns] / width)
    col_ref[...] = new
    ratio = flat_ref[1:2, :columns] / new
    spots = lax.broadcasted_iota(jnp.int32, (1, 128), 1)
    scales = (spots >= 11) & (spots < 15)
    gradient = jnp.where(scales, line, 0.0)
    second = decay * scale_ref[...] + (1.0 - decay) * (gradient * gradient + eps_one)
    step = gradient * lax.rsqrt(second)
    second_ref[...] = second
    step_ref[...] = step
    out = jnp.where(spots == 7, jnp.sum(step * step, 1, keepdims=True), 0.0)
    for k in range(6):
        value = jnp.sum(ratio[:, starts[k] : starts[k + 1]], 1, keepdims=True) * (spot_of(line, k) / width)
        if k == 5:
            own_ref[...] = jnp.where(spots == 5, value, 0.0)
        else:
            out = jnp.where(spots == k, value, out)
    part_ref[...] = out


def finish(flat, col_old, scale_line, decay, width, starts):
    return pl.pallas_call(
        functools.partial(finish_kernel, decay=decay, width=width, starts=starts),
        out_shape=[jax.ShapeDtypeStruct(col_old.shape, full_type)]
        + [jax.ShapeDtypeStruct((1, 128), full_type)] * 4,
        compiler_params=pltpu.CompilerParams(vmem_limit_bytes=62 * 2**20),
        cost_estimate=cost("finish"),
        name="finish",
    )(flat, col_old, scale_line)


def renew_kernel(
    line_ref, part_ref, own_ref, early_ref, rows_ref, col_ref, ada_col_ref,
    qkv_g, proj_g, one_g, two_g, head_g, ada_g, step_ref, scale_step_ref,
    qkv_ref, proj_ref, one_ref, two_ref, head_ref, ada_ref, tab_ref, scale_ref,
    qkv_out, proj_out, one_out, two_out, head_out, ada_out, tab_out, scale_out, proj_turned, two_turned,
    *, width, entries, starts
):
    n = one_g.shape[0]
    line, part = line_ref[...], part_ref[...]

    def factor(k):
        step = spot_of(own_ref[...], 5) if k == 5 else spot_of(line, 10) if k == 6 else spot_of(part, k)
        weight = spot_of(early_ref[...], 21) if k == 7 else spot_of(line, {5: 8, 6: 9}.get(k, 16 + k))
        ratio = jnp.sqrt(step / entries[k]) / clip_rms
        spread = jnp.maximum(eps_two, jnp.sqrt(weight / entries[k]))
        return rate_step * spread / jnp.maximum(1.0, ratio)

    def row(k):
        rows = jnp.concatenate([rows_ref[k : k + 1, :], jnp.zeros((127, n), full_type)], 0)
        return rows.T[:, 0:1]

    def change(k, gradient, columns):
        mean = spot_of(line, k) / width
        return factor(k) * (gradient * lax.rsqrt(row(k) * columns / mean))

    ada_out[...] = ada_ref[...] - change(5, ada_g[...], ada_col_ref[...])
    at = pl.program_id(0)

    @pl.when(at == 0)
    def _():
        size = qkv_g.shape[2]
        for c in range(3):
            qkv_out[c] = qkv_ref[c] - change(0, qkv_g[c], col_ref[:, c * size : (c + 1) * size])

    @pl.when(at == 1)
    def _():
        gradient = proj_g[...]
        proj_turned[...] = gradient.T
        proj_out[...] = proj_ref[...] - change(1, gradient, col_ref[:, starts[1] : starts[2]]).T
        scale_out[...] = scale_ref[...] - factor(7) * scale_step_ref[...]

    @pl.when(at == 2)
    def _():
        one_out[...] = one_ref[...] - change(2, one_g[...], col_ref[:, starts[2] : starts[3]])

    @pl.when(at == 3)
    def _():
        gradient = two_g[...]
        two_turned[...] = gradient.T
        two_out[...] = two_ref[...] - change(3, gradient, col_ref[:, starts[3] : starts[4]]).T

    @pl.when(at == 4)
    def _():
        head_out[...] = head_ref[...] - change(4, head_g[...], col_ref[:, starts[4] : starts[5]])

    @pl.when(at == 5)
    def _():
        tab_out[...] = tab_ref[...] - factor(6) * step_ref[...]


def renew(lines, rows, columns, grads, steps, olds, width, entries, starts):
    n, tile = grads[2].shape[0], 1024
    ada = pl.BlockSpec((n, tile), lambda i: (0, i))
    first = starts[5] // tile

    def wholes(arrays):
        return [whole(a.shape) for a in arrays]

    outs = [a.shape for a in olds] + [olds[1].shape, olds[3].shape]
    out_specs = [ada if k == 5 else fixed(shape) for k, shape in enumerate(outs)]
    return call(
        functools.partial(renew_kernel, width=width, entries=entries, starts=starts),
        (olds[5].shape[1] // tile,),
        wholes(lines)
        + [whole(rows.shape), whole(columns.shape), pl.BlockSpec((1, tile), lambda i: (0, first + i))]
        + wholes(grads[:5])
        + [ada]
        + wholes(steps)
        + wholes(olds[:5])
        + [ada]
        + wholes(olds[6:]),
        out_specs,
        [(shape, full_type) for shape in outs],
        [],
        "renew",
    )(*lines, rows, columns, columns, *grads, *steps, *olds)


def head_lanes(shape):
    return lax.broadcasted_iota(jnp.int32, shape, len(shape) - 1) < 64


def per_head(values, first):
    left = jnp.sum(jnp.where(first, values, 0.0), -1, keepdims=True)
    right = jnp.sum(jnp.where(first, 0.0, values), -1, keepdims=True)
    return jnp.where(first, left, right)


def attend_kernel(
    q_ref, k_ref, v_ref, gain_ref, col_ref, row_ref, proj_ref,
    mix_ref, lse_ref, top_ref, bottom_ref, q_s, k_s, v_s, bias_s, sum_s
):
    length = q_ref.shape[0]
    tile = length // 2
    first = head_lanes((length, 128))
    query = q_ref[...]
    key = k_ref[...]
    q_s[...] = low(
        query * (lax.rsqrt(per_head(query * query, first) / 64.0 + eps_norm) * gain_ref[...])
    )
    k_s[...] = low(key * (lax.rsqrt(per_head(key * key, first) / 64.0 + eps_norm) * 0.125))
    v_s[...] = low(v_ref[...])
    first_t = head_lanes((tile, 128))

    @pl.when(pl.program_id(0) == 0)
    def _():
        ck = row_ref[2:3, :]
        for i in range(2):
            rows = slice(i * tile, (i + 1) * tile)
            shape = (tile, length)
            here = lax.broadcasted_iota(jnp.int32, shape, 1) - lax.broadcasted_iota(jnp.int32, shape, 0)
            keep = ((ck <= col_ref[rows, 0:1]) & (ck >= col_ref[rows, 1:2])) | (here == i * tile)
            bias_s[rows, :] = jnp.where(keep, 0.0, -1e30)
        sum_s[...] = jnp.zeros_like(sum_s)

    for i, out_ref in enumerate((top_ref, bottom_ref)):
        rows = slice(i * tile, (i + 1) * tile)
        query_t = q_s[rows, :]
        mixed, logs = [], []
        for head in range(2):
            chosen = first_t if head == 0 else ~first_t
            scores = dot_nt(jnp.where(chosen, query_t, jnp.zeros_like(query_t)), k_s[...]) + bias_s[rows, :]
            exponent = jnp.exp(scores)
            total = jnp.sum(exponent, -1, keepdims=True)
            mixed.append(dot_nn(low(exponent * (1.0 / total)), v_s[...]))
            logs.append(jnp.log(total))
        mixed = low(jnp.where(first_t, mixed[0], mixed[1]))
        mix_ref[rows, :] = mixed
        turned = jnp.where(first_t, logs[0], logs[1]).T
        lse_ref[0, 0:1, rows] = turned[0:1, :]
        lse_ref[0, 1:2, rows] = turned[64:65, :]
        part = sum_s[rows, :] + dot_nt(mixed, proj_ref[...])
        sum_s[rows, :] = part

        @pl.when(pl.program_id(0) == pl.num_programs(0) - 1)
        def _():
            out_ref[...] = low(part)


def attend(qkv, gain, cols, rows, proj):
    length = qkv.shape[0]
    pairs = qkv.shape[1] // 384
    width = proj.shape[0]
    block = pl.BlockSpec((length, 128), lambda p: (0, p))
    return call(
        attend_kernel,
        (pairs,),
        [
            block,
            pl.BlockSpec((length, 128), lambda p: (0, pairs + p)),
            pl.BlockSpec((length, 128), lambda p: (0, 2 * pairs + p)),
            pl.BlockSpec((1, 128), lambda p: (0, p)),
            whole((length, 128)),
            whole((8, length)),
            pl.BlockSpec((width, 128), lambda p: (0, p)),
        ],
        [block, pl.BlockSpec((1, 2, length), lambda p: (p, 0, 0))] + [fixed((length // 2, width))] * 2,
        [((length, 128 * pairs), low_type), ((pairs, 2, length), full_type)]
        + [((length // 2, width), low_type)] * 2,
        [pltpu.VMEM((length, 128), low_type)] * 3
        + [pltpu.VMEM((length, length), full_type), pltpu.VMEM((length, width), full_type)],
        "attend",
    )(qkv, qkv, qkv, gain, cols, rows, proj)


def attend_back_kernel(
    q_ref, k_ref, v_ref, gain_ref, col_ref, line_ref, lse_ref, pa_ref, pb_ref, pc_ref, pd_ref,
    proj_ref, wq_ref, wk_ref, wv_ref, row_ref, d_ref, ds_ref, top_ref, bottom_ref,
    q_s, k_s, v_s, dm_ref, dqa, dka, dva, bias_s, sum_s
):
    length = q_ref.shape[0]
    first = head_lanes((length, 128))
    query = q_ref[...]
    key = k_ref[...]
    gain = gain_ref[...]
    q_n = lax.rsqrt(per_head(query * query, first) / 64.0 + eps_norm)
    k_n = lax.rsqrt(per_head(key * key, first) / 64.0 + eps_norm)
    q_s[...] = low(query * (q_n * gain))
    k_s[...] = low(key * (k_n * 0.125))
    v_s[...] = low(v_ref[...])
    quarter = length // 4
    for k, ref in enumerate((pa_ref, pb_ref, pc_ref, pd_ref)):
        rows = slice(k * quarter, (k + 1) * quarter)
        dm_ref[rows, :] = low(dot_nn(ref[...], proj_ref[...]))

    @pl.when(pl.program_id(0) == 0)
    def _():
        sum_s[...] = jnp.zeros_like(sum_s)
        for k, ref in enumerate((pa_ref, pb_ref, pc_ref, pd_ref)):
            row_ref[k * quarter : (k + 1) * quarter, :] = ref[...]

    tile = length // 2
    first_t = head_lanes((tile, 128))

    @pl.when(pl.program_id(0) == 0)
    def _():
        ck = col_ref[:, 2:3]
        for i in range(2):
            rows = slice(i * tile, (i + 1) * tile)
            shape = (length, tile)
            here = lax.broadcasted_iota(jnp.int32, shape, 0) - lax.broadcasted_iota(jnp.int32, shape, 1)
            keep = ((ck <= line_ref[0:1, rows]) & (ck >= line_ref[1:2, rows])) | (here == i * tile)
            bias_s[:, rows] = jnp.where(keep, 0.0, -1e30)

    d_keys, d_values = None, None
    for i in range(2):
        rows = slice(i * tile, (i + 1) * tile)
        query_t = q_s[rows, :]
        dmix_t = dm_ref[rows, :]
        d_query = []
        for head in range(2):
            chosen = first_t if head == 0 else ~first_t
            zero = jnp.zeros_like(query_t)
            query_h = jnp.where(chosen, query_t, zero)
            dmix_h = jnp.where(chosen, dmix_t, zero)
            scores = dot_nt(k_s[...], query_h) + bias_s[:, rows]
            attention = jnp.exp(scores - lse_ref[0, head : head + 1, rows])
            part = dot_nn(low(attention), dmix_h)
            d_values = part if d_values is None else d_values + part
            d_att = dot_nt(v_s[...], dmix_h)
            inner = jnp.sum(attention * d_att, 0, keepdims=True)
            d_scores = low(attention * (d_att - inner))
            part = dot_nn(d_scores, query_h)
            d_keys = part if d_keys is None else d_keys + part
            d_query.append(dot_tn(d_scores, k_s[...]))
        dqa[rows, :] = jnp.where(first_t, d_query[0], d_query[1])
    dka[...] = d_keys
    dva[...] = d_values
    q_hat = query * q_n
    k_hat = key * k_n
    d_query = dqa[...]
    along = d_query * q_hat
    ds_ref[0] = jnp.sum(along, 0, keepdims=True) * gain
    group = d_ref.shape[1] // 3
    start = pl.program_id(0) * 128

    def columns(c):
        return pl.ds(pl.multiple_of(start + c * group, 128), 128)

    out_q = low(gain * (d_query - q_hat * (per_head(along, first) / 64.0)) * q_n)
    d_ref[:, columns(0)] = out_q
    d_key = dka[...]
    out_k = low(
        0.125 * (d_key - k_hat * (per_head(d_key * k_hat, first) / 64.0)) * k_n
    )
    out_v = low(dva[...])
    d_ref[:, columns(1)] = out_k
    d_ref[:, columns(2)] = out_v
    half = length // 2
    for rows, out_ref in ((slice(0, half), top_ref), (slice(half, length), bottom_ref)):
        part = sum_s[rows, :] + dot_nt(out_q[rows], wq_ref[...])
        part = part + dot_nt(out_k[rows], wk_ref[...]) + dot_nt(out_v[rows], wv_ref[...])
        sum_s[rows, :] = part

        @pl.when(pl.program_id(0) == pl.num_programs(0) - 1)
        def _():
            out_ref[...] = low(part)


def attend_back(qkv, gain, cols, rows, lse, pieces, proj, w):
    length = qkv.shape[0]
    pairs = qkv.shape[1] // 384
    width = proj.shape[0]

    def part(rows, number):
        return pl.BlockSpec((rows, 128), lambda p: (0, number * pairs + p))

    return call(
        attend_back_kernel,
        (pairs,),
        [
            part(length, 0),
            part(length, 1),
            part(length, 2),
            pl.BlockSpec((1, 128), lambda p: (0, p)),
            whole((length, 128)),
            whole((8, length)),
            pl.BlockSpec((1, 2, length), lambda p: (p, 0, 0)),
        ]
        + [whole(pieces[0].shape)] * 4
        + [part(width, 0), part(width, 0), part(width, 1), part(width, 2)],
        [
            fixed((length, width)),
            fixed((length, 384 * pairs)),
            pl.BlockSpec((1, 1, 128), lambda p: (p, 0, 0)),
            fixed((length // 2, width)),
            fixed((length // 2, width)),
        ],
        [
            ((length, width), low_type),
            ((length, 384 * pairs), low_type),
            ((pairs, 1, 128), full_type),
            ((length // 2, width), low_type),
            ((length // 2, width), low_type),
        ],
        [pltpu.VMEM((length, 128), low_type)] * 4
        + [pltpu.VMEM((length, 128), full_type)] * 3
        + [pltpu.VMEM((length, length), full_type), pltpu.VMEM((length, width), full_type)],
        "attend_back",
    )(qkv, qkv, qkv, gain, cols, rows, lse, *pieces, proj, w, w, w)


def body(
    vq_in, codes, segment, live, labels, level_weight, qkv_w, proj_w, fc1_w, fc2_w, head_w, ada_w,
    tables, head_scale, d_stats, qkv_stat, proj_stat, fc1_stat, fc2_stat, head_stat, ada_stat,
    tables_v, scale_v,
):
    g_count = lax.axis_size("g")
    dp_count = g_count * lax.axis_size("c")
    mp_count = lax.axis_size("h") * lax.axis_size("l")
    at_c, at_h, at_l = lax.axis_index("c"), lax.axis_index("h"), lax.axis_index("l")
    row_count, seq_len, code_dim = vq_in.shape
    item_count = labels.shape[1]
    level_count = level_weight.shape[0]
    slice_width = tables.shape[1]
    width = slice_width * dp_count
    half, quarter = seq_len // 2, seq_len // 4
    table_rows = tables.shape[0]
    lead = code_dim + level_count
    per_row = row_count * item_count
    note_rows = -(-(2 * per_row + 3) // slice_width)
    lead_pad = -(-(lead + note_rows) // 16) * 16

    def halves(a):
        n = a.shape[-1] // 2
        lower, upper = low(a[..., :n]), low(a[..., n:])
        return jnp.where(at_c == 0, lower, upper), jnp.where(at_c == 0, upper, lower)

    first_mine, first_other = halves(jnp.concatenate([qkv_w, proj_w.T[None]], 0))
    first_near = ordered(at_c, first_mine, over_c(first_other), 1)

    place, weight, weight_here = row_layout(level_weight, segment, live)
    weight_here = weight_here[0, 0]

    per_row = row_count * item_count
    note_rows = -(-(2 * per_row + 3) // slice_width)
    lead_pad = -(-(lead + note_rows) // 16) * 16
    tables_low = low(tables)
    label_flat = labels.reshape(-1)
    digits = jnp.stack([weight_here // 4096, (weight_here // 64) % 64, weight_here % 64])
    note = jnp.concatenate([label_flat // 32, label_flat % 32, digits])
    note = jnp.pad(low(note), (0, (lead_pad - lead) * slice_width - note.shape[0]))
    note = note.reshape(lead_pad - lead, slice_width)
    packed = tie(jnp.concatenate([tables_low[:lead], note], 0), first_near)
    gathered, first_far = lax.optimization_barrier(
        (lax.all_gather(packed, DP, axis=0), over_h(first_near))
    )
    lead_table = jnp.transpose(gathered, (1, 0, 2)).reshape(lead_pad, width)
    notes = gathered[:, lead : lead + note_rows].reshape(dp_count, -1).astype(jnp.int32)
    labels_all = (notes[:, :per_row] * 32 + notes[:, per_row : 2 * per_row]).reshape(-1)
    weight_sum = full(
        jnp.sum(
            notes[:, 2 * per_row] * 4096
            + notes[:, 2 * per_row + 1] * 64
            + notes[:, 2 * per_row + 2]
        )
    )

    class_hot = (
        labels_all[:, None] + lead == jnp.arange(table_rows, dtype=jnp.int32)[None, :]
    )
    class_vec = dot_nn(low(class_hot), tables_low)
    sigma = jax.nn.sigmoid(class_vec)
    activated = low(class_vec * sigma)
    act_pairs = activated.reshape(g_count, 2, per_row, slice_width)
    act_mine = jnp.where(at_h == 0, act_pairs[:, 0], act_pairs[:, 1]).reshape(-1, slice_width)
    ada_low = low(ada_w)
    mod_part = dot_nn(act_mine, ada_low)
    mod_half = ada_w.shape[1] // 2
    left, right = mod_part[:, :mod_half], mod_part[:, mod_half:]
    mod_send = jnp.where(at_c == 0, right, left)
    mod_sum = jnp.where(at_c == 0, left, right) + over_c(mod_send)
    mod_first = mod_sum
    mod_sum = scatter_g(mod_sum)
    mod_items = ordered(at_c, mod_sum, over_c(mod_sum), 1).reshape(row_count, item_count, 8, width)
    mod_rows = jnp.transpose(mod_items, (0, 2, 1, 3))

    fc1_wide, fc2_wide = tie((fc1_w, fc2_w), mod_send)

    def near_rows(w):
        kept, other = halves(w)
        return ordered(at_c, kept, over_c(other), 0)

    def gathered_weight(a):
        wide = lax.all_gather(a.reshape(-1, a.shape[2]), "g", axis=0, tiled=True)
        return wide.reshape((g_count,) + a.shape)

    feed_near = jnp.concatenate([near_rows(fc1_wide), near_rows(fc2_wide.T)], 1)
    qkv_piece = ordered(at_h, first_near[None], first_far[None], 0)

    def window(*values):
        return lax.optimization_barrier(values)

    def far_part(r):
        return low(full(top[r][quarter:]) + full(moved[r][quarter:]))

    def turn(norm, kernel, filler=lambda: None, beside=None, keep=lambda done: None):
        moved[1] = over_c(bottom[1])
        first, moved[1] = window(norm(0, (top[0], moved[0], across[0])), moved[1])
        across[1] = over_l(far_part(1))
        pieces = [[first, over_l(first), over_c(first), None], None]
        done, across[1], pieces[0][2] = window(filler(), across[1], pieces[0][2])
        keep(done)
        second, pieces[0][1] = window(norm(1, (top[1], moved[1], across[1])), pieces[0][1])
        pieces[1] = [second, over_l(second), over_c(second), None]
        pieces[0][3] = over_c(pieces[0][1])
        kernel_out, pieces[1], beside = window(kernel(0, pieces[0]), pieces[1][:3], beside)
        return pieces, kernel_out, done, beside

    def launch():
        moved[0] = over_c(bottom[0])
        sent = far_part(0)
        across[0] = over_l(sent)
        return sent

    head_gain = tie(head_scale, mod_first)
    gain_own = jnp.where(at_c == 0, head_gain[:2], head_gain[2:])

    info = full(jnp.stack([codes, place, live, weight], 1))
    info_other, vq_other = over_c(info), over_c(vq_in)
    at = jnp.stack([full(at_c == at_h).astype(jnp.int32), at_c, at_l])
    arranged, olds, qkv_pieces, feed_far, gain_far = window(
        arrange(at, tie(info, mod_first), info_other, vq_in, vq_other, lead_pad),
        old_stats(*tie((qkv_w, proj_w, fc1_w, fc2_w, head_w, ada_w, tables, head_scale[None]), mod_first)),
        [qkv_piece] + [over_g(qkv_piece, k) for k in range(1, 4)] if g_count == 4 else [],
        over_h(feed_near),
        over_h(gain_own),
    )
    gains = jnp.exp(ordered(at_h, gain_own, gain_far, 0)) / 8.0
    gain_row = jnp.repeat(gains, 64)[None, :]
    feats, hot, cols, rows = (arranged[k::4] for k in range(4))
    head_near = near_rows(tie(head_w, olds))
    feats_first = tie(feats[0], gain_row)
    inputs_one, qkv_rows, mixed_rows, lse_rows, top, bottom, stream_zero = ([None] * 2 for _ in range(7))
    if g_count == 4:
        inputs_one[0], qkv_rows[0], stream_zero[0], qkv_full, proj_full = enter_first(
            lax.axis_index("g"), feats_first, lead_table, hot[0], mod_rows[0], qkv_pieces
        )
    else:
        wide_piece = lax.all_gather(qkv_piece, "g", axis=0)
        wide_piece = jnp.transpose(wide_piece, (0, 3, 2, 1, 4)).reshape(width, -1)
        qkv_full, proj_full = wide_piece[:, :768], wide_piece[:, 768:]
        inputs_one[0], qkv_rows[0], stream_zero[0] = enter(feats_first, lead_table, hot[0], mod_rows[0], qkv_full)
    feed_full = gathered_weight(ordered(at_h, feed_near[None], feed_far[None], 0))

    moved, across = [None] * 2, [None] * 2

    def attention(r, given):
        mixed_rows[r], lse_rows[r], top[r], bottom[r] = attend(
            given, gain_row, cols[r], rows[r], proj_full
        )
        return top[r], bottom[r]

    (top[0], bottom[0]), head_far = window(attention(0, qkv_rows[0]), over_h(head_near))
    held = [gathered_weight(ordered(at_h, head_near[None], head_far[None], 0))]
    moved[0] = over_c(bottom[0])
    (inputs_one[1], qkv_rows[1], stream_zero[1]), moved[0] = window(
        enter(tie(feats[1], bottom[0]), lead_table, hot[1], mod_rows[1], qkv_full), moved[0]
    )
    sent = far_part(0)
    across[0] = over_l(sent)
    (top[1], bottom[1]), across[0] = window(attention(1, tie(qkv_rows[1], sent)), across[0])

    branch_one, stream_one, acts, slopes, inputs_two = ([None] * 2 for _ in range(5))

    def norm_two(r, parts):
        branch_one[r], stream_one[r], given = onward(parts, stream_zero[r], hot[r], mod_rows[r], (2, 3, 4))
        return given

    def forward(r, pieces):
        inputs_two[r], acts[r], slopes[r], top[r], bottom[r] = feed(pieces, feed_full)
        return top[r], bottom[r]

    pieces_two, (top[0], bottom[0]), _, _ = turn(norm_two, forward)
    pieces_two[1].append(over_c(pieces_two[1][1]))
    sent = launch()
    (top[1], bottom[1]), across[0] = window(
        forward(1, [tie(pieces_two[1][0], sent)] + pieces_two[1][1:]), across[0]
    )

    block_codes = head_w.shape[1]
    half_codes = block_codes // 2
    column = jnp.arange(2 * half_codes, dtype=jnp.int32)
    block_here = (column // half_codes) * 2 + at_l
    column_code = full(block_here * block_codes + at_c * half_codes + column % half_codes)[None, :]
    branch_two, stream_two, logits, stats, d_logits, losses, others, inputs_out = ([None] * 2 for _ in range(8))

    def norm_out(r, parts):
        branch_two[r], stream_two[r], given = onward(parts, stream_one[r], hot[r], mod_rows[r], (5, 6, 7))
        return given

    def score(r, pieces):
        inputs_out[r], logits[r], stats[r] = head(pieces, held[0], cols[r], column_code)
        return stats[r]

    def compare(r):
        return [over_c(stats[r]), over_l(stats[r]), over_cl(stats[r])]

    def score_back(r):
        lines, losses[r] = merge(weight_sum, stats[r], *others[r], rows[r])
        d_logits[r], top[r], bottom[r] = head_back(logits[r], held[0], cols[r], column_code, lines)
        return top[r], bottom[r]

    pieces_out, stats[0], _, _ = turn(
        norm_out, score, lambda: held[0], keep=lambda done: held.__setitem__(0, done)
    )
    pieces_out[1].append(over_c(pieces_out[1][1]))
    stats[1], others[0] = window(score(1, pieces_out[1]), compare(0))
    (top[0], bottom[0]), others[1] = window(score_back(0), compare(1))
    sent = launch()
    logits[1] = tie(logits[1], sent)
    (top[1], bottom[1]), across[0] = window(score_back(1), across[0])

    def reduced(a):
        shape = a.shape[1:]
        a = lax.psum_scatter(a.reshape(-1, shape[2]), "g", scatter_dimension=0, tiled=True)
        return a.reshape(shape)

    def theirs(a):
        return jnp.where(at_h == 0, a[1], a[0])

    def settle(a, other):
        a = full(jnp.where(at_h == 0, a[0], a[1])) + full(other)
        rows = a.shape[0] // 2
        kept = jnp.where(at_c == 0, a[:rows], a[rows:])
        return kept, over_c(jnp.where(at_c == 0, a[rows:], a[:rows]))

    d_two, d_one, items_out, items_two, d_hidden, d_branch_two, d_branch_one = ([None] * 2 for _ in range(7))

    def back_out(r, parts):
        d_two[r], given, items_out[r] = back(
            parts, stream_two[r], hot[r], mod_rows[r], (7, 5), None, branch_two[r], None
        )
        return given

    def backward(r, pieces):
        d_branch_two[r], d_hidden[r], top[r], bottom[r] = feed_back(pieces, slopes[r], feed_full)
        return top[r], bottom[r]

    pieces_d_two, (top[0], bottom[0]), head_part, _ = turn(
        back_out, backward, lambda: head_grad_of(inputs_out, d_logits, g_count)
    )
    head_sum = reduced(head_part)
    pieces_d_two[1].append(over_c(pieces_d_two[1][1]))
    sent = launch()
    (top[1], bottom[1]), across[0], head_sum = window(
        backward(1, [tie(pieces_d_two[1][0], sent)] + pieces_d_two[1][1:]), across[0], head_sum
    )

    d_qkv, scale_rows = ([None] * 2 for _ in range(2))

    def back_two(r, parts):
        d_one[r], given, items_two[r] = back(
            parts, stream_one[r], hot[r], mod_rows[r], (4, 2), d_two[r], branch_one[r], None
        )
        return given

    def attention_back(r, pieces):
        d_branch_one[r], d_qkv[r], scale_rows[r], top[r], bottom[r] = attend_back(
            qkv_rows[r], gain_row, cols[r], rows[r], lse_rows[r], pieces, proj_full, qkv_full
        )
        return top[r], bottom[r]

    pieces_d_one, (top[0], bottom[0]), feed_part, head_other = turn(
        back_two,
        attention_back,
        lambda: feed_grad_of(inputs_two, d_hidden, d_branch_two, acts, g_count),
        over_h(theirs(head_sum)),
    )
    feed_sum = reduced(feed_part)
    pieces_d_one[1].append(over_c(pieces_d_one[1][1]))
    sent = launch()
    leaving = theirs(feed_sum)
    (top[1], bottom[1]), across[0], feed_other = window(
        attention_back(1, [tie(pieces_d_one[1][0], sent, leaving)] + pieces_d_one[1][1:]), across[0], over_h(leaving)
    )
    moved[1] = over_c(bottom[1])
    items_one, lead_parts = ([None] * 2 for _ in range(2))

    def back_one(r, parts):
        items_one[r], lead_parts[r] = back(
            parts, stream_zero[r], hot[r], mod_rows[r], (1,), d_one[r], None, feats[r]
        )
        return items_one[r]

    items_one[0], moved[1] = window(back_one(0, (top[0], moved[0], across[0])), moved[1])
    sent = far_part(1)
    across[1] = over_l(sent)
    first_part = first_grad_of(inputs_one, tie(d_qkv, sent), d_branch_one, mixed_rows, g_count)
    first_part, across[1] = window(first_part, across[1])
    first_sum = reduced(first_part)
    back_one(1, (top[1], moved[1], across[1]))
    lead_part = lead_parts[0] + lead_parts[1]

    def flat_items(items, number):
        return jnp.concatenate([items[r][number, :item_count] for r in range(2)], 0)

    d_items = jnp.concatenate(
        [flat_items(items_one, 0), flat_items(items_one, 1), flat_items(items_two, 2)]
        + [flat_items(items_two, 0), flat_items(items_two, 1), flat_items(items_out, 2)]
        + [flat_items(items_out, 0), flat_items(items_out, 1)],
        1,
    )
    left, right = d_items[:, :mod_half], d_items[:, mod_half:]
    d_items = jnp.where(at_c == 0, left, right) + over_c(jnp.where(at_c == 0, right, left))
    d_items = low(d_items + over_l(d_items))
    d_items, first_sum = window(ordered(at_h, d_items, over_h(d_items), 0), first_sum)
    leaving = theirs(first_sum)
    d_items = gather_g(tie(d_items, leaving))
    d_items = ordered(at_c, d_items, over_c(d_items), 1)
    ada_grad = dot_tn(activated, d_items)
    d_act_vec = dot_nt(d_items, ada_low)
    d_class = d_act_vec * (sigma * (1.0 + class_vec * (1.0 - sigma)))
    lead_part = jnp.transpose(lead_part.reshape(lead_pad, dp_count, slice_width), (1, 0, 2))
    lead_grad = jnp.sum(lax.all_to_all(lead_part, DP, 0, 0, tiled=True).reshape(dp_count, lead_pad, slice_width), 0)
    lead_grad = lead_grad + over_l(lead_grad)
    lead_grad = lead_grad + over_h(lead_grad)
    tables_grad = dot_tn(full(class_hot), d_class, highest)
    tables_grad = tables_grad + jnp.pad(lead_grad[:lead], ((0, table_rows - lead), (0, 0)))

    head_grad = ordered(at_c, *settle(tie(head_sum, items_one[0]), head_other), 1)
    kept, moved_half = settle(feed_sum, feed_other)
    n = kept.shape[1] // 2
    fc1_grad = ordered(at_c, kept[:, :n], moved_half[:, :n], 1)
    fc2_grad = ordered(at_c, kept[:, n:], moved_half[:, n:], 1)
    ada_grad, tables_grad, first_other = window(ada_grad, tables_grad, over_h(leaving))
    kept, moved_half = settle(first_sum, first_other)
    first_halves = jnp.stack([kept, moved_half])
    first_halves = jnp.where(at_c == 0, first_halves, first_halves[::-1])
    first_halves = jnp.transpose(first_halves.reshape(2, slice_width, 4, -1), (2, 1, 0, 3))
    first_halves = first_halves.reshape(4, slice_width, -1)
    qkv_grad, proj_grad = first_halves[:3], first_halves[3]

    decay = 1.0 - STEP ** (-0.8)
    grads = [qkv_grad, proj_grad, fc1_grad, fc2_grad, head_grad, ada_grad]
    wide = [g.size // slice_width * (mp_count if k < 5 else 1) for k, g in enumerate(grads)]
    sizes = [g.size // slice_width for g in grads]
    starts = [sum(sizes[:k]) for k in range(7)]

    def over_mp(a):
        a = a + over_l(a)
        return a + over_h(a)

    spots = jnp.arange(128, dtype=jnp.int32)[None, :]
    early_line = over_mp(tie(olds[:1] + jnp.where(spots == 22, losses[0] + losses[1], 0.0), lead_part))
    tail = early_line + olds[1:]
    rows_all = over_mp(row_stats(*grads[:5]))
    wide_column = jnp.array(wide[:5], full_type)[:, None]
    row_new = decay * d_stats[:5] + (1.0 - decay) * (rows_all[:5] / wide_column)
    tables_v_new = decay * tables_v + (1.0 - decay) * (tables_grad * tables_grad + eps_one)
    tables_step = tables_grad * lax.rsqrt(tables_v_new)
    tables_sum = jnp.sum(tables_step * tables_step)[None, None]
    scales = tie(scale_rows[0] + scale_rows[1], lead_part)
    scales = jnp.where(at_h == 0, scales[0], scales[1]) + over_h(
        jnp.where(at_h == 0, scales[1], scales[0])
    )
    flat, ada_row = column_stats(at_c, row_new, d_stats[5:6], tail, tables_sum, scales, grads, decay)
    d_stats_new = jnp.concatenate([row_new, ada_row[:1]], 0)
    if g_count == 4:
        flat = flat + over_c(flat)
        flat = flat + over_g(flat, 1)
        flat = flat + over_g(flat, 2)
    else:
        flat = lax.psum(flat, DP)
    col_old = jnp.concatenate(
        [qkv_stat.reshape(-1), proj_stat, fc1_stat, fc2_stat, head_stat, ada_stat]
    )[None, :]
    heads = head_scale.shape[0]
    scale_line = jnp.pad(scale_v, (11, 128 - 11 - heads), constant_values=1.0)[None, :]
    col_line, part_line, own_line, second_line, scale_step = finish(
        flat, col_old, scale_line, decay, width, starts
    )
    col_new = [col_line[0, starts[k] : starts[k + 1]] for k in range(6)]
    line = flat[:1, starts[6] :]
    scale_grad = line[0, 11 : 11 + heads]
    loss_sum = line[0, 22]
    scale_v_new = second_line[0, 11 : 11 + heads]
    entries = [width * wide[k] for k in range(6)] + [table_rows * width, heads * mp_count]
    news = renew(
        (line, over_mp(part_line), own_line, early_line),
        d_stats_new,
        col_line,
        grads,
        (tables_step, scale_step),
        (
            qkv_w, proj_w, fc1_w, fc2_w, head_w, ada_w, tables,
            jnp.pad(head_scale, (11, 128 - 11 - heads))[None, :],
        ),
        width,
        entries,
        starts,
    )
    return (
        loss_sum,
        weight_sum,
        qkv_grad,
        news[8],
        fc1_grad,
        news[9],
        head_grad,
        ada_grad,
        tables_grad,
        scale_grad,
        d_stats_new,
        col_new[0].reshape(3, -1),
        col_new[1],
        col_new[2],
        col_new[3],
        col_new[4],
        col_new[5],
        tables_v_new,
        scale_v_new,
        news[0],
        news[1],
        news[2],
        news[3],
        news[4],
        news[5],
        news[6],
        news[7][0, 11 : 11 + heads],
    )


def solution(mesh):
    inner = Mesh(
        mesh.devices.reshape(mesh.shape["dp"] // 2, 2, mesh.shape["mp"] // 2, 2),
        ("g", "c", "h", "l"),
    )
    return jax.shard_map(
        body,
        mesh=inner,
        in_specs=(
            P(DP, None, None),
            P(DP, None),
            P(DP, None),
            P(DP, None),
            P(DP, None),
            P(),
            P(None, DP, MP),
            P(MP, DP),
            P(DP, MP),
            P(MP, DP),
            P(DP, MP),
            P(DP, None),
            P(None, DP),
            P(MP),
            P(None, DP),
            P(None, MP),
            P(MP),
            P(MP),
            P(MP),
            P(MP),
            P(),
            P(None, DP),
            P(MP),
        ),
        out_specs=(
            P(),
            P(),
            P(None, DP, MP),
            P(MP, DP),
            P(DP, MP),
            P(MP, DP),
            P(DP, MP),
            P(DP, None),
            P(None, DP),
            P(MP),
            P(None, DP),
            P(None, MP),
            P(MP),
            P(MP),
            P(MP),
            P(MP),
            P(),
            P(None, DP),
            P(MP),
            P(None, DP, MP),
            P(MP, DP),
            P(DP, MP),
            P(MP, DP),
            P(DP, MP),
            P(DP, None),
            P(None, DP),
            P(MP),
        ),
        check_vma=False,
    )
```

```python
import functools
import math

import jax
import jax.numpy as jnp
from jax import lax
from jax.experimental import pallas as pl
from jax.experimental.pallas import tpu as pltpu
from jax.sharding import Mesh, PartitionSpec as P

STEP = 8
level_starts = (1, 5, 14, 30, 55, 91, 155, 255, 424)
eps_norm = 1e-06
eps_one = 1e-30
eps_two = 0.001
rate_step = 0.3
clip_rms = 1.0
low_type = jnp.bfloat16
full_type = jnp.float32
high = lax.Precision.HIGH
highest = lax.Precision.HIGHEST
swap_pairs = ((0, 1), (1, 0))
busy_us = {
    "row_layout": 2, "enter": 5, "enter_first": 6, "attend": 11, "onward": 2, "feed": 5, "head": 6, "merge": 2,
    "head_back": 5, "back": 5, "feed_back": 7, "attend_back": 16, "old_stats": 2, "row_stats": 3,
    "column_stats": 5, "finish": 2, "head_grad": 6, "feed_grad": 12, "first_grad": 6,
    "renew": 8, "arrange": 2,
}
DP = ("g", "c")
MP = ("h", "l")


def cost(name):
    return pl.CostEstimate(flops=busy_us[name] * 10**9, transcendentals=0, bytes_accessed=busy_us[name] * 10**6)


def low(a):
    return a.astype(low_type)


def full(a):
    return a.astype(full_type)


def dot_nn(a, b, precision=None):
    return jnp.dot(a, b, preferred_element_type=full_type, precision=precision)


def dot_nt(a, b, precision=None):
    return lax.dot_general(
        a, b, (((1,), (1,)), ((), ())), preferred_element_type=full_type, precision=precision
    )


def dot_tn(a, b, precision=None):
    return lax.dot_general(
        a, b, (((0,), (0,)), ((), ())), preferred_element_type=full_type, precision=precision
    )


def over_c(a):
    return lax.ppermute(a, "c", swap_pairs)


def over_l(a):
    return lax.ppermute(a, "l", swap_pairs)


def over_h(a):
    return lax.ppermute(a, "h", swap_pairs)


def over_cl(a):
    return lax.ppermute(a, ("c", "l"), [(i, i ^ 3) for i in range(4)])


def over_g(a, k):
    return lax.ppermute(a, "g", [(i, i ^ k) for i in range(lax.axis_size("g"))])


def ordered(flag, mine, other, axis):
    return jnp.where(
        flag == 0,
        jnp.concatenate([mine, other], axis),
        jnp.concatenate([other, mine], axis),
    )


def gather_g(a):
    count = lax.axis_size("g")
    if count != 4:
        return lax.all_gather(a, "g", axis=0, tiled=True)
    here = lax.axis_index("g")
    out = jnp.zeros((4,) + a.shape, a.dtype)
    for k in range(4):
        piece = a if k == 0 else over_g(a, k)
        out = lax.dynamic_update_index_in_dim(out, piece, here ^ k, 0)
    return out.reshape((4 * a.shape[0],) + a.shape[1:])


def scatter_g(a):
    count = lax.axis_size("g")
    if count != 4:
        return full(lax.psum_scatter(a, "g", scatter_dimension=0, tiled=True))
    here = lax.axis_index("g")
    blocks = a.reshape((4, a.shape[0] // 4) + a.shape[1:])
    total = full(lax.dynamic_index_in_dim(blocks, here, 0, False))
    for k in range(1, 4):
        total = total + full(over_g(lax.dynamic_index_in_dim(blocks, here ^ k, 0, False), k))
    return total


def tie(a, *others):
    return lax.optimization_barrier((a,) + others)[0]


def centre(values):
    centered = values - jnp.mean(values, -1, keepdims=True)
    scale = lax.rsqrt(jnp.mean(centered * centered, -1, keepdims=True) + eps_norm)
    return centered * scale, scale


def centre_back(normed, scale, incoming):
    return (
        incoming
        - jnp.mean(incoming, -1, keepdims=True)
        - normed * jnp.mean(incoming * normed, -1, keepdims=True)
    ) * scale


def gelu_parts(values):
    root = math.sqrt(2.0 / math.pi)
    square = values * values
    bent = jnp.tanh(values * (root + (root * 0.044715) * square))
    half = 0.5 + 0.5 * bent
    slope = half + values * (0.5 - 0.5 * (bent * bent)) * (root + (root * 3.0 * 0.044715) * square)
    return values * half, slope


def split_parts(a, count):
    parts = []
    for _ in range(count):
        parts.append(low(a))
        a = a - full(parts[-1])
    return parts


def item_parts(vectors):
    return jnp.concatenate(split_parts(vectors, 3) + [jnp.zeros(vectors.shape, low_type)], 0)


def item_sums(hot, values):
    upper, lower = split_parts(values, 2)
    return (dot_tn(hot, upper) + dot_tn(hot, lower))[:8]


def whole(shape):
    return pl.BlockSpec(shape, lambda i: (0,) * len(shape), pipeline_mode=pl.Buffered(1))


def tiled(tile, columns):
    return pl.BlockSpec((tile, columns), lambda i: (i, 0))


def call(kernel, grid, in_specs, out_specs, out_shape, scratch, name):
    return pl.pallas_call(
        kernel,
        grid=grid,
        in_specs=in_specs,
        out_specs=out_specs,
        out_shape=[jax.ShapeDtypeStruct(shape, dtype) for shape, dtype in out_shape],
        scratch_shapes=scratch,
        compiler_params=pltpu.CompilerParams(vmem_limit_bytes=62 * 2**20),
        cost_estimate=cost(name),
        name=name,
    )


def rows_kernel(lw_ref, seg_ref, live_ref, place_ref, weight_ref, sum_ref):
    seg, live = seg_ref[...], live_ref[...]
    at = lax.broadcasted_iota(jnp.int32, seg.shape, 1)
    first = jnp.zeros_like(seg)
    for item in range(1, 4):
        count = jnp.sum(full(jnp.where(seg < item, 1, 0)), 1, keepdims=True).astype(jnp.int32)
        first = jnp.where(seg == item, count, first)
    within = at - first
    level = jnp.zeros_like(seg)
    for start in level_starts:
        level = level + jnp.where(within >= start, 1, 0)
    weight = jnp.zeros_like(seg)
    for position in range(lw_ref.shape[0]):
        weight = jnp.where(level == position, lw_ref[position], weight)
    weight = weight * live
    place_ref[...] = seg * 16 + level
    weight_ref[...] = weight
    each = jnp.sum(full(weight), 1, keepdims=True)
    sum_ref[...] = jnp.sum(each, 0, keepdims=True).astype(jnp.int32)


def row_layout(level_weight, segment, live):
    shape = segment.shape
    return pl.pallas_call(
        rows_kernel,
        in_specs=[pl.BlockSpec(memory_space=pltpu.SMEM)] + [pl.BlockSpec(memory_space=pltpu.VMEM)] * 2,
        out_shape=[
            jax.ShapeDtypeStruct(shape, jnp.int32),
            jax.ShapeDtypeStruct(shape, jnp.int32),
            jax.ShapeDtypeStruct((1, 1), jnp.int32),
        ],
        compiler_params=pltpu.CompilerParams(vmem_limit_bytes=62 * 2**20),
        cost_estimate=cost("row_layout"),
        name="row_layout",
    )(level_weight, segment, live)


def arrange_kernel(at_ref, mine_ref, other_ref, vq_ref, vq_other_ref, *refs):
    quarter = mine_ref.shape[2] // 4
    cols_s, vq_s = refs[-2:]
    use_mine, at_c, at_l = at_ref[0], at_ref[1], at_ref[2]
    n = 4 * quarter
    lane = lax.broadcasted_iota(jnp.int32, (n, 128), 1)
    for r in range(2):
        feat_ref, hot_ref, col_ref, row_ref = refs[4 * r : 4 * r + 4]
        info = jnp.where(use_mine == 1, mine_ref[r], other_ref[r])
        cols_s[...] = jnp.concatenate([info, jnp.zeros((124, n), full_type)], 0).T
        vq_s[...] = jnp.where(use_mine == 1, full(vq_ref[r]), full(vq_other_ref[r]))
        cols, vqs = [], []
        for k in range(4):
            start = jnp.bitwise_xor(at_c, k // 2) * 2 + jnp.bitwise_xor(at_l, k % 2)
            rows = pl.ds(pl.multiple_of(start * quarter, quarter), quarter)
            cols.append(cols_s[rows, :])
            vqs.append(vq_s[rows, :])
        cols = jnp.concatenate(cols, 0)
        code, place, live, weight = (cols[:, k : k + 1] for k in range(4))
        segment = jnp.floor(place * (1.0 / 16.0))
        base = segment * 16.0
        key = jnp.where(live > 0.0, place, 1048576.0)
        out = jnp.zeros((n, 128), full_type)
        for k, column in enumerate((place, base, key, code, weight)):
            out = jnp.where(lane == k, column, out)
        col_ref[...] = out
        row_ref[...] = out.T[0:8, :]
        spot = lax.broadcasted_iota(jnp.int32, (n, 16), 1)
        hit = (full(spot % 4) == segment) & (spot < 12)
        hot_ref[...] = low(jnp.where(hit, 1.0, 0.0))
        code_dim, padded = vq_ref.shape[2], feat_ref.shape[1]
        spread = lax.broadcasted_iota(jnp.int32, (code_dim, padded), 0) == lax.broadcasted_iota(
            jnp.int32, (code_dim, padded), 1
        )
        feats = dot_nn(low(jnp.concatenate(vqs, 0)), low(jnp.where(spread, 1.0, 0.0)))
        level = lax.broadcasted_iota(jnp.int32, (n, padded), 1) - code_dim
        feat_ref[...] = low(feats + jnp.where(full(level) == place - base, 1.0, 0.0))


def arrange(at, mine, other, vq, vq_other, padded):
    n, code_dim = vq.shape[1:]
    shapes = [((n, padded), low_type), ((n, 16), low_type), ((n, 128), full_type), ((8, n), full_type)] * 2
    return pl.pallas_call(
        arrange_kernel,
        in_specs=[pl.BlockSpec(memory_space=pltpu.SMEM)] + [pl.BlockSpec(memory_space=pltpu.VMEM)] * 4,
        out_shape=[jax.ShapeDtypeStruct(shape, dtype) for shape, dtype in shapes],
        scratch_shapes=[pltpu.VMEM((n, 128), full_type), pltpu.VMEM((n, code_dim), full_type)],
        compiler_params=pltpu.CompilerParams(vmem_limit_bytes=62 * 2**20),
        cost_estimate=cost("arrange"),
        name="arrange",
    )(at, mine, other, vq, vq_other)


def enter_tile(feat_ref, table_ref, hot_ref, w, in_ref, qkv_ref, stream_ref, parts_s):
    stream = dot_nn(feat_ref[...], table_ref[...])

    @pl.when(pl.program_id(0) == 0)
    def _():
        stream_ref[...] = stream[: stream_ref.shape[0]]

    normed, _ = centre(stream)
    hot = hot_ref[...]
    given = low(normed * (1.0 + dot_nn(hot, parts_s[1])) + dot_nn(hot, parts_s[0]))
    in_ref[...] = given
    qkv_ref[...] = dot_nn(given, w)


def enter_parts(mod_ref, parts_s):
    parts_s[0] = item_parts(mod_ref[0])
    parts_s[1] = item_parts(mod_ref[1])


def enter_kernel(feat_ref, table_ref, hot_ref, mod_ref, w_ref, in_ref, qkv_ref, stream_ref, parts_s):
    @pl.when(pl.program_id(0) == 0)
    def _():
        enter_parts(mod_ref, parts_s)

    enter_tile(feat_ref, table_ref, hot_ref, w_ref[...], in_ref, qkv_ref, stream_ref, parts_s)


def enter(feats, table, hot, mods, w):
    n, k = feats.shape
    width, columns = w.shape
    tile = n // 2
    return call(
        enter_kernel,
        (2,),
        [tiled(tile, k), whole((k, width)), tiled(tile, 16), whole(mods.shape), whole(w.shape)],
        [tiled(tile, width), tiled(tile, columns), fixed((tile // 2, width))],
        [((n, width), low_type), ((n, columns), full_type), ((tile // 2, width), full_type)],
        [pltpu.VMEM((2, 16, width), low_type)],
        "enter",
    )(feats, table, hot, mods, w)


def enter_first_kernel(
    at_ref, feat_ref, table_ref, hot_ref, mod_ref, a_ref, b_ref, c_ref, d_ref, in_ref, qkv_ref, stream_ref,
    w_ref, p_ref, parts_s
):
    @pl.when(pl.program_id(0) == 0)
    def _():
        enter_parts(mod_ref, parts_s)
        for k, ref in enumerate((a_ref, b_ref, c_ref, d_ref)):
            rows = ref.shape[2]
            start = pl.multiple_of(jnp.bitwise_xor(at_ref[0], k) * rows, rows)
            for j in range(2):
                for c in range(3):
                    w_ref[pl.ds(start, rows), (2 * c + j) * 128 : (2 * c + j + 1) * 128] = ref[j, c]
                p_ref[pl.ds(start, rows), j * 128 : (j + 1) * 128] = ref[j, 3]

    enter_tile(feat_ref, table_ref, hot_ref, w_ref[...], in_ref, qkv_ref, stream_ref, parts_s)


def enter_first(here, feats, table, hot, mods, pieces):
    n, k = feats.shape
    width = table.shape[1]
    columns = 768
    tile = n // 2
    shape = pieces[0].shape
    return call(
        enter_first_kernel,
        (n // tile,),
        [pl.BlockSpec(memory_space=pltpu.SMEM), tiled(tile, k), whole((k, width)), tiled(tile, 16), whole(mods.shape)]
        + [whole(shape)] * 4,
        [tiled(tile, width), tiled(tile, columns), fixed((tile // 2, width))]
        + [fixed((width, columns)), fixed((width, columns // 3))],
        [((n, width), low_type), ((n, columns), full_type), ((tile // 2, width), full_type)]
        + [((width, columns), low_type), ((width, columns // 3), low_type)],
        [pltpu.VMEM((2, 16, width), low_type)],
        "enter_first",
    )(here[None], feats, table, hot, mods, *pieces)


def onward_kernel(a_ref, b_ref, c_ref, x_ref, hot_ref, mod_ref, br_ref, y_ref, in_ref, parts_s, *, picks):
    @pl.when(pl.program_id(0) == 0)
    def _():
        for k, pick in enumerate(picks):
            parts_s[k] = item_parts(mod_ref[pick])

    branch = full(a_ref[...]) + full(b_ref[...]) + full(c_ref[...])
    br_ref[...] = branch
    hot = hot_ref[...]
    stream = x_ref[...] + dot_nn(hot, parts_s[0]) * branch
    y_ref[...] = stream
    normed, _ = centre(stream)
    in_ref[...] = low(normed * (1.0 + dot_nn(hot, parts_s[2])) + dot_nn(hot, parts_s[1]))


def onward(parts, stream, hot, mods, picks):
    n, width = parts[2].shape
    tile = n
    return call(
        functools.partial(onward_kernel, picks=picks),
        (n // tile,),
        [tiled(tile, width)] * 4 + [tiled(tile, 16), whole(mods.shape)],
        [tiled(tile, width)] * 3,
        [((n, width), full_type), ((n, width), full_type), ((n, width), low_type)],
        [pltpu.VMEM((3, 16, width), low_type)],
        "onward",
    )(*parts, stream, hot, mods)


def back_kernel(*refs, gated, carried, picks):
    refs = list(refs)
    a_ref, b_ref, c_ref, x_ref, hot_ref, mod_ref = refs[:6]
    del refs[:6]
    res_ref = refs.pop(0) if carried else None
    br_ref = refs.pop(0) if gated else None
    feat_ref = None if gated else refs.pop(0)
    res_out = refs.pop(0) if gated else None
    d_ref = refs.pop(0) if gated else None
    items_ref = refs.pop(0)
    lead_ref = None if gated else refs.pop(0)
    parts_s = refs.pop(0)

    @pl.when(pl.program_id(0) == 0)
    def _():
        for k, pick in enumerate(picks):
            parts_s[k] = item_parts(mod_ref[pick])
        items_ref[...] = jnp.zeros_like(items_ref)
        if not gated:
            lead_ref[...] = jnp.zeros_like(lead_ref)

    hot = hot_ref[...]
    incoming = full(a_ref[...]) + full(b_ref[...]) + full(c_ref[...])
    normed, scale = centre(x_ref[...])
    items_ref[0] += item_sums(hot, incoming)
    items_ref[1] += item_sums(hot, incoming * normed)
    res = centre_back(normed, scale, incoming * (1.0 + dot_nn(hot, parts_s[0])))
    if carried:
        res = res + res_ref[...]
    if gated:
        res_out[...] = res
        items_ref[2] += item_sums(hot, res * br_ref[...])
        d_ref[...] = low(res * dot_nn(hot, parts_s[1]))
    else:
        upper, lower = split_parts(res, 2)
        feats = feat_ref[...]
        lead_ref[...] += dot_tn(feats, upper) + dot_tn(feats, lower)


def back(parts, stream, hot, mods, picks, carried, branch, feats):
    n, width = parts[2].shape
    tile = n
    gated, has = branch is not None, carried is not None
    extra = ([carried] if has else []) + ([branch] if gated else [feats])
    specs = [tiled(tile, width)] * 4 + [tiled(tile, 16), whole(mods.shape)]
    specs += [tiled(tile, a.shape[1]) for a in extra]
    count = 3 if gated else 2
    out_specs, out_shape = [], []
    if gated:
        out_specs += [tiled(tile, width)] * 2
        out_shape += [((n, width), full_type), ((n, width), low_type)]
    out_specs.append(fixed((count, 8, width)))
    out_shape.append(((count, 8, width), full_type))
    if not gated:
        out_specs.append(fixed((feats.shape[1], width)))
        out_shape.append(((feats.shape[1], width), full_type))
    return call(
        functools.partial(back_kernel, gated=gated, carried=has, picks=picks),
        (n // tile,),
        specs,
        out_specs,
        out_shape,
        [pltpu.VMEM((2, 16, width), low_type)],
        "back",
    )(*parts, stream, hot, mods, *extra)


def either(a_ref, b_ref, c_ref, d_ref):
    top = jnp.concatenate([a_ref[...], b_ref[...]], 0)
    return jnp.where(pl.program_id(0) == 0, top, jnp.concatenate([c_ref[...], d_ref[...]], 0))


def put(value, top_ref, bottom_ref):
    @pl.when(pl.program_id(0) == 0)
    def _():
        top_ref[...] = value

    @pl.when(pl.program_id(0) == 1)
    def _():
        bottom_ref[...] = value


def fixed(shape):
    return pl.BlockSpec(shape, lambda i: (0,) * len(shape))


def column_half(shape, number):
    return pl.BlockSpec(
        shape[:3] + (shape[3] // 2,), lambda i: (0, 0, 0, number), pipeline_mode=pl.Buffered(1)
    )


def block_of(ref, h):
    return ref[:, h].reshape(-1, ref.shape[3])


def feed_kernel(a_ref, b_ref, c_ref, d_ref, one_ref, two_ref, row_ref, act_ref, slope_ref, top_ref, bottom_ref):
    given = either(a_ref, b_ref, c_ref, d_ref)
    row_ref[...] = given
    units = one_ref.shape[3]
    total = None
    for h in range(2):
        at = slice(h * units, (h + 1) * units)
        act, slope = gelu_parts(dot_nn(given, block_of(one_ref, h)))
        act = low(act)
        act_ref[:, at] = act
        slope_ref[:, at] = slope
        part = dot_nt(act, block_of(two_ref, h))
        total = part if total is None else total + part
    put(low(total), top_ref, bottom_ref)


def feed(pieces, both):
    tile, width = 2 * pieces[0].shape[0], pieces[0].shape[1]
    units = both.shape[3]
    return call(
        feed_kernel,
        (2,),
        [whole(pieces[0].shape)] * 4 + [column_half(both.shape, k) for k in range(2)],
        [tiled(tile, width), tiled(tile, units), tiled(tile, units), fixed((tile, width)), fixed((tile, width))],
        [((2 * tile, width), low_type), ((2 * tile, units), low_type), ((2 * tile, units), full_type)]
        + [((tile, width), low_type)] * 2,
        [],
        "feed",
    )(*pieces, both, both)


def feed_back_kernel(a_ref, b_ref, c_ref, d_ref, slope_ref, one_ref, two_ref, row_ref, dh_ref, top_ref, bottom_ref):
    given = either(a_ref, b_ref, c_ref, d_ref)
    row_ref[...] = given
    units = one_ref.shape[3]
    total = None
    for h in range(2):
        at = slice(h * units, (h + 1) * units)
        d_hidden = low(dot_nn(given, block_of(two_ref, h)) * slope_ref[:, at])
        dh_ref[:, at] = d_hidden
        part = dot_nt(d_hidden, block_of(one_ref, h))
        total = part if total is None else total + part
    put(low(total), top_ref, bottom_ref)


def feed_back(pieces, slope, both):
    tile, width = 2 * pieces[0].shape[0], pieces[0].shape[1]
    units = both.shape[3]
    return call(
        feed_back_kernel,
        (2,),
        [whole(pieces[0].shape)] * 4 + [tiled(tile, units)] + [column_half(both.shape, k) for k in range(2)],
        [tiled(tile, width), tiled(tile, units), fixed((tile, width)), fixed((tile, width))],
        [((2 * tile, width), low_type), ((2 * tile, units), low_type)] + [((tile, width), low_type)] * 2,
        [],
        "feed_back",
    )(*pieces, slope, both, both)


def head_kernel(a_ref, b_ref, c_ref, d_ref, w_ref, code_ref, column_ref, row_ref, logit_ref, stat_ref):
    given = either(a_ref, b_ref, c_ref, d_ref)
    row_ref[...] = given
    logits = jnp.concatenate([dot_nn(given, block_of(w_ref, h)) for h in range(2)], 1)
    logit_ref[...] = logits
    peak = jnp.max(logits, 1, keepdims=True)
    total = jnp.sum(jnp.exp(logits - peak), 1, keepdims=True)
    picked = jnp.sum(jnp.where(code_ref[:, 3:4] == column_ref[...], logits, 0.0), 1, keepdims=True)
    lane = lax.broadcasted_iota(jnp.int32, (logits.shape[0], 128), 1)
    turned = jnp.where(lane == 0, peak, jnp.where(lane == 1, total, picked)).T
    stat_ref[...] = turned[0:8, :]


def head(pieces, w, code, column):
    tile, width = 2 * pieces[0].shape[0], pieces[0].shape[1]
    units = 2 * w.shape[3]
    return call(
        head_kernel,
        (2,),
        [whole(pieces[0].shape)] * 4 + [whole(w.shape), tiled(tile, 128), whole((1, units))],
        [tiled(tile, width), tiled(tile, units), pl.BlockSpec((8, tile), lambda i: (0, i))],
        [((2 * tile, width), low_type), ((2 * tile, units), full_type), ((8, 2 * tile), full_type)],
        [],
        "head",
    )(*pieces, w, code, column)


def merge_kernel(sum_ref, here_ref, c_ref, l_ref, d_ref, weight_ref, out_ref, loss_ref):
    half = here_ref.shape[1] // 2

    def over_core(a):
        return jnp.concatenate([a[:, half:], a[:, :half]], 1)

    def over_line(a):
        return jnp.concatenate(
            [pltpu.roll(a[:, :half], half // 2, 1), pltpu.roll(a[:, half:], half // 2, 1)], 1
        )

    parts = (here_ref[...], over_core(c_ref[...]), over_line(l_ref[...]), over_core(over_line(d_ref[...])))
    peak = functools.reduce(jnp.maximum, [part[0:1] for part in parts])
    total = sum(part[1:2] * jnp.exp(part[0:1] - peak) for part in parts)
    picked = sum(part[2:3] for part in parts)
    log_total = peak + jnp.log(total)
    weight = weight_ref[4:5, :]
    spot = lax.broadcasted_iota(jnp.int32, (1, 2 * half), 1)
    loss = jnp.where(spot < half // 2, weight * (log_total - picked), 0.0)
    loss_ref[...] = jnp.broadcast_to(jnp.sum(loss, 1, keepdims=True), loss_ref.shape)
    blank = jnp.zeros((126, 2 * half), full_type)
    out_ref[...] = jnp.concatenate([log_total, weight / sum_ref[0], blank], 0).T


def merge(weight_sum, here, over_core, over_line, over_both, weights):
    n = here.shape[1]
    return pl.pallas_call(
        merge_kernel,
        in_specs=[pl.BlockSpec(memory_space=pltpu.SMEM)] + [pl.BlockSpec(memory_space=pltpu.VMEM)] * 5,
        out_shape=[jax.ShapeDtypeStruct((n, 128), full_type), jax.ShapeDtypeStruct((1, 128), full_type)],
        compiler_params=pltpu.CompilerParams(vmem_limit_bytes=62 * 2**20),
        cost_estimate=cost("merge"),
        name="merge",
    )(weight_sum[None], here, over_core, over_line, over_both, weights)


def head_back_kernel(logit_ref, w_ref, code_ref, column_ref, line_ref, d_ref, top_ref, bottom_ref):
    hit = jnp.where(code_ref[:, 3:4] == column_ref[...], 1.0, 0.0)
    line = line_ref[...]
    d_logits = low(line[:, 1:2] * (jnp.exp(logit_ref[...] - line[:, 0:1]) - hit))
    d_ref[...] = d_logits
    units = w_ref.shape[3]
    total = dot_nt(d_logits[:, :units], block_of(w_ref, 0)) + dot_nt(d_logits[:, units:], block_of(w_ref, 1))
    put(low(total), top_ref, bottom_ref)


def head_back(logits, w, code, column, lines):
    n, units = logits.shape
    width = w.shape[0] * w.shape[2]
    tile = n // 2
    return call(
        head_back_kernel,
        (2,),
        [tiled(tile, units), whole(w.shape), tiled(tile, 128), whole((1, units)), tiled(tile, 128)],
        [tiled(tile, units), fixed((tile, width)), fixed((tile, width))],
        [((n, units), low_type)] + [((tile, width), low_type)] * 2,
        [],
        "head_back",
    )(logits, w, code, column, lines)


def old_stats_kernel(qkv_ref, proj_ref, one_ref, two_ref, head_ref, ada_ref, tab_ref, scale_ref, out_ref):
    def total(values):
        return jnp.sum(jnp.sum(values * values, 1, keepdims=True), 0, keepdims=True)

    spot = lax.broadcasted_iota(jnp.int32, (1, 128), 1)
    line = jnp.zeros((1, 128), full_type)
    sums = [sum(total(qkv_ref[c]) for c in range(3))]
    sums += [total(ref[...]) for ref in (proj_ref, one_ref, two_ref, head_ref, scale_ref)]
    for k, value in enumerate(sums):
        line = jnp.where(spot == 16 + k, value, line)
    out_ref[0:1, :] = line
    line = jnp.where(spot == 8, total(ada_ref[...]), 0.0)
    out_ref[1:2, :] = jnp.where(spot == 9, total(tab_ref[...]), line)


def old_stats(*olds):
    return pl.pallas_call(
        old_stats_kernel,
        out_shape=jax.ShapeDtypeStruct((2, 128), full_type),
        compiler_params=pltpu.CompilerParams(vmem_limit_bytes=62 * 2**20),
        cost_estimate=cost("old_stats"),
        name="old_stats",
    )(*olds)


def put_rows(out_ref, start, value):
    groups, _, rows, _ = out_ref.shape
    for g in range(groups):
        out_ref[g, 0, :, start : start + value.shape[1]] = value[g * rows : (g + 1) * rows]


def head_grad_kernel(a_ref, b_ref, c_ref, d_ref, out_ref):
    put_rows(out_ref, 0, low(dot_tn(a_ref[...], c_ref[...]) + dot_tn(b_ref[...], d_ref[...])))


def head_grad_of(inputs, wanted, groups):
    n, width = inputs[0].shape
    columns = wanted[0].shape[1] // 2
    block = pl.BlockSpec((n, columns), lambda i: (0, i))
    return call(
        head_grad_kernel,
        (2,),
        [whole((n, width))] * 2 + [block] * 2,
        [pl.BlockSpec((groups, 1, width // groups, columns), lambda i: (0, i, 0, 0))],
        [((groups, 2, width // groups, columns), low_type)],
        [],
        "head_grad",
    )(*inputs, *wanted)[0]


def feed_grad_kernel(a_ref, b_ref, c_ref, d_ref, e_ref, f_ref, g_ref, h_ref, out_ref):
    @pl.when(pl.program_id(0) < 2)
    def _():
        put_rows(out_ref, 0, low(dot_tn(a_ref[...], c_ref[...]) + dot_tn(b_ref[...], d_ref[...])))

    @pl.when(pl.program_id(0) >= 2)
    def _():
        put_rows(out_ref, 0, low(dot_tn(e_ref[...], g_ref[...]) + dot_tn(f_ref[...], h_ref[...])))


def feed_grad_of(inputs, d_hidden, d_branch, acts, groups):
    n, width = inputs[0].shape
    columns = acts[0].shape[1] // 2
    early = pl.BlockSpec((n, columns), lambda i: (0, jnp.minimum(i, 1)))
    late = pl.BlockSpec((n, columns), lambda i: (0, jnp.maximum(i - 2, 0)))
    return call(
        feed_grad_kernel,
        (4,),
        [whole((n, width))] * 2 + [early] * 2 + [whole((n, width))] * 2 + [late] * 2,
        [pl.BlockSpec((groups, 1, width // groups, columns), lambda i: (0, i % 2, 0, i // 2))],
        [((groups, 2, width // groups, 2 * columns), low_type)],
        [],
        "feed_grad",
    )(*inputs, *d_hidden, *d_branch, *acts)[0]


def first_grad_kernel(a_ref, b_ref, c_ref, d_ref, e_ref, f_ref, g_ref, h_ref, out_ref):
    group = c_ref.shape[1] // 3
    start = pl.program_id(0) * 128

    def columns(ref):
        return jnp.concatenate(
            [ref[:, pl.ds(pl.multiple_of(start + c * group, 128), 128)] for c in range(3)], 1
        )

    put_rows(out_ref, 0, low(dot_tn(a_ref[...], columns(c_ref)) + dot_tn(b_ref[...], columns(d_ref))))
    put_rows(out_ref, 384, low(dot_tn(e_ref[...], g_ref[...]) + dot_tn(f_ref[...], h_ref[...])))


def first_grad_of(inputs, d_qkv, d_branch, mixed, groups):
    n, width = inputs[0].shape
    return call(
        first_grad_kernel,
        (2,),
        [whole((n, width))] * 2 + [whole(d_qkv[0].shape)] * 2 + [whole((n, width))] * 2
        + [pl.BlockSpec((n, 128), lambda i: (0, i))] * 2,
        [pl.BlockSpec((groups, 1, width // groups, 512), lambda i: (0, i, 0, 0))],
        [((groups, 2, width // groups, 512), low_type)],
        [],
        "first_grad",
    )(*inputs, *d_qkv, *d_branch, *mixed)[0]


def row_stats_kernel(qkv_ref, proj_ref, one_ref, two_ref, head_ref, out_ref):
    n = out_ref.shape[1]
    lane = lax.broadcasted_iota(jnp.int32, (n, 128), 1)
    out = jnp.zeros((n, 128), full_type)
    qkv = sum(jnp.sum(qkv_ref[c] * qkv_ref[c], 1, keepdims=True) for c in range(3))
    sums = [qkv + 3 * qkv_ref.shape[2] * eps_one]
    for ref in (proj_ref, one_ref, two_ref, head_ref):
        values = ref[...]
        sums.append(jnp.sum(values * values, 1, keepdims=True) + ref.shape[1] * eps_one)
    for k, column in enumerate(sums):
        out = jnp.where(lane == k, column, out)
    out_ref[...] = out.T[0:8, :]


def row_stats(*gradients):
    n = gradients[1].shape[0]
    return pl.pallas_call(
        row_stats_kernel,
        out_shape=jax.ShapeDtypeStruct((8, n), full_type),
        compiler_params=pltpu.CompilerParams(vmem_limit_bytes=62 * 2**20),
        cost_estimate=cost("row_stats"),
        name="row_stats",
    )(*gradients)


def column_stats_kernel(
    at_ref, row_ref, old_ref, tail_ref, tables_ref, scale_ref, qkv_ref, proj_ref, one_ref, two_ref, head_ref, ada_ref, out_ref, new_ref, *, decay
):
    n = proj_ref.shape[0]
    rows = row_ref[...]
    padded = jnp.concatenate([rows, jnp.zeros((128 - rows.shape[0], n), full_type)], 0).T
    at = 0
    pieces = [(qkv_ref[c], 0) for c in range(3)]
    pieces += [(ref[...], k + 1) for k, ref in enumerate((proj_ref, one_ref, two_ref, head_ref))]
    for values, k in pieces:
        square = values * values
        columns = square.shape[1]
        out_ref[0:1, at : at + columns] = jnp.sum(square, 0, keepdims=True) + n * eps_one
        out_ref[1:2, at : at + columns] = jnp.sum(
            square * (1.0 / padded[:, k : k + 1]), 0, keepdims=True
        )
        at += columns
    columns = ada_ref.shape[1]
    step = 1024
    total = jnp.zeros((n, 1), full_type)
    for start in range(0, columns, step):
        values = ada_ref[:, start : start + step]
        total = total + jnp.sum(values * values, 1, keepdims=True)
    old = jnp.concatenate([old_ref[...], jnp.zeros((127, n), full_type)], 0).T[:, 0:1]
    row = decay * old + (1.0 - decay) * (total / columns + eps_one)
    lane = lax.broadcasted_iota(jnp.int32, (n, 128), 1)
    new_ref[...] = jnp.where(lane == 0, row, 0.0).T[0:8, :]
    for start in range(0, columns, step):
        values = ada_ref[:, start : start + step]
        square = values * values
        out_ref[0:1, at : at + step] = jnp.sum(square, 0, keepdims=True) + n * eps_one
        out_ref[1:2, at : at + step] = jnp.sum(square * (1.0 / row), 0, keepdims=True)
        at += step
    spots = lax.broadcasted_iota(jnp.int32, (1, 128), 1)
    line = tail_ref[...]
    for k in range(5):
        line = jnp.where(spots == k, jnp.sum(rows[k : k + 1, :], 1, keepdims=True), line)
    line = jnp.where(spots == 5, jnp.sum(row, 0, keepdims=True), line)
    line = jnp.where(spots == 10, tables_ref[...], line)
    scales = scale_ref[...]
    for k in range(2):
        value = jnp.sum(jnp.where((spots < 64) == (k == 0), scales, 0.0), 1, keepdims=True)
        line = jnp.where(spots == 11 + k + 2 * at_ref[0], value, line)
    out_ref[0:1, at : at + 128] = line
    out_ref[1:2, at : at + 128] = jnp.zeros_like(line)


def column_stats(at_c, row_new, old, tail, tables_sum, scales, gradients, decay):
    n = gradients[1].shape[0]
    columns = sum(g.size // n for g in gradients)
    return pl.pallas_call(
        functools.partial(column_stats_kernel, decay=decay),
        out_shape=[
            jax.ShapeDtypeStruct((2, columns + 128), full_type),
            jax.ShapeDtypeStruct((8, n), full_type),
        ],
        in_specs=[pl.BlockSpec(memory_space=pltpu.SMEM)]
        + [pl.BlockSpec(memory_space=pltpu.VMEM)] * (5 + len(gradients)),
        compiler_params=pltpu.CompilerParams(vmem_limit_bytes=62 * 2**20),
        cost_estimate=cost("column_stats"),
        name="column_stats",
    )(at_c[None], row_new, old, tail, tables_sum, scales, *gradients)


def spot_of(line, k):
    spots = lax.broadcasted_iota(jnp.int32, line.shape, 1)
    return jnp.sum(jnp.where(spots == k, line, 0.0), 1, keepdims=True)


def finish_kernel(
    flat_ref, old_ref, scale_ref, col_ref, part_ref, own_ref, second_ref, step_ref, *, decay, width, starts
):
    columns = old_ref.shape[1]
    line = flat_ref[0:1, columns:]
    new = decay * old_ref[...] + (1.0 - decay) * (flat_ref[0:1, :columns] / width)
    col_ref[...] = new
    ratio = flat_ref[1:2, :columns] / new
    spots = lax.broadcasted_iota(jnp.int32, (1, 128), 1)
    scales = (spots >= 11) & (spots < 15)
    gradient = jnp.where(scales, line, 0.0)
    second = decay * scale_ref[...] + (1.0 - decay) * (gradient * gradient + eps_one)
    step = gradient * lax.rsqrt(second)
    second_ref[...] = second
    step_ref[...] = step
    out = jnp.where(spots == 7, jnp.sum(step * step, 1, keepdims=True), 0.0)
    for k in range(6):
        value = jnp.sum(ratio[:, starts[k] : starts[k + 1]], 1, keepdims=True) * (spot_of(line, k) / width)
        if k == 5:
            own_ref[...] = jnp.where(spots == 5, value, 0.0)
        else:
            out = jnp.where(spots == k, value, out)
    part_ref[...] = out


def finish(flat, col_old, scale_line, decay, width, starts):
    return pl.pallas_call(
        functools.partial(finish_kernel, decay=decay, width=width, starts=starts),
        out_shape=[jax.ShapeDtypeStruct(col_old.shape, full_type)]
        + [jax.ShapeDtypeStruct((1, 128), full_type)] * 4,
        compiler_params=pltpu.CompilerParams(vmem_limit_bytes=62 * 2**20),
        cost_estimate=cost("finish"),
        name="finish",
    )(flat, col_old, scale_line)


def renew_kernel(
    line_ref, part_ref, own_ref, early_ref, rows_ref, col_ref, ada_col_ref,
    qkv_g, proj_g, one_g, two_g, head_g, ada_g, step_ref, scale_step_ref,
    qkv_ref, proj_ref, one_ref, two_ref, head_ref, ada_ref, tab_ref, scale_ref,
    qkv_out, proj_out, one_out, two_out, head_out, ada_out, tab_out, scale_out, proj_turned, two_turned,
    *, width, entries, starts
):
    n = one_g.shape[0]
    line, part = line_ref[...], part_ref[...]

    def factor(k):
        step = spot_of(own_ref[...], 5) if k == 5 else spot_of(line, 10) if k == 6 else spot_of(part, k)
        weight = spot_of(early_ref[...], 21) if k == 7 else spot_of(line, {5: 8, 6: 9}.get(k, 16 + k))
        ratio = jnp.sqrt(step / entries[k]) / clip_rms
        spread = jnp.maximum(eps_two, jnp.sqrt(weight / entries[k]))
        return rate_step * spread / jnp.maximum(1.0, ratio)

    def row(k):
        rows = jnp.concatenate([rows_ref[k : k + 1, :], jnp.zeros((127, n), full_type)], 0)
        return rows.T[:, 0:1]

    def change(k, gradient, columns):
        mean = spot_of(line, k) / width
        return factor(k) * (gradient * lax.rsqrt(row(k) * columns / mean))

    ada_out[...] = ada_ref[...] - change(5, ada_g[...], ada_col_ref[...])
    at = pl.program_id(0)

    @pl.when(at == 0)
    def _():
        size = qkv_g.shape[2]
        for c in range(3):
            qkv_out[c] = qkv_ref[c] - change(0, qkv_g[c], col_ref[:, c * size : (c + 1) * size])

    @pl.when(at == 1)
    def _():
        gradient = proj_g[...]
        proj_turned[...] = gradient.T
        proj_out[...] = proj_ref[...] - change(1, gradient, col_ref[:, starts[1] : starts[2]]).T
        scale_out[...] = scale_ref[...] - factor(7) * scale_step_ref[...]

    @pl.when(at == 2)
    def _():
        one_out[...] = one_ref[...] - change(2, one_g[...], col_ref[:, starts[2] : starts[3]])

    @pl.when(at == 3)
    def _():
        gradient = two_g[...]
        two_turned[...] = gradient.T
        two_out[...] = two_ref[...] - change(3, gradient, col_ref[:, starts[3] : starts[4]]).T

    @pl.when(at == 4)
    def _():
        head_out[...] = head_ref[...] - change(4, head_g[...], col_ref[:, starts[4] : starts[5]])

    @pl.when(at == 5)
    def _():
        tab_out[...] = tab_ref[...] - factor(6) * step_ref[...]


def renew(lines, rows, columns, grads, steps, olds, width, entries, starts):
    n, tile = grads[2].shape[0], 1024
    ada = pl.BlockSpec((n, tile), lambda i: (0, i))
    first = starts[5] // tile

    def wholes(arrays):
        return [whole(a.shape) for a in arrays]

    outs = [a.shape for a in olds] + [olds[1].shape, olds[3].shape]
    out_specs = [ada if k == 5 else fixed(shape) for k, shape in enumerate(outs)]
    return call(
        functools.partial(renew_kernel, width=width, entries=entries, starts=starts),
        (olds[5].shape[1] // tile,),
        wholes(lines)
        + [whole(rows.shape), whole(columns.shape), pl.BlockSpec((1, tile), lambda i: (0, first + i))]
        + wholes(grads[:5])
        + [ada]
        + wholes(steps)
        + wholes(olds[:5])
        + [ada]
        + wholes(olds[6:]),
        out_specs,
        [(shape, full_type) for shape in outs],
        [],
        "renew",
    )(*lines, rows, columns, columns, *grads, *steps, *olds)


def head_lanes(shape):
    return lax.broadcasted_iota(jnp.int32, shape, len(shape) - 1) < 64


def per_head(values, first):
    left = jnp.sum(jnp.where(first, values, 0.0), -1, keepdims=True)
    right = jnp.sum(jnp.where(first, 0.0, values), -1, keepdims=True)
    return jnp.where(first, left, right)


def attend_kernel(
    q_ref, k_ref, v_ref, gain_ref, col_ref, row_ref, proj_ref,
    mix_ref, lse_ref, top_ref, bottom_ref, q_s, k_s, v_s, bias_s, sum_s
):
    length = q_ref.shape[0]
    tile = length // 2
    first = head_lanes((length, 128))
    query = q_ref[...]
    key = k_ref[...]
    q_s[...] = low(
        query * (lax.rsqrt(per_head(query * query, first) / 64.0 + eps_norm) * gain_ref[...])
    )
    k_s[...] = low(key * (lax.rsqrt(per_head(key * key, first) / 64.0 + eps_norm) * 0.125))
    v_s[...] = low(v_ref[...])
    first_t = head_lanes((tile, 128))

    @pl.when(pl.program_id(0) == 0)
    def _():
        ck = row_ref[2:3, :]
        for i in range(2):
            rows = slice(i * tile, (i + 1) * tile)
            shape = (tile, length)
            here = lax.broadcasted_iota(jnp.int32, shape, 1) - lax.broadcasted_iota(jnp.int32, shape, 0)
            keep = ((ck <= col_ref[rows, 0:1]) & (ck >= col_ref[rows, 1:2])) | (here == i * tile)
            bias_s[rows, :] = jnp.where(keep, 0.0, -1e30)
        sum_s[...] = jnp.zeros_like(sum_s)

    for i, out_ref in enumerate((top_ref, bottom_ref)):
        rows = slice(i * tile, (i + 1) * tile)
        query_t = q_s[rows, :]
        mixed, logs = [], []
        for head in range(2):
            chosen = first_t if head == 0 else ~first_t
            scores = dot_nt(jnp.where(chosen, query_t, jnp.zeros_like(query_t)), k_s[...]) + bias_s[rows, :]
            exponent = jnp.exp(scores)
            total = jnp.sum(exponent, -1, keepdims=True)
            mixed.append(dot_nn(low(exponent * (1.0 / total)), v_s[...]))
            logs.append(jnp.log(total))
        mixed = low(jnp.where(first_t, mixed[0], mixed[1]))
        mix_ref[rows, :] = mixed
        turned = jnp.where(first_t, logs[0], logs[1]).T
        lse_ref[0, 0:1, rows] = turned[0:1, :]
        lse_ref[0, 1:2, rows] = turned[64:65, :]
        part = sum_s[rows, :] + dot_nt(mixed, proj_ref[...])
        sum_s[rows, :] = part

        @pl.when(pl.program_id(0) == pl.num_programs(0) - 1)
        def _():
            out_ref[...] = low(part)


def attend(qkv, gain, cols, rows, proj):
    length = qkv.shape[0]
    pairs = qkv.shape[1] // 384
    width = proj.shape[0]
    block = pl.BlockSpec((length, 128), lambda p: (0, p))
    return call(
        attend_kernel,
        (pairs,),
        [
            block,
            pl.BlockSpec((length, 128), lambda p: (0, pairs + p)),
            pl.BlockSpec((length, 128), lambda p: (0, 2 * pairs + p)),
            pl.BlockSpec((1, 128), lambda p: (0, p)),
            whole((length, 128)),
            whole((8, length)),
            pl.BlockSpec((width, 128), lambda p: (0, p)),
        ],
        [block, pl.BlockSpec((1, 2, length), lambda p: (p, 0, 0))] + [fixed((length // 2, width))] * 2,
        [((length, 128 * pairs), low_type), ((pairs, 2, length), full_type)]
        + [((length // 2, width), low_type)] * 2,
        [pltpu.VMEM((length, 128), low_type)] * 3
        + [pltpu.VMEM((length, length), full_type), pltpu.VMEM((length, width), full_type)],
        "attend",
    )(qkv, qkv, qkv, gain, cols, rows, proj)


def attend_back_kernel(
    q_ref, k_ref, v_ref, gain_ref, col_ref, line_ref, lse_ref, pa_ref, pb_ref, pc_ref, pd_ref,
    proj_ref, wq_ref, wk_ref, wv_ref, row_ref, d_ref, ds_ref, top_ref, bottom_ref,
    q_s, k_s, v_s, dm_ref, dqa, dka, dva, bias_s, sum_s
):
    length = q_ref.shape[0]
    first = head_lanes((length, 128))
    query = q_ref[...]
    key = k_ref[...]
    gain = gain_ref[...]
    q_n = lax.rsqrt(per_head(query * query, first) / 64.0 + eps_norm)
    k_n = lax.rsqrt(per_head(key * key, first) / 64.0 + eps_norm)
    q_s[...] = low(query * (q_n * gain))
    k_s[...] = low(key * (k_n * 0.125))
    v_s[...] = low(v_ref[...])
    quarter = length // 4
    for k, ref in enumerate((pa_ref, pb_ref, pc_ref, pd_ref)):
        rows = slice(k * quarter, (k + 1) * quarter)
        dm_ref[rows, :] = low(dot_nn(ref[...], proj_ref[...]))

    @pl.when(pl.program_id(0) == 0)
    def _():
        sum_s[...] = jnp.zeros_like(sum_s)
        for k, ref in enumerate((pa_ref, pb_ref, pc_ref, pd_ref)):
            row_ref[k * quarter : (k + 1) * quarter, :] = ref[...]

    tile = length // 2
    first_t = head_lanes((tile, 128))

    @pl.when(pl.program_id(0) == 0)
    def _():
        ck = col_ref[:, 2:3]
        for i in range(2):
            rows = slice(i * tile, (i + 1) * tile)
            shape = (length, tile)
            here = lax.broadcasted_iota(jnp.int32, shape, 0) - lax.broadcasted_iota(jnp.int32, shape, 1)
            keep = ((ck <= line_ref[0:1, rows]) & (ck >= line_ref[1:2, rows])) | (here == i * tile)
            bias_s[:, rows] = jnp.where(keep, 0.0, -1e30)

    d_keys, d_values = None, None
    for i in range(2):
        rows = slice(i * tile, (i + 1) * tile)
        query_t = q_s[rows, :]
        dmix_t = dm_ref[rows, :]
        d_query = []
        for head in range(2):
            chosen = first_t if head == 0 else ~first_t
            zero = jnp.zeros_like(query_t)
            query_h = jnp.where(chosen, query_t, zero)
            dmix_h = jnp.where(chosen, dmix_t, zero)
            scores = dot_nt(k_s[...], query_h) + bias_s[:, rows]
            attention = jnp.exp(scores - lse_ref[0, head : head + 1, rows])
            part = dot_nn(low(attention), dmix_h)
            d_values = part if d_values is None else d_values + part
            d_att = dot_nt(v_s[...], dmix_h)
            inner = jnp.sum(attention * d_att, 0, keepdims=True)
            d_scores = low(attention * (d_att - inner))
            part = dot_nn(d_scores, query_h)
            d_keys = part if d_keys is None else d_keys + part
            d_query.append(dot_tn(d_scores, k_s[...]))
        dqa[rows, :] = jnp.where(first_t, d_query[0], d_query[1])
    dka[...] = d_keys
    dva[...] = d_values
    q_hat = query * q_n
    k_hat = key * k_n
    d_query = dqa[...]
    along = d_query * q_hat
    ds_ref[0] = jnp.sum(along, 0, keepdims=True) * gain
    group = d_ref.shape[1] // 3
    start = pl.program_id(0) * 128

    def columns(c):
        return pl.ds(pl.multiple_of(start + c * group, 128), 128)

    out_q = low(gain * (d_query - q_hat * (per_head(along, first) / 64.0)) * q_n)
    d_ref[:, columns(0)] = out_q
    d_key = dka[...]
    out_k = low(
        0.125 * (d_key - k_hat * (per_head(d_key * k_hat, first) / 64.0)) * k_n
    )
    out_v = low(dva[...])
    d_ref[:, columns(1)] = out_k
    d_ref[:, columns(2)] = out_v
    half = length // 2
    for rows, out_ref in ((slice(0, half), top_ref), (slice(half, length), bottom_ref)):
        part = sum_s[rows, :] + dot_nt(out_q[rows], wq_ref[...])
        part = part + dot_nt(out_k[rows], wk_ref[...]) + dot_nt(out_v[rows], wv_ref[...])
        sum_s[rows, :] = part

        @pl.when(pl.program_id(0) == pl.num_programs(0) - 1)
        def _():
            out_ref[...] = low(part)


def attend_back(qkv, gain, cols, rows, lse, pieces, proj, w):
    length = qkv.shape[0]
    pairs = qkv.shape[1] // 384
    width = proj.shape[0]

    def part(rows, number):
        return pl.BlockSpec((rows, 128), lambda p: (0, number * pairs + p))

    return call(
        attend_back_kernel,
        (pairs,),
        [
            part(length, 0),
            part(length, 1),
            part(length, 2),
            pl.BlockSpec((1, 128), lambda p: (0, p)),
            whole((length, 128)),
            whole((8, length)),
            pl.BlockSpec((1, 2, length), lambda p: (p, 0, 0)),
        ]
        + [whole(pieces[0].shape)] * 4
        + [part(width, 0), part(width, 0), part(width, 1), part(width, 2)],
        [
            fixed((length, width)),
            fixed((length, 384 * pairs)),
            pl.BlockSpec((1, 1, 128), lambda p: (p, 0, 0)),
            fixed((length // 2, width)),
            fixed((length // 2, width)),
        ],
        [
            ((length, width), low_type),
            ((length, 384 * pairs), low_type),
            ((pairs, 1, 128), full_type),
            ((length // 2, width), low_type),
            ((length // 2, width), low_type),
        ],
        [pltpu.VMEM((length, 128), low_type)] * 4
        + [pltpu.VMEM((length, 128), full_type)] * 3
        + [pltpu.VMEM((length, length), full_type), pltpu.VMEM((length, width), full_type)],
        "attend_back",
    )(qkv, qkv, qkv, gain, cols, rows, lse, *pieces, proj, w, w, w)


def body(
    vq_in, codes, segment, live, labels, level_weight, qkv_w, proj_w, fc1_w, fc2_w, head_w, ada_w,
    tables, head_scale, d_stats, qkv_stat, proj_stat, fc1_stat, fc2_stat, head_stat, ada_stat,
    tables_v, scale_v,
):
    g_count = lax.axis_size("g")
    dp_count = g_count * lax.axis_size("c")
    mp_count = lax.axis_size("h") * lax.axis_size("l")
    at_c, at_h, at_l = lax.axis_index("c"), lax.axis_index("h"), lax.axis_index("l")
    row_count, seq_len, code_dim = vq_in.shape
    item_count = labels.shape[1]
    level_count = level_weight.shape[0]
    slice_width = tables.shape[1]
    width = slice_width * dp_count
    half, quarter = seq_len // 2, seq_len // 4
    table_rows = tables.shape[0]
    lead = code_dim + level_count
    per_row = row_count * item_count
    note_rows = -(-(2 * per_row + 3) // slice_width)
    lead_pad = -(-(lead + note_rows) // 16) * 16

    def halves(a):
        n = a.shape[-1] // 2
        lower, upper = low(a[..., :n]), low(a[..., n:])
        return jnp.where(at_c == 0, lower, upper), jnp.where(at_c == 0, upper, lower)

    first_mine, first_other = halves(jnp.concatenate([qkv_w, proj_w.T[None]], 0))
    first_near = ordered(at_c, first_mine, over_c(first_other), 1)

    place, weight, weight_here = row_layout(level_weight, segment, live)
    weight_here = weight_here[0, 0]

    per_row = row_count * item_count
    note_rows = -(-(2 * per_row + 3) // slice_width)
    lead_pad = -(-(lead + note_rows) // 16) * 16
    tables_low = low(tables)
    label_flat = labels.reshape(-1)
    digits = jnp.stack([weight_here // 4096, (weight_here // 64) % 64, weight_here % 64])
    note = jnp.concatenate([label_flat // 32, label_flat % 32, digits])
    note = jnp.pad(low(note), (0, (lead_pad - lead) * slice_width - note.shape[0]))
    note = note.reshape(lead_pad - lead, slice_width)
    packed = tie(jnp.concatenate([tables_low[:lead], note], 0), first_near)
    gathered, first_far = lax.optimization_barrier(
        (lax.all_gather(packed, DP, axis=0), over_h(first_near))
    )
    lead_table = jnp.transpose(gathered, (1, 0, 2)).reshape(lead_pad, width)
    notes = gathered[:, lead : lead + note_rows].reshape(dp_count, -1).astype(jnp.int32)
    labels_all = (notes[:, :per_row] * 32 + notes[:, per_row : 2 * per_row]).reshape(-1)
    weight_sum = full(
        jnp.sum(
            notes[:, 2 * per_row] * 4096
            + notes[:, 2 * per_row + 1] * 64
            + notes[:, 2 * per_row + 2]
        )
    )

    class_hot = (
        labels_all[:, None] + lead == jnp.arange(table_rows, dtype=jnp.int32)[None, :]
    )
    class_vec = dot_nn(low(class_hot), tables_low)
    sigma = jax.nn.sigmoid(class_vec)
    activated = low(class_vec * sigma)
    act_pairs = activated.reshape(g_count, 2, per_row, slice_width)
    act_mine = jnp.where(at_h == 0, act_pairs[:, 0], act_pairs[:, 1]).reshape(-1, slice_width)
    ada_low = low(ada_w)
    mod_part = dot_nn(act_mine, ada_low)
    mod_half = ada_w.shape[1] // 2
    left, right = mod_part[:, :mod_half], mod_part[:, mod_half:]
    mod_send = jnp.where(at_c == 0, right, left)
    mod_sum = jnp.where(at_c == 0, left, right) + over_c(mod_send)
    mod_first = mod_sum
    mod_sum = scatter_g(mod_sum)
    mod_items = ordered(at_c, mod_sum, over_c(mod_sum), 1).reshape(row_count, item_count, 8, width)
    mod_rows = jnp.transpose(mod_items, (0, 2, 1, 3))

    fc1_wide, fc2_wide = tie((fc1_w, fc2_w), mod_send)

    def near_rows(w):
        kept, other = halves(w)
        return ordered(at_c, kept, over_c(other), 0)

    def gathered_weight(a):
        wide = lax.all_gather(a.reshape(-1, a.shape[2]), "g", axis=0, tiled=True)
        return wide.reshape((g_count,) + a.shape)

    feed_near = jnp.concatenate([near_rows(fc1_wide), near_rows(fc2_wide.T)], 1)
    qkv_piece = ordered(at_h, first_near[None], first_far[None], 0)

    def window(*values):
        return lax.optimization_barrier(values)

    def far_part(r):
        return low(full(top[r][quarter:]) + full(moved[r][quarter:]))

    def turn(norm, kernel, filler=lambda: None, beside=None, keep=lambda done: None):
        moved[1] = over_c(bottom[1])
        first, moved[1] = window(norm(0, (top[0], moved[0], across[0])), moved[1])
        across[1] = over_l(far_part(1))
        pieces = [[first, over_l(first), over_c(first), None], None]
        done, across[1], pieces[0][2] = window(filler(), across[1], pieces[0][2])
        keep(done)
        second, pieces[0][1] = window(norm(1, (top[1], moved[1], across[1])), pieces[0][1])
        pieces[1] = [second, over_l(second), over_c(second), None]
        pieces[0][3] = over_c(pieces[0][1])
        kernel_out, pieces[1], beside = window(kernel(0, pieces[0]), pieces[1][:3], beside)
        return pieces, kernel_out, done, beside

    def launch():
        moved[0] = over_c(bottom[0])
        sent = far_part(0)
        across[0] = over_l(sent)
        return sent

    head_gain = tie(head_scale, mod_first)
    gain_own = jnp.where(at_c == 0, head_gain[:2], head_gain[2:])

    info = full(jnp.stack([codes, place, live, weight], 1))
    info_other, vq_other = over_c(info), over_c(vq_in)
    at = jnp.stack([full(at_c == at_h).astype(jnp.int32), at_c, at_l])
    arranged, olds, qkv_pieces, feed_far, gain_far = window(
        arrange(at, tie(info, mod_first), info_other, vq_in, vq_other, lead_pad),
        old_stats(*tie((qkv_w, proj_w, fc1_w, fc2_w, head_w, ada_w, tables, head_scale[None]), mod_first)),
        [qkv_piece] + [over_g(qkv_piece, k) for k in range(1, 4)] if g_count == 4 else [],
        over_h(feed_near),
        over_h(gain_own),
    )
    gains = jnp.exp(ordered(at_h, gain_own, gain_far, 0)) / 8.0
    gain_row = jnp.repeat(gains, 64)[None, :]
    feats, hot, cols, rows = (arranged[k::4] for k in range(4))
    head_near = near_rows(tie(head_w, olds))
    feats_first = tie(feats[0], gain_row)
    inputs_one, qkv_rows, mixed_rows, lse_rows, top, bottom, stream_zero = ([None] * 2 for _ in range(7))
    if g_count == 4:
        inputs_one[0], qkv_rows[0], stream_zero[0], qkv_full, proj_full = enter_first(
            lax.axis_index("g"), feats_first, lead_table, hot[0], mod_rows[0], qkv_pieces
        )
    else:
        wide_piece = lax.all_gather(qkv_piece, "g", axis=0)
        wide_piece = jnp.transpose(wide_piece, (0, 3, 2, 1, 4)).reshape(width, -1)
        qkv_full, proj_full = wide_piece[:, :768], wide_piece[:, 768:]
        inputs_one[0], qkv_rows[0], stream_zero[0] = enter(feats_first, lead_table, hot[0], mod_rows[0], qkv_full)
    feed_full = gathered_weight(ordered(at_h, feed_near[None], feed_far[None], 0))

    moved, across = [None] * 2, [None] * 2

    def attention(r, given):
        mixed_rows[r], lse_rows[r], top[r], bottom[r] = attend(
            given, gain_row, cols[r], rows[r], proj_full
        )
        return top[r], bottom[r]

    (top[0], bottom[0]), head_far = window(attention(0, qkv_rows[0]), over_h(head_near))
    held = [gathered_weight(ordered(at_h, head_near[None], head_far[None], 0))]
    moved[0] = over_c(bottom[0])
    (inputs_one[1], qkv_rows[1], stream_zero[1]), moved[0] = window(
        enter(tie(feats[1], bottom[0]), lead_table, hot[1], mod_rows[1], qkv_full), moved[0]
    )
    sent = far_part(0)
    across[0] = over_l(sent)
    (top[1], bottom[1]), across[0] = window(attention(1, tie(qkv_rows[1], sent)), across[0])

    branch_one, stream_one, acts, slopes, inputs_two = ([None] * 2 for _ in range(5))

    def norm_two(r, parts):
        branch_one[r], stream_one[r], given = onward(parts, stream_zero[r], hot[r], mod_rows[r], (2, 3, 4))
        return given

    def forward(r, pieces):
        inputs_two[r], acts[r], slopes[r], top[r], bottom[r] = feed(pieces, feed_full)
        return top[r], bottom[r]

    pieces_two, (top[0], bottom[0]), _, _ = turn(norm_two, forward)
    pieces_two[1].append(over_c(pieces_two[1][1]))
    sent = launch()
    (top[1], bottom[1]), across[0] = window(
        forward(1, [tie(pieces_two[1][0], sent)] + pieces_two[1][1:]), across[0]
    )

    block_codes = head_w.shape[1]
    half_codes = block_codes // 2
    column = jnp.arange(2 * half_codes, dtype=jnp.int32)
    block_here = (column // half_codes) * 2 + at_l
    column_code = full(block_here * block_codes + at_c * half_codes + column % half_codes)[None, :]
    branch_two, stream_two, logits, stats, d_logits, losses, others, inputs_out = ([None] * 2 for _ in range(8))

    def norm_out(r, parts):
        branch_two[r], stream_two[r], given = onward(parts, stream_one[r], hot[r], mod_rows[r], (5, 6, 7))
        return given

    def score(r, pieces):
        inputs_out[r], logits[r], stats[r] = head(pieces, held[0], cols[r], column_code)
        return stats[r]

    def compare(r):
        return [over_c(stats[r]), over_l(stats[r]), over_cl(stats[r])]

    def score_back(r):
        lines, losses[r] = merge(weight_sum, stats[r], *others[r], rows[r])
        d_logits[r], top[r], bottom[r] = head_back(logits[r], held[0], cols[r], column_code, lines)
        return top[r], bottom[r]

    pieces_out, stats[0], _, _ = turn(
        norm_out, score, lambda: held[0], keep=lambda done: held.__setitem__(0, done)
    )
    pieces_out[1].append(over_c(pieces_out[1][1]))
    stats[1], others[0] = window(score(1, pieces_out[1]), compare(0))
    (top[0], bottom[0]), others[1] = window(score_back(0), compare(1))
    sent = launch()
    logits[1] = tie(logits[1], sent)
    (top[1], bottom[1]), across[0] = window(score_back(1), across[0])

    def reduced(a):
        shape = a.shape[1:]
        a = lax.psum_scatter(a.reshape(-1, shape[2]), "g", scatter_dimension=0, tiled=True)
        return a.reshape(shape)

    def theirs(a):
        return jnp.where(at_h == 0, a[1], a[0])

    def settle(a, other):
        a = full(jnp.where(at_h == 0, a[0], a[1])) + full(other)
        rows = a.shape[0] // 2
        kept = jnp.where(at_c == 0, a[:rows], a[rows:])
        return kept, over_c(jnp.where(at_c == 0, a[rows:], a[:rows]))

    d_two, d_one, items_out, items_two, d_hidden, d_branch_two, d_branch_one = ([None] * 2 for _ in range(7))

    def back_out(r, parts):
        d_two[r], given, items_out[r] = back(
            parts, stream_two[r], hot[r], mod_rows[r], (7, 5), None, branch_two[r], None
        )
        return given

    def backward(r, pieces):
        d_branch_two[r], d_hidden[r], top[r], bottom[r] = feed_back(pieces, slopes[r], feed_full)
        return top[r], bottom[r]

    pieces_d_two, (top[0], bottom[0]), head_part, _ = turn(
        back_out, backward, lambda: head_grad_of(inputs_out, d_logits, g_count)
    )
    head_sum = reduced(head_part)
    pieces_d_two[1].append(over_c(pieces_d_two[1][1]))
    sent = launch()
    (top[1], bottom[1]), across[0], head_sum = window(
        backward(1, [tie(pieces_d_two[1][0], sent)] + pieces_d_two[1][1:]), across[0], head_sum
    )

    d_qkv, scale_rows = ([None] * 2 for _ in range(2))

    def back_two(r, parts):
        d_one[r], given, items_two[r] = back(
            parts, stream_one[r], hot[r], mod_rows[r], (4, 2), d_two[r], branch_one[r], None
        )
        return given

    def attention_back(r, pieces):
        d_branch_one[r], d_qkv[r], scale_rows[r], top[r], bottom[r] = attend_back(
            qkv_rows[r], gain_row, cols[r], rows[r], lse_rows[r], pieces, proj_full, qkv_full
        )
        return top[r], bottom[r]

    pieces_d_one, (top[0], bottom[0]), feed_part, head_other = turn(
        back_two,
        attention_back,
        lambda: feed_grad_of(inputs_two, d_hidden, d_branch_two, acts, g_count),
        over_h(theirs(head_sum)),
    )
    feed_sum = reduced(feed_part)
    pieces_d_one[1].append(over_c(pieces_d_one[1][1]))
    sent = launch()
    leaving = theirs(feed_sum)
    (top[1], bottom[1]), across[0], feed_other = window(
        attention_back(1, [tie(pieces_d_one[1][0], sent, leaving)] + pieces_d_one[1][1:]), across[0], over_h(leaving)
    )
    moved[1] = over_c(bottom[1])
    items_one, lead_parts = ([None] * 2 for _ in range(2))

    def back_one(r, parts):
        items_one[r], lead_parts[r] = back(
            parts, stream_zero[r], hot[r], mod_rows[r], (1,), d_one[r], None, feats[r]
        )
        return items_one[r]

    items_one[0], moved[1] = window(back_one(0, (top[0], moved[0], across[0])), moved[1])
    sent = far_part(1)
    across[1] = over_l(sent)
    first_part = first_grad_of(inputs_one, tie(d_qkv, sent), d_branch_one, mixed_rows, g_count)
    first_part, across[1] = window(first_part, across[1])
    first_sum = reduced(first_part)
    back_one(1, (top[1], moved[1], across[1]))
    lead_part = lead_parts[0] + lead_parts[1]

    def flat_items(items, number):
        return jnp.concatenate([items[r][number, :item_count] for r in range(2)], 0)

    d_items = jnp.concatenate(
        [flat_items(items_one, 0), flat_items(items_one, 1), flat_items(items_two, 2)]
        + [flat_items(items_two, 0), flat_items(items_two, 1), flat_items(items_out, 2)]
        + [flat_items(items_out, 0), flat_items(items_out, 1)],
        1,
    )
    left, right = d_items[:, :mod_half], d_items[:, mod_half:]
    d_items = jnp.where(at_c == 0, left, right) + over_c(jnp.where(at_c == 0, right, left))
    d_items = low(d_items + over_l(d_items))
    d_items, first_sum = window(ordered(at_h, d_items, over_h(d_items), 0), first_sum)
    leaving = theirs(first_sum)
    d_items = gather_g(tie(d_items, leaving))
    d_items = ordered(at_c, d_items, over_c(d_items), 1)
    ada_grad = dot_tn(activated, d_items)
    d_act_vec = dot_nt(d_items, ada_low)
    d_class = d_act_vec * (sigma * (1.0 + class_vec * (1.0 - sigma)))
    lead_part = jnp.transpose(lead_part.reshape(lead_pad, dp_count, slice_width), (1, 0, 2))
    lead_grad = jnp.sum(lax.all_to_all(lead_part, DP, 0, 0, tiled=True).reshape(dp_count, lead_pad, slice_width), 0)
    lead_grad = lead_grad + over_l(lead_grad)
    lead_grad = lead_grad + over_h(lead_grad)
    tables_grad = dot_tn(full(class_hot), d_class, highest)
    tables_grad = tables_grad + jnp.pad(lead_grad[:lead], ((0, table_rows - lead), (0, 0)))

    head_grad = ordered(at_c, *settle(tie(head_sum, items_one[0]), head_other), 1)
    kept, moved_half = settle(feed_sum, feed_other)
    n = kept.shape[1] // 2
    fc1_grad = ordered(at_c, kept[:, :n], moved_half[:, :n], 1)
    fc2_grad = ordered(at_c, kept[:, n:], moved_half[:, n:], 1)
    ada_grad, tables_grad, first_other = window(ada_grad, tables_grad, over_h(leaving))
    kept, moved_half = settle(first_sum, first_other)
    first_halves = jnp.stack([kept, moved_half])
    first_halves = jnp.where(at_c == 0, first_halves, first_halves[::-1])
    first_halves = jnp.transpose(first_halves.reshape(2, slice_width, 4, -1), (2, 1, 0, 3))
    first_halves = first_halves.reshape(4, slice_width, -1)
    qkv_grad, proj_grad = first_halves[:3], first_halves[3]

    decay = 1.0 - STEP ** (-0.8)
    grads = [qkv_grad, proj_grad, fc1_grad, fc2_grad, head_grad, ada_grad]
    wide = [g.size // slice_width * (mp_count if k < 5 else 1) for k, g in enumerate(grads)]
    sizes = [g.size // slice_width for g in grads]
    starts = [sum(sizes[:k]) for k in range(7)]

    def over_mp(a):
        a = a + over_l(a)
        return a + over_h(a)

    spots = jnp.arange(128, dtype=jnp.int32)[None, :]
    early_line = over_mp(tie(olds[:1] + jnp.where(spots == 22, losses[0] + losses[1], 0.0), lead_part))
    tail = early_line + olds[1:]
    rows_all = over_mp(row_stats(*grads[:5]))
    wide_column = jnp.array(wide[:5], full_type)[:, None]
    row_new = decay * d_stats[:5] + (1.0 - decay) * (rows_all[:5] / wide_column)
    tables_v_new = decay * tables_v + (1.0 - decay) * (tables_grad * tables_grad + eps_one)
    tables_step = tables_grad * lax.rsqrt(tables_v_new)
    tables_sum = jnp.sum(tables_step * tables_step)[None, None]
    scales = tie(scale_rows[0] + scale_rows[1], lead_part)
    scales = jnp.where(at_h == 0, scales[0], scales[1]) + over_h(
        jnp.where(at_h == 0, scales[1], scales[0])
    )
    flat, ada_row = column_stats(at_c, row_new, d_stats[5:6], tail, tables_sum, scales, grads, decay)
    d_stats_new = jnp.concatenate([row_new, ada_row[:1]], 0)
    if g_count == 4:
        flat = flat + over_c(flat)
        flat = flat + over_g(flat, 1)
        flat = flat + over_g(flat, 2)
    else:
        flat = lax.psum(flat, DP)
    col_old = jnp.concatenate(
        [qkv_stat.reshape(-1), proj_stat, fc1_stat, fc2_stat, head_stat, ada_stat]
    )[None, :]
    heads = head_scale.shape[0]
    scale_line = jnp.pad(scale_v, (11, 128 - 11 - heads), constant_values=1.0)[None, :]
    col_line, part_line, own_line, second_line, scale_step = finish(
        flat, col_old, scale_line, decay, width, starts
    )
    col_new = [col_line[0, starts[k] : starts[k + 1]] for k in range(6)]
    line = flat[:1, starts[6] :]
    scale_grad = line[0, 11 : 11 + heads]
    loss_sum = line[0, 22]
    scale_v_new = second_line[0, 11 : 11 + heads]
    entries = [width * wide[k] for k in range(6)] + [table_rows * width, heads * mp_count]
    news = renew(
        (line, over_mp(part_line), own_line, early_line),
        d_stats_new,
        col_line,
        grads,
        (tables_step, scale_step),
        (
            qkv_w, proj_w, fc1_w, fc2_w, head_w, ada_w, tables,
            jnp.pad(head_scale, (11, 128 - 11 - heads))[None, :],
        ),
        width,
        entries,
        starts,
    )
    return (
        loss_sum,
        weight_sum,
        qkv_grad,
        news[8],
        fc1_grad,
        news[9],
        head_grad,
        ada_grad,
        tables_grad,
        scale_grad,
        d_stats_new,
        col_new[0].reshape(3, -1),
        col_new[1],
        col_new[2],
        col_new[3],
        col_new[4],
        col_new[5],
        tables_v_new,
        scale_v_new,
        news[0],
        news[1],
        news[2],
        news[3],
        news[4],
        news[5],
        news[6],
        news[7][0, 11 : 11 + heads],
    )


def solution(mesh):
    inner = Mesh(
        mesh.devices.reshape(mesh.shape["dp"] // 2, 2, mesh.shape["mp"] // 2, 2),
        ("g", "c", "h", "l"),
    )
    return jax.shard_map(
        body,
        mesh=inner,
        in_specs=(
            P(DP, None, None),
            P(DP, None),
            P(DP, None),
            P(DP, None),
            P(DP, None),
            P(),
            P(None, DP, MP),
            P(MP, DP),
            P(DP, MP),
            P(MP, DP),
            P(DP, MP),
            P(DP, None),
            P(None, DP),
            P(MP),
            P(None, DP),
            P(None, MP),
            P(MP),
            P(MP),
            P(MP),
            P(MP),
            P(),
            P(None, DP),
            P(MP),
        ),
        out_specs=(
            P(),
            P(),
            P(None, DP, MP),
            P(MP, DP),
            P(DP, MP),
            P(MP, DP),
            P(DP, MP),
            P(DP, None),
            P(None, DP),
            P(MP),
            P(None, DP),
            P(None, MP),
            P(MP),
            P(MP),
            P(MP),
            P(MP),
            P(),
            P(None, DP),
            P(MP),
            P(None, DP, MP),
            P(MP, DP),
            P(DP, MP),
            P(MP, DP),
            P(DP, MP),
            P(DP, None),
            P(None, DP),
            P(MP),
        ),
        check_vma=False,
    )
```
